32 devices in a mesh: groups: 2 (over y), resp: 4 (over z), section: 4 (over x, core).
Axes of the slice: x: 2, y: 2, z: 4, core: 2. Of those that a mesh axis runs over, the one named last changes fastest.
Arguments:
- completion_rows: bfloat16 [2, 8, 64, 4096], P(None, ('groups', 'resp')), parts along dimension 1, may hold values from -16 to 16
- prompt_pool: bfloat16 [4, 8, 64, 4096], P('section', ('groups', 'resp')), parts along dimension 1, may hold values from -16 to 16
- norm_gain: float32 [4, 4096], P('section'), may hold values from 0.5 to 1.5
- short_taps: float32 [4, 7, 4096], P('section'), may hold values from -2.4 to 2.4
- long_taps: float32 [4, 128, 256], P('section'), may hold values from -0.5 to 0.5
- score_head: float32 [4096], replicated, may hold values from -0.09375 to 0.09375
- live_lengths: int32 [2, 8], P(None, ('groups', 'resp')), parts along dimension 1, may hold values from 16 to 64, as said below
- prompt_owner: int32 [4], P('groups'), parts along dimension 0, may hold values from 0 to 3
- pair_index: int32 [2, 16, 2], P(None, 'groups'), parts along dimension 1, may hold values from 0 to 3
Outputs:
- scores: bfloat16 [2, 8], P(None, ('groups', 'resp')), parts along dimension 1
- gain_grad: float32 [4, 8192], P('section', 'groups'), parts along dimension 1
- short_grad: float32 [4, 14, 4096], P('section', 'groups'), parts along dimension 1
- long_grad: float32 [4, 256, 256], P('section', 'groups'), parts along dimension 1
The draws below stay inside these ranges and needn't reach their ends.
There are 2 independent parts, one for each index of `groups`. The reference program is written for one: setup_inputs(seed, part) draws one part's arguments, and reference() takes and returns one part's arrays. A program takes and returns all parts, laid end to end along the dimension named above; an argument that names none is the same for every part. Nothing has to cross between parts.
Inputs may be any that keep to these rules, and one draw needn't show every extreme that they name: `live_lengths`: live rows of each completion, counted from its first row; in each microbatch one completion has all 64 rows live and another a quarter of 64. `pair_index`: the two members of a pair may coincide.
All inputs are finite; a program needn't handle non-finite values.
Results may differ from the reference program's by a relative error of at most 0.0097.
Values may be sent and summed in bfloat16 or wider, within the bound.
A program may use at most 256 MiB of HBM per device.

```python
import math
import jax
import jax.numpy as jnp
from jax import lax

D = 4096
FG = 256
KL = 128
SHORT = 7
L = 64
PW = 64
MB = 2
COMP = 4
NP = 8
N_RESP = 4
N_SECTION = 4


def rough_rows(key, shape):
    values = jax.random.normal(key, shape, jnp.float32)
    return jnp.clip(values, -16.0, 16.0)


def draw_completion_rows(key, part):
    return rough_rows(jax.random.fold_in(key, 11), (MB, COMP, L, D)).astype(jnp.bfloat16)


def draw_prompt_pool(key, part):
    return rough_rows(jax.random.fold_in(key, 12), (N_SECTION, N_RESP, PW, D)).astype(jnp.bfloat16)


def draw_live_lengths(key, part):
    folded = jax.random.fold_in(key, 21)
    first_key, second_key = jax.random.split(folded)
    base = jax.random.randint(first_key, (MB, COMP), L // 4, L + 1, dtype=jnp.int32)
    orders = jax.vmap(lambda single: jax.random.permutation(single, COMP))(jax.random.split(second_key, MB))
    ranked = jnp.argsort(orders, axis=1, stable=True)
    lengths_out = jnp.where(ranked == 0, L, jnp.where(ranked == 1, L // 4, base))
    return lengths_out.astype(jnp.int32)


def set_ends(array, own_key, low, high):
    spot = [jax.random.randint(jax.random.fold_in(own_key, axis), (), 0, length) for axis, length in enumerate(array.shape)]
    main_axis = array.shape.index(max(array.shape))
    beside = spot[:main_axis] + [(spot[main_axis] + 1) % array.shape[main_axis]] + spot[main_axis + 1:]
    return array.at[tuple(spot)].set(low).at[tuple(beside)].set(high)


def level_of(own_key, dims, pieces, low, largest):
    factor_of = 1.0
    for position, shards_of in pieces:
        draws = jax.random.uniform(jax.random.fold_in(jax.random.fold_in(own_key, 6), position), (shards_of,), jnp.float32, low / len(pieces), largest / len(pieces))
        factor_of = factor_of * jnp.repeat(jnp.exp(draws), dims[position] // shards_of).reshape((-1,) + (1,) * (len(dims) - 1 - position))
    return factor_of


def scatter_about(own_key, shape, width, limit, shards=(), kind=jnp.bfloat16):
    drawn = width * jax.random.normal(own_key, shape, jnp.float32)
    if shards:
        drawn = drawn * level_of(own_key, shape, shards, -0.22, 0.18)
    return jnp.clip(drawn, -limit, limit).astype(kind)


def setup_inputs(seed: int = 0, part: int = 0) -> dict:
    key_of = jax.random.split(jax.random.key(seed), 10)
    part_keys = jax.random.split(jax.random.fold_in(key_of[9], part), 10)
    return {
        "completion_rows": draw_completion_rows(jax.random.fold_in(jax.random.fold_in(key_of[9], part), 71), part),
        "prompt_pool": draw_prompt_pool(jax.random.fold_in(jax.random.fold_in(key_of[9], part), 71), part),
        "norm_gain": jnp.clip(1.0 + 0.1 * jax.random.normal(key_of[2], (N_SECTION, D), jnp.float32), 0.5, 1.5),
        "short_taps": scatter_about(key_of[3], (N_SECTION, SHORT, D), 0.4, 2.4, ((0, 4),), jnp.float32),
        "long_taps": scatter_about(key_of[4], (N_SECTION, KL, FG), KL ** -0.5, 0.5, ((0, 4),), jnp.float32),
        "score_head": scatter_about(key_of[5], (D,), D ** -0.5, 0.09375, (), jnp.float32),
        "live_lengths": draw_live_lengths(jax.random.fold_in(jax.random.fold_in(key_of[9], part), 71), part),
        "prompt_owner": jax.random.randint(part_keys[7], (MB,), 0, N_RESP).astype(jnp.int32),
        "pair_index": set_ends(jax.random.randint(part_keys[8], (MB, NP, 2), 0, COMP), jax.random.fold_in(part_keys[8], 1), 0, COMP - 1).astype(jnp.int32),
    }


def long_conv(values, taps_grouped):
    channels = values.shape[1]
    spread = jnp.repeat(taps_grouped, channels // taps_grouped.shape[1], axis=1)
    count_rows = values.shape[0]
    fft_len = 2 ** int(math.ceil(math.log2(count_rows + spread.shape[0])))
    spectrum = jnp.fft.rfft(values, n=fft_len, axis=0) * jnp.fft.rfft(spread, n=fft_len, axis=0)
    return jnp.fft.irfft(spectrum, n=fft_len, axis=0)[:count_rows]

def mixer(comp_rows, prompt_rows, gain_row, short_row, long_row):
    joined = jnp.concatenate([prompt_rows, comp_rows], axis=0).astype(jnp.float32)
    factor = lax.rsqrt(lax.optimization_barrier(jnp.mean(joined * joined, axis=1, keepdims=True)) + 1e-06)
    normed = joined * factor * gain_row[None, :]
    count_rows = joined.shape[0]
    tap_count = short_row.shape[0]
    padded = jnp.pad(normed, ((tap_count - 1, 0), (0, 0)))
    shorter = jnp.zeros_like(normed)
    for offset in range(tap_count):
        begin = tap_count - 1 - offset
        shorter = shorter + short_row[offset][None, :] * padded[begin:begin + count_rows]
    longer = long_conv(shorter, long_row)
    offset_rows = prompt_rows.shape[0]
    return joined[offset_rows:] + normed[offset_rows:] * longer[offset_rows:]

def pair_slopes(table, pair_index):
    labels = jnp.arange(table.shape[1], dtype=jnp.int32)
    winner = (pair_index[:, :, 0:1] == labels).astype(jnp.float32)
    loser = (pair_index[:, :, 1:2] == labels).astype(jnp.float32)
    margin = lax.optimization_barrier(jnp.sum((winner - loser) * table[:, None, :], axis=2))
    weight = jax.nn.sigmoid(-margin)
    return lax.optimization_barrier(jnp.sum((loser - winner) * weight[:, :, None], axis=1))

def cotangent_rows(slope_arg, head_arg, length_arg, count_rows):
    live = (jnp.arange(count_rows, dtype=jnp.int32) < length_arg).astype(jnp.float32)
    return slope_arg * live[:, None] * head_arg[None, :] / jnp.sqrt(length_arg.astype(jnp.float32))

def reference(completion_rows, prompt_pool, norm_gain, short_taps, long_taps, score_head, live_lengths, prompt_owner, pair_index):
    saved = []
    score_list = []
    for batch_id in range(MB):
        moving = completion_rows[batch_id]
        kept = []
        for section_id in range(N_SECTION):
            prompt_now = lax.dynamic_index_in_dim(prompt_pool[section_id], prompt_owner[batch_id], 0, keepdims=False)
            kept.append((moving, prompt_now))

            def forward_one(rows_arg, prompt_arg=prompt_now, section_arg=section_id):
                return mixer(rows_arg, prompt_arg, norm_gain[section_arg], short_taps[section_arg], long_taps[section_arg]).astype(jnp.bfloat16)
            moving = lax.map(forward_one, moving)
        per_row = jnp.einsum('cld,d->cl', moving.astype(jnp.float32), score_head, precision=lax.Precision.HIGHEST)
        live = jnp.arange(L, dtype=jnp.int32)[None, :] < live_lengths[batch_id][:, None]
        totals = lax.optimization_barrier(jnp.sum(jnp.where(live, per_row, 0.0), axis=1))
        score_list.append(totals / jnp.sqrt(live_lengths[batch_id].astype(jnp.float32)))
        saved.append(kept)
    raw_score = jnp.stack(score_list, axis=0)
    slopes = pair_slopes(raw_score, pair_index)
    gain_acc = [jnp.zeros((D,), jnp.float32) for section_id in range(N_SECTION)]
    short_acc = [jnp.zeros((SHORT, D), jnp.float32) for section_id in range(N_SECTION)]
    long_acc = [jnp.zeros((KL, FG), jnp.float32) for section_id in range(N_SECTION)]
    for batch_id in range(MB):
        cotangent = jax.vmap(cotangent_rows, in_axes=(0, None, 0, None))(slopes[batch_id], score_head, live_lengths[batch_id], L)
        for section_id in reversed(range(N_SECTION)):
            rows_in, prompt_now = saved[batch_id][section_id]

            def visit(carry, item, prompt_arg=prompt_now, section_arg=section_id):
                rows_arg, cot_arg = item

                def local_layer(rows_var, gain_var, short_var, long_var):
                    return mixer(rows_var, prompt_arg, gain_var, short_var, long_var)
                primal, puller = jax.vjp(local_layer, rows_arg, norm_gain[section_arg], short_taps[section_arg], long_taps[section_arg])
                grad_rows, grad_gain, grad_short, grad_long = puller(cot_arg)
                return ((carry[0] + grad_gain, carry[1] + grad_short, carry[2] + grad_long), grad_rows)
            start = (jnp.zeros((D,), jnp.float32), jnp.zeros((SHORT, D), jnp.float32), jnp.zeros((KL, FG), jnp.float32))
            summed, grad_inputs = lax.scan(visit, start, (rows_in, cotangent))
            gain_acc[section_id] = gain_acc[section_id] + summed[0]
            short_acc[section_id] = short_acc[section_id] + summed[1]
            long_acc[section_id] = long_acc[section_id] + summed[2]
            cotangent = lax.optimization_barrier(grad_inputs).astype(jnp.float32)
    return (raw_score.astype(jnp.bfloat16), jnp.stack(gain_acc, axis=0), jnp.stack(short_acc, axis=0), jnp.stack(long_acc, axis=0))
```

```python
import functools

import jax
import jax.numpy as jnp
from jax import lax
from jax.experimental import pallas as pl
from jax.experimental.pallas import tpu as pltpu
from jax.sharding import PartitionSpec as P

LANES = 128
MESH = pl.DeviceIdType.MESH
F32 = jnp.float32
BF16 = jnp.bfloat16


def rows_to_line(block):
    line = jnp.sum(jnp.transpose(block), axis=0, keepdims=True)
    return jnp.broadcast_to(line, (8, LANES))


def line_to_rows(tile):
    return jnp.transpose(jnp.broadcast_to(tile[0:1], (LANES, LANES)))


def kernel(
    dims,
    direct,
    comp_ref,
    prompt_ref,
    gain_hbm,
    short_hbm,
    taps_hbm,
    owner_ref,
    head_ref,
    ends_ref,
    length_ref,
    score_ref,
    *rest,
):
    sections, n_resp, micro, length, prompt_len, chans, per_group, width = dims
    outs, rest = (rest[:3], rest[3:]) if direct else (rest[:1], rest[1:])
    (
        toep,
        toep_t,
        pool,
        chosen_rows,
        gain_ref,
        short_ref,
        taps_ref,
        rows_in,
        short_out,
        long_out,
        fac_p,
        fac_c,
        upstream,
        partial,
        stat_acc,
        score_acc,
        prompt_acc,
        stat_out,
        stat_in,
        resp_out,
        resp_in,
        tiles_own,
        tiles_in,
        tiles_sum,
        tiles_all,
        local_sem,
        weight_sems,
        spread_sems,
        pool_sems,
        stat_sems,
        resp_sems,
        part_sems,
        tile_send,
        tile_recv,
    ) = rest
    groups = LANES // per_group
    blocks = chans // LANES
    group_rows = blocks * groups
    total = prompt_len + length
    me = lax.axis_index("section")
    me_resp = lax.axis_index("resp")
    own_lanes = pl.ds(pl.multiple_of(me * chans, chans), chans)

    def lane_slice(block):
        return pl.ds(pl.multiple_of(block * LANES, LANES), LANES)

    def head_slice(block):
        return pl.ds(pl.multiple_of(me * chans + block * LANES, LANES), LANES)

    def wide_slice(block):
        return pl.ds(pl.multiple_of(block * micro * LANES, LANES), micro * LANES)

    def loop(low, high, step_of):
        def run(index, carry):
            step_of(index)
            return carry

        lax.fori_loop(low, high, run, 0)

    def swap(axis, count, mine, out_ref, in_ref, sems):
        def copy(step):
            return pltpu.make_async_remote_copy(
                src_ref=out_ref,
                dst_ref=in_ref.at[mine],
                send_sem=sems.at[0, step],
                recv_sem=sems.at[1, step],
                device_id={axis: lax.rem(mine + step, count)},
                device_id_type=MESH,
            )

        loop(1, count, lambda step: copy(step).start())
        in_ref[mine] = out_ref[...]
        return lambda: loop(1, count, lambda step: copy(step).wait())

    def start_stats(slot, first, second):
        stat_out[slot, 0] = first
        stat_out[slot, 1] = second
        wait = swap(
            "section", sections, me, stat_out.at[slot], stat_in.at[slot], stat_sems.at[slot]
        )

        def finish():
            wait()
            return jnp.sum(stat_in[slot], axis=0)

        return finish

    def weight_copies(step):
        peer = lax.rem(me + step, sections)
        lanes = pl.ds(pl.multiple_of(peer * chans, chans), chans)
        rows = pl.ds(pl.multiple_of(peer * group_rows, group_rows), group_rows)
        return [
            pltpu.make_async_remote_copy(
                src_ref=source,
                dst_ref=target,
                send_sem=weight_sems.at[0, kind, step],
                recv_sem=weight_sems.at[1, kind, step],
                device_id={"section": peer},
                device_id_type=MESH,
            )
            for kind, source, target in (
                (0, gain_hbm.at[:, lanes], gain_ref.at[me]),
                (2, short_hbm.at[:, lanes], short_ref.at[me]),
                (1, taps_hbm.at[rows, :], taps_ref.at[me]),
            )
        ]

    def start_weights(step):
        for copy in weight_copies(step):
            copy.start()

    def wait_weights(step):
        for copy in weight_copies(step):
            copy.wait()

    own_rows = pl.ds(pl.multiple_of(me * group_rows, group_rows), group_rows)
    local_copies = [
        pltpu.make_async_copy(comp_ref.at[:, own_lanes], rows_in.at[0], local_sem.at[0]),
        pltpu.make_async_copy(gain_hbm.at[:, own_lanes], gain_ref.at[me], local_sem.at[1]),
        pltpu.make_async_copy(short_hbm.at[:, own_lanes], short_ref.at[me], local_sem.at[3]),
        pltpu.make_async_copy(taps_hbm.at[own_rows, :], taps_ref.at[me], local_sem.at[2]),
    ]

    def spread_copy(step):
        peer = lax.rem(me + step, sections)
        lanes = pl.ds(pl.multiple_of(peer * chans, chans), chans)
        return pltpu.make_async_remote_copy(
            src_ref=prompt_ref.at[:, lanes],
            dst_ref=pool.at[me, me_resp],
            send_sem=spread_sems.at[0, step],
            recv_sem=spread_sems.at[1, step],
            device_id={"section": peer},
            device_id_type=MESH,
        )

    def pool_copy(s, step):
        return pltpu.make_async_remote_copy(
            src_ref=pool.at[s, me_resp],
            dst_ref=pool.at[s, me_resp],
            send_sem=pool_sems.at[0, s, step],
            recv_sem=pool_sems.at[1, s, step],
            device_id={"resp": lax.rem(me_resp + step, n_resp)},
            device_id_type=MESH,
        )

    def own_pool():
        return pltpu.make_async_copy(
            prompt_ref.at[:, own_lanes], pool.at[me, me_resp], local_sem.at[4]
        )

    def start_pool(s):
        step = lax.rem(me - s + sections, sections)

        @pl.when(step == 0)
        def _():
            own_pool().wait()

        @pl.when(step > 0)
        def _():
            spread_copy(step).wait()

        loop(1, n_resp, lambda d: pool_copy(s, d).start())

    def wait_pool(s):
        loop(1, n_resp, lambda d: pool_copy(s, d).wait())

    if direct:
        own_pool().start()
        loop(1, sections, lambda step: spread_copy(step).start())
    for copy in local_copies:
        copy.start()
    loop(1, sections, start_weights)
    if direct:
        start_pool(0)
    for copy in local_copies:
        copy.wait()

    def first_stats(block):
        wide = rows_in[0, :, lane_slice(block)].astype(F32)
        stat_acc[...] += wide * wide

    stat_acc[...] = jnp.zeros_like(stat_acc)
    loop(0, blocks, first_stats)
    loop(1, sections, wait_weights)

    t_row = lax.broadcasted_iota(jnp.int32, (length, LANES), 0)
    s_lane = lax.broadcasted_iota(jnp.int32, (length, LANES), 1)
    keep = s_lane <= prompt_len + t_row
    s_row = lax.broadcasted_iota(jnp.int32, (total, LANES), 0)
    t_lane = lax.broadcasted_iota(jnp.int32, (total, LANES), 1)
    keep_t = s_row <= prompt_len + t_lane

    def build(s, block):
        rows = pl.ds(pl.multiple_of(block * groups, groups), groups)
        both = taps_ref[s, rows, :]
        flipped, plain = both[:, :LANES], both[:, LANES:]
        for g in range(groups):
            base = pl.multiple_of((block * groups + g) * length, length)
            wide = jnp.broadcast_to(flipped[g : g + 1], (length, LANES))
            wide = pltpu.roll(wide, prompt_len, 1, stride=1, stride_axis=0)
            wide = jnp.where(keep, wide, 0.0)
            high = wide.astype(BF16)
            low = (wide - high.astype(F32)).astype(BF16)
            toep[s, pl.ds(base, length), :] = jnp.concatenate([high, high, low], axis=1)
            base = pl.multiple_of((block * groups + g) * total, total)
            wide = jnp.broadcast_to(plain[g : g + 1], (total, LANES))
            wide = pltpu.roll(wide, prompt_len, 1, stride=1, stride_axis=0)
            toep_t[s, pl.ds(base, total), :] = jnp.where(keep_t, wide, 0.0).astype(BF16)

    def choose(s, block):
        lanes = lane_slice(block)
        for m in range(micro):
            rows = slice(m * prompt_len, (m + 1) * prompt_len)
            if direct:
                picked = jnp.zeros((prompt_len, LANES), F32)
                for r in range(n_resp):
                    flag = jnp.full((prompt_len, LANES), owner_ref[m], jnp.int32) == r
                    picked = jnp.where(flag, pool[s, r, :, lanes].astype(F32), picked)
                chosen_rows[s, rows, lanes] = picked.astype(BF16)
            else:
                picked = prompt_ref[s, rows, lanes].astype(F32)
                chosen_rows[s, rows, lanes] = prompt_ref[s, rows, lanes]
            prompt_acc[rows, :] += picked * picked

    row_id = lax.broadcasted_iota(jnp.int32, (total, LANES), 0)
    wide_group = (
        lax.broadcasted_iota(jnp.int32, (1, micro * LANES), 1) % LANES
    ) // per_group
    tap_count = short_ref.shape[1]

    def pick(stacked, rows):
        out = stacked[0:rows]
        for g in range(1, groups):
            out = jnp.where(wide_group == g, stacked[g * rows : (g + 1) * rows], out)
        return out

    def joined_rows(s, m, lanes):
        rows_p = slice(m * prompt_len, (m + 1) * prompt_len)
        rows_c = slice(m * length, (m + 1) * length)
        joined = jnp.concatenate(
            [chosen_rows[s, rows_p, lanes].astype(F32), rows_in[s, rows_c, lanes].astype(F32)],
            axis=0,
        )
        factor = jnp.concatenate([fac_p[s, rows_p, :], fac_c[s, rows_c, :]], axis=0)
        return joined, factor

    def forward(s, carry):
        if direct:
            wait_pool(s)

            @pl.when(s + 1 < sections)
            def _():
                start_pool(s + 1)

        prompt_acc[...] = jnp.zeros_like(prompt_acc)
        loop(0, blocks, lambda block: choose(s, block))
        finish = start_stats(s, rows_to_line(stat_acc[...]), rows_to_line(prompt_acc[...]))
        loop(0, blocks, lambda block: build(s, block))
        sums = finish()
        fac_c[s] = lax.rsqrt(line_to_rows(sums[0]) * (1.0 / width) + 1e-06)
        fac_p[s] = lax.rsqrt(line_to_rows(sums[1]) * (1.0 / width) + 1e-06)
        stat_acc[...] = jnp.zeros_like(stat_acc)
        score_acc[...] = jnp.zeros_like(score_acc)

        def run(block, carry):
            lanes = lane_slice(block)
            wide = wide_slice(block)
            gain = gain_ref[s, :, lanes]
            short = short_ref[s, :, lanes]
            parts, lows, saved = [], [], []
            for m in range(micro):
                joined, factor = joined_rows(s, m, lanes)
                normed = joined * factor * gain
                shorter = normed * short[0:1]
                for j in range(1, tap_count):
                    moved = jnp.where(row_id >= j, pltpu.roll(normed, j, 0), 0.0)
                    shorter = shorter + moved * short[j : j + 1]
                high = shorter.astype(BF16)
                parts.append(high)
                lows.append((shorter - high.astype(F32)).astype(BF16))
                saved.append((joined[prompt_len:], normed[prompt_len:]))
            high = jnp.concatenate(parts, axis=1)
            short_out[s, :, wide] = high
            rhs = jnp.concatenate([high, jnp.concatenate(lows, axis=1), high], axis=0)
            base = pl.multiple_of(block * groups * length, groups * length)
            stacked = jnp.dot(
                toep[s, pl.ds(base, groups * length), :], rhs, preferred_element_type=F32
            )
            longer_all = pick(stacked, length)
            for m in range(micro):
                rows = slice(m * length, (m + 1) * length)
                longer = longer_all[:, m * LANES : (m + 1) * LANES]
                long_out[s, rows, lanes] = longer
                mixed = (saved[m][0] + saved[m][1] * longer).astype(BF16)
                rows_in[s + 1, rows, lanes] = mixed
                mixed = mixed.astype(F32)
                stat_acc[rows, :] += mixed * mixed
                score_acc[rows, :] += mixed * head_ref[0:1, head_slice(block)]
            return carry

        lax.fori_loop(0, blocks, run, 0)

        return carry

    lax.fori_loop(0, sections, forward, 0)

    live = []
    for m in range(micro):
        count = jnp.full((length, LANES), length_ref[m, 0], jnp.int32)
        live.append(jnp.where(t_row < count, 1.0, 0.0) / jnp.sqrt(count.astype(F32)))
    tile_rows = []
    for m in range(micro):
        rows = slice(m * length, (m + 1) * length)
        line = jnp.sum(score_acc[rows, :] * live[m], axis=0, keepdims=True)
        tile_rows.append(jnp.broadcast_to(jnp.sum(line, axis=1, keepdims=True), (1, LANES)))
    tile_rows.append(jnp.zeros((8 - micro, LANES), F32))
    score_tile = jnp.concatenate(tile_rows, axis=0)
    own_score = start_stats(sections, score_tile, score_tile)()[0]
    score_ref[...] = own_score
    resp_out[...] = own_score
    swap("resp", n_resp, me_resp, resp_out, resp_in, resp_sems)()
    winner, loser = ends_ref[0], ends_ref[1]

    def signs(r):
        return jnp.where(winner == r, 1.0, 0.0) - jnp.where(loser == r, 1.0, 0.0)

    margin = lax.fori_loop(
        0, n_resp, lambda r, acc: acc + resp_in[r] * signs(r), jnp.zeros((8, LANES), F32)
    )
    weight = 1.0 / (1.0 + jnp.exp(margin))
    slopes = -jnp.sum(signs(me_resp) * weight, axis=1, keepdims=True)

    def seed(block, carry):
        lanes = lane_slice(block)
        for m in range(micro):
            rows = slice(m * length, (m + 1) * length)
            upstream[rows, lanes] = live[m] * slopes[m : m + 1] * head_ref[0:1, head_slice(block)]
        return carry

    lax.fori_loop(0, blocks, seed, 0)

    keep_pair = total - 1 - s_lane <= prompt_len + t_row
    reverse = (
        lax.broadcasted_iota(jnp.int32, (total, total), 0)
        + lax.broadcasted_iota(jnp.int32, (total, total), 1)
        == total - 1
    )
    reverse = jnp.where(reverse, 1.0, 0.0).astype(BF16)

    share = 2 * blocks // n_resp

    def part_slice(r):
        return pl.ds(r * share, share)

    def part_steps(s, action):
        def each(step):
            peer = lax.rem(me_resp + step, n_resp)
            action(
                pltpu.make_async_remote_copy(
                    src_ref=tiles_own.at[s, part_slice(peer)],
                    dst_ref=tiles_in.at[s, me_resp],
                    send_sem=part_sems.at[0, s, step],
                    recv_sem=part_sems.at[1, s, step],
                    device_id={"resp": peer},
                    device_id_type=MESH,
                )
            )

        loop(1, n_resp, each)

    def tile_copy(s, step, k, r):
        return pltpu.make_async_remote_copy(
            src_ref=tiles_sum.at[s],
            dst_ref=tiles_all.at[k, r],
            send_sem=tile_send.at[s, step],
            recv_sem=tile_recv.at[k, r],
            device_id={"section": s, "resp": lax.rem(me_resp + step, n_resp)},
            device_id_type=MESH,
        )

    def tile_steps(s, action):
        def each(step):
            @pl.when(jnp.logical_not((s == me) & (step == 0)))
            def _():
                action(tile_copy(s, step, me, me_resp))

        loop(0, n_resp, each)

    def backward(step, carry):
        s = sections - 1 - step
        stat_acc[...] = jnp.zeros_like(stat_acc)

        def run(block, carry):
            lanes = lane_slice(block)
            wide = wide_slice(block)
            gain = gain_ref[s, :, lanes]
            short = short_ref[s, :, lanes]
            parts, saved = [], []
            for m in range(micro):
                rows = slice(m * length, (m + 1) * length)
                joined, factor = joined_rows(s, m, lanes)
                scaled = joined * factor
                normed = scaled * gain
                above = upstream[rows, lanes]
                parts.append((above * normed[prompt_len:]).astype(BF16))
                saved.append((joined[prompt_len:], scaled, normed, above))
            d_long = jnp.concatenate(parts, axis=1)
            base = pl.multiple_of(block * groups * total, groups * total)
            stacked = jnp.dot(
                toep_t[s, pl.ds(base, groups * total), :][:, :length],
                d_long,
                preferred_element_type=F32,
            )
            d_short_all = pick(stacked, total)
            turned = jnp.dot(reverse, short_out[s, :, wide], preferred_element_type=F32)
            d_wide = d_long.astype(F32)
            masked = jnp.concatenate(
                [
                    jnp.where(wide_group == g, d_wide, 0.0).astype(BF16)
                    for g in range(groups)
                ],
                axis=0,
            )
            pairs = lax.dot_general(
                masked,
                turned.astype(BF16),
                (((1,), (1,)), ((), ())),
                preferred_element_type=F32,
            )
            lines = []
            for g in range(groups):
                one = jnp.where(keep_pair, pairs[g * length : (g + 1) * length], 0.0)
                one = pltpu.roll(one, LANES + 1 - length, 1, stride=1, stride_axis=0)
                lines.append(jnp.sum(one, axis=0, keepdims=True))
            tiles_own[s, 2 * block + 1] = jnp.concatenate(lines, axis=0)
            grads = [jnp.zeros((1, LANES), F32)] * (tap_count + 1)
            for m in range(micro):
                rows = slice(m * length, (m + 1) * length)
                joined_c, scaled, normed, above = saved[m]
                d_short = d_short_all[:, m * LANES : (m + 1) * LANES]
                d_normed = d_short * short[0:1]
                grads[1] = grads[1] + jnp.sum(d_short * normed, axis=0, keepdims=True)
                for j in range(1, tap_count):
                    moved = jnp.where(
                        row_id < total - j, pltpu.roll(d_short, total - j, 0), 0.0
                    )
                    d_normed = d_normed + moved * short[j : j + 1]
                    grads[1 + j] = grads[1 + j] + jnp.sum(
                        moved * normed, axis=0, keepdims=True
                    )
                direct = above * long_out[s, rows, lanes]
                d_normed = jnp.concatenate(
                    [d_normed[:prompt_len], d_normed[prompt_len:] + direct], axis=0
                )
                grads[0] = grads[0] + jnp.sum(d_normed * scaled, axis=0, keepdims=True)
                inner = d_normed[prompt_len:] * gain
                partial[rows, lanes] = inner
                stat_acc[rows, :] += inner * joined_c
            tiles_own[s, 2 * block] = jnp.concatenate(grads, axis=0)
            return carry

        lax.fori_loop(0, blocks, run, 0)

        if direct:
            part_steps(s, lambda copy: copy.start())
            parts_in = tiles_in.at[s]
            parts_in[me_resp] = tiles_own[s, part_slice(me_resp)]

        @pl.when(s > 0)
        def _():
            line = rows_to_line(stat_acc[...])
            all_sums = start_stats(sections + 1 + step, line, line)()[0]
            factor = fac_c[s]
            pull = line_to_rows(all_sums) * (1.0 / width) * factor * factor * factor

            def finish(block, carry):
                lanes = lane_slice(block)
                grad = (
                    upstream[:, lanes]
                    + factor * partial[:, lanes]
                    - rows_in[s, :, lanes].astype(F32) * pull
                )
                upstream[:, lanes] = grad.astype(BF16).astype(F32)
                return carry

            lax.fori_loop(0, blocks, finish, 0)

        if direct:
            part_steps(s, lambda copy: copy.wait())
            tiles_sum[s] = jnp.sum(tiles_in[s], axis=0)

            @pl.when(s == me)
            def _():
                tiles_all[me, me_resp] = tiles_sum[s]

            tile_steps(s, lambda copy: copy.start())

        return carry

    lax.fori_loop(0, sections, backward, 0)

    if direct:
        loop(0, sections, lambda s: tile_steps(s, lambda copy: copy.wait_send()))

        def arrive(step):
            k, r = step // n_resp, step % n_resp

            @pl.when(jnp.logical_not((k == me) & (r == me_resp)))
            def _():
                tile_copy(0, 0, k, r).wait_recv()

        loop(0, sections * n_resp, arrive)
        gain_out, taps_short_out, taps_long_out = outs
        per_line = LANES // groups
        for line in range(sections * blocks // per_line):
            lines = []
            for place in range(per_line):
                block = line * per_line + place
                lanes = slice(block * LANES, (block + 1) * LANES)
                owner, local = divmod(2 * block, 2 * blocks)
                first, second = (divmod(local + kind, share) for kind in range(2))
                tile = tiles_all[owner, first[0], first[1]]
                gain_out[:, lanes] = tile[0:1]
                taps_short_out[:, lanes] = tile[1:]
                lines.append(tiles_all[owner, second[0], second[1]])
            lanes = slice(line * LANES, (line + 1) * LANES)
            taps_long_out[:, lanes] = jnp.transpose(jnp.concatenate(lines, axis=0))
    else:
        outs[0][...] = tiles_own[...]


def run_kernel(dims, direct, *arrays):
    sections, n_resp, micro, length, prompt_len, chans, per_group, width = dims
    rows = micro * length
    total = prompt_len + length
    group_total = chans // per_group
    tile = (8, LANES)
    tiles = 2 * chans // LANES
    share = tiles // n_resp if direct else 1
    ranks = n_resp if direct else 1
    vmem = pl.BlockSpec(memory_space=pltpu.VMEM)
    hbm = pl.BlockSpec(memory_space=pl.ANY)
    smem = pl.BlockSpec(memory_space=pltpu.SMEM)
    tap_count = arrays[3].shape[0]
    if direct:
        out_shapes = [(1, width), (tap_count, width), (LANES, width // per_group)]
    else:
        out_shapes = [(sections, tiles) + tile]
    return pl.pallas_call(
        functools.partial(kernel, dims, direct),
        out_shape=(
            jax.ShapeDtypeStruct(tile, F32),
            *(jax.ShapeDtypeStruct(shape, F32) for shape in out_shapes),
        ),
        in_specs=[hbm, hbm if direct else vmem, hbm, hbm, hbm, smem, vmem, vmem, smem],
        out_specs=(vmem,) * (1 + len(out_shapes)),
        scratch_shapes=[
            pltpu.VMEM((sections, group_total * length, 3 * LANES), BF16),
            pltpu.VMEM((sections, group_total * total, LANES), BF16),
            pltpu.VMEM((sections, ranks, prompt_len, chans), BF16),
            pltpu.VMEM((sections, micro * prompt_len, chans), BF16),
            pltpu.VMEM((sections, 1, chans), F32),
            pltpu.VMEM((sections, tap_count, chans), F32),
            pltpu.VMEM((sections, group_total, 2 * LANES), F32),
            pltpu.VMEM((sections + 1, rows, chans), BF16),
            pltpu.VMEM((sections, total, micro * chans), BF16),
            pltpu.VMEM((sections, rows, chans), F32),
            pltpu.VMEM((sections, micro * prompt_len, LANES), F32),
            pltpu.VMEM((sections, rows, LANES), F32),
            pltpu.VMEM((rows, chans), F32),
            pltpu.VMEM((rows, chans), F32),
            pltpu.VMEM((rows, LANES), F32),
            pltpu.VMEM((rows, LANES), F32),
            pltpu.VMEM((micro * prompt_len, LANES), F32),
            pltpu.VMEM((2 * sections, 2) + tile, F32),
            pltpu.VMEM((2 * sections, sections, 2) + tile, F32),
            pltpu.VMEM(tile, F32),
            pltpu.VMEM((n_resp,) + tile, F32),
            pltpu.VMEM((sections, tiles) + tile, F32),
            pltpu.VMEM((sections, ranks, share) + tile, F32),
            pltpu.VMEM((sections, share) + tile, F32),
            pltpu.VMEM((sections, ranks, share) + tile, F32),
            pltpu.SemaphoreType.DMA((5,)),
            pltpu.SemaphoreType.DMA((2, 3, sections)),
            pltpu.SemaphoreType.DMA((2, sections)),
            pltpu.SemaphoreType.DMA((2, sections, ranks)),
            pltpu.SemaphoreType.DMA((2 * sections, 2, sections)),
            pltpu.SemaphoreType.DMA((2, n_resp)),
            pltpu.SemaphoreType.DMA((2, sections, ranks)),
            pltpu.SemaphoreType.DMA((sections, ranks)),
            pltpu.SemaphoreType.DMA((sections, ranks)),
        ],
        compiler_params=pltpu.CompilerParams(
            has_side_effects=True, vmem_limit_bytes=56 * 1024 * 1024
        ),
    )(*arrays)


def body(
    completion_rows,
    prompt_pool,
    norm_gain,
    short_taps,
    long_taps,
    score_head,
    live_lengths,
    prompt_owner,
    pair_index,
):
    sections = lax.axis_size("section")
    n_resp = lax.axis_size("resp")
    me_resp = lax.axis_index("resp")
    micro, _, length, width = completion_rows.shape
    prompt_len = prompt_pool.shape[2]
    chans = width // sections
    tap_len, group_all = long_taps.shape[1:]
    per_group = width // group_all
    dims = (sections, n_resp, micro, length, prompt_len, chans, per_group, width)

    tiles = 2 * chans // LANES
    direct = n_resp <= 8 and tiles % n_resp == 0

    taps = long_taps[0].T
    flipped = jnp.concatenate([taps[:, :1], taps[:, :0:-1]], axis=1)
    taps = jnp.concatenate([flipped, taps], axis=1)
    prompts = prompt_pool[0, 0]
    if not direct:
        split = prompts.reshape(prompt_len, sections, chans).transpose(1, 0, 2)
        split = lax.all_to_all(split, "section", 0, 0, tiled=True)
        here = (prompt_owner == me_resp)[None, :, None, None]
        split = lax.psum(jnp.where(here, split[:, None], jnp.zeros((), BF16)), "resp")
        prompts = split.reshape(sections, micro * prompt_len, chans)
    rows = completion_rows.reshape(micro * length, width)
    head = score_head[None]

    ends = jnp.pad(
        pair_index.transpose(2, 0, 1),
        ((0, 0), (0, 8 - micro), (0, LANES - pair_index.shape[1])),
        constant_values=-1,
    )
    scores, *grads = run_kernel(
        dims,
        direct,
        rows,
        prompts,
        norm_gain,
        short_taps[0],
        taps,
        prompt_owner,
        head,
        ends,
        live_lengths,
    )
    scores = scores[:micro, :1].astype(BF16)
    if direct:
        return (scores, grads[0], grads[1][None], grads[2][None])
    grads = lax.psum(grads[0], "resp")
    grads = lax.all_to_all(grads, "section", 0, 0, tiled=True)
    grads = grads.reshape(sections * tiles // 2, 2, 8, LANES)
    gs_grad = grads[:, 0].transpose(1, 0, 2).reshape(8, width)
    taps_grad = grads[:, 1].reshape(group_all, tap_len).T
    return (
        scores,
        gs_grad[:1],
        gs_grad[None, 1:],
        taps_grad[None],
    )


def wide_kernel(
    dims,
    comp_hbm,
    prompt_hbm,
    gain_hbm,
    short_hbm,
    taps_hbm,
    head_hbm,
    owner_ref,
    pair_ref,
    length_ref,
    score_ref,
    gain_out,
    taps_short_out,
    taps_long_out,
    comp_full,
    prompt_full,
    taps_full,
    head_own,
    comp_in,
    pool,
    gain_in,
    short_in,
    taps_src,
    taps_in,
    order_c,
    order_p,
    lined,
    first_out,
    first_in,
    stat_out,
    stat_in,
    rows_in,
    prompt_rows,
    long_out,
    short_out,
    toep,
    toep_p,
    toep_t,
    params,
    heads,
    fac_c,
    fac_p,
    normed_buf,
    d_short_buf,
    upstream,
    inner_buf,
    d_long_buf,
    acc_ref,
    tiles_own,
    tiles_all,
    local_sem,
    comp_send,
    comp_recv,
    weight_send,
    weight_recv,
    pool_send,
    pool_recv,
    first_send,
    first_recv,
    stat_send,
    stat_recv,
    tile_send,
    tile_recv,
):
    sections, n_resp, micro, length, chans, per_group, width = dims
    comps = micro * n_resp
    ranks = sections * n_resp
    blocks = chans // LANES
    per_block = LANES // per_group
    groups = blocks * per_block
    tap_count = short_in.shape[1]
    total = 2 * length
    me = lax.axis_index("section")
    me_resp = lax.axis_index("resp")
    rank = me_resp * sections + me

    def loop(low, high, step_of):
        def run(index, carry):
            step_of(index)
            return carry

        lax.fori_loop(low, high, run, 0)

    def place(peer):
        return {"section": lax.rem(peer, sections), "resp": peer // sections}

    def lanes_of(peer):
        return pl.ds(pl.multiple_of(peer * chans, chans), chans)

    def groups_of(peer):
        return pl.ds(pl.multiple_of(peer * groups, groups), groups)

    def remote(src, dst, send_sem, recv_sem, device):
        return pltpu.make_async_remote_copy(
            src_ref=src,
            dst_ref=dst,
            send_sem=send_sem,
            recv_sem=recv_sem,
            device_id=device,
            device_id_type=MESH,
        )

    load_comp = pltpu.make_async_copy(comp_hbm, comp_full, local_sem.at[0])
    load_prompt = pltpu.make_async_copy(prompt_hbm, prompt_full, local_sem.at[1])
    load_taps = pltpu.make_async_copy(taps_hbm, taps_full, local_sem.at[2])
    load_head = pltpu.make_async_copy(head_hbm.at[:, lanes_of(rank)], head_own, local_sem.at[3])
    own_comp = pltpu.make_async_copy(
        comp_hbm.at[:, lanes_of(rank)], comp_in.at[me_resp], local_sem.at[4]
    )
    own_pool = pltpu.make_async_copy(
        prompt_hbm.at[:, lanes_of(rank)], pool.at[me, me_resp], local_sem.at[5]
    )
    own_gain = pltpu.make_async_copy(
        gain_hbm.at[:, lanes_of(rank)], gain_in.at[me], local_sem.at[6]
    )
    own_short = pltpu.make_async_copy(
        short_hbm.at[:, :, lanes_of(rank)], short_in.at[me], local_sem.at[7]
    )

    def comp_copy(step):
        peer_resp = lax.rem(me_resp + step, n_resp)
        return remote(
            comp_hbm.at[:, lanes_of(peer_resp * sections + me)],
            comp_in.at[me_resp],
            comp_send.at[step],
            comp_recv.at[me_resp],
            {"resp": peer_resp},
        )

    def comp_wait(step):
        source = lax.rem(me_resp + step, n_resp)
        remote(
            comp_hbm.at[:, lanes_of(rank)],
            comp_in.at[source],
            comp_send.at[step],
            comp_recv.at[source],
            {"resp": source},
        ).wait_recv()

    def weight_parts(peer_rank, source):
        return (
            (gain_hbm.at[:, lanes_of(peer_rank)], gain_in.at[source]),
            (short_hbm.at[:, :, lanes_of(peer_rank)], short_in.at[source]),
            (taps_src.at[groups_of(peer_rank), :], taps_in.at[source]),
        )

    def weight_copy(kind, step):
        peer = lax.rem(me + step, sections)
        src, dst = weight_parts(me_resp * sections + peer, me)[kind]
        return remote(
            src, dst, weight_send.at[kind, step], weight_recv.at[kind, me], {"section": peer}
        )

    def weight_wait(kind, step):
        source = lax.rem(me + step, sections)
        src, dst = weight_parts(rank, source)[kind]
        remote(
            src,
            dst,
            weight_send.at[kind, step],
            weight_recv.at[kind, source],
            {"section": source},
        ).wait_recv()

    def pool_copy(step):
        peer = lax.rem(rank + step, ranks)
        return remote(
            prompt_hbm.at[:, lanes_of(peer)],
            pool.at[me, me_resp],
            pool_send.at[step],
            pool_recv.at[rank],
            place(peer),
        )

    def pool_wait(s):
        def each(r):
            source = r * sections + s

            @pl.when(source != rank)
            def _():
                remote(
                    prompt_hbm.at[:, lanes_of(rank)],
                    pool.at[s, r],
                    pool_send.at[0],
                    pool_recv.at[source],
                    place(source),
                ).wait_recv()

            @pl.when(source == rank)
            def _():
                own_pool.wait()

        loop(0, n_resp, each)

    def first_copy(step):
        peer = lax.rem(rank + step, ranks)
        return remote(
            first_out, first_in.at[rank], first_send.at[step], first_recv.at[rank], place(peer)
        )

    def first_wait(step):
        source = lax.rem(rank + step, ranks)
        remote(
            first_out,
            first_in.at[source],
            first_send.at[step],
            first_recv.at[source],
            place(source),
        ).wait_recv()

    def stat_start(slot, tile):
        stat_out[slot] = tile
        for step in range(1, ranks):
            peer = lax.rem(rank + step, ranks)
            remote(
                stat_out.at[slot],
                stat_in.at[slot, rank],
                stat_send.at[slot, step],
                stat_recv.at[slot, rank],
                place(peer),
            ).start()
        stat_in[slot, rank] = tile

    def stat_finish(slot):
        for step in range(1, ranks):
            source = lax.rem(rank + step, ranks)
            remote(
                stat_out.at[slot],
                stat_in.at[slot, source],
                stat_send.at[slot, step],
                stat_recv.at[slot, source],
                place(source),
            ).wait_recv()
        return jnp.sum(stat_in[slot], axis=0)

    def tile_copy(s, step):
        return remote(
            tiles_own.at[s],
            tiles_all.at[rank],
            tile_send.at[s, step],
            tile_recv.at[rank],
            {"section": s, "resp": lax.rem(me_resp + step, n_resp)},
        )

    def tile_steps(s, action):
        def each(step):
            @pl.when(jnp.logical_not((s == me) & (step == 0)))
            def _():
                action(tile_copy(s, step))

        loop(0, n_resp, each)

    for copy in (load_taps, load_comp, load_prompt, load_head):
        copy.start()
    for copy in (own_comp, own_pool, own_gain, own_short):
        copy.start()
    barrier = pltpu.get_barrier_semaphore()
    loop(
        1,
        ranks,
        lambda step: pl.semaphore_signal(
            barrier,
            inc=1,
            device_id=place(lax.rem(rank + step, ranks)),
            device_id_type=MESH,
        ),
    )

    tile_row = lax.broadcasted_iota(jnp.int32, (LANES, LANES), 0)
    tile_lane = lax.broadcasted_iota(jnp.int32, (LANES, LANES), 1)
    row_target = (tile_row // per_group) * LANES + tile_row % per_group
    prompt_key = (tile_lane // (n_resp * per_group)) * (n_resp * per_group) + (
        tile_lane % per_group
    )

    def fill_order(c):
        rows = pl.ds(pl.multiple_of(c * LANES, LANES), LANES)
        for n in range(per_block):
            hit = row_target + c * per_group == tile_lane + n * LANES
            order_c[rows, n * LANES : (n + 1) * LANES] = jnp.where(hit, 1.0, 0.0).astype(BF16)

    loop(0, comps, fill_order)
    for m in range(micro):
        for n in range(per_block):
            hit = row_target + m * n_resp * per_group == prompt_key + n * LANES
            order_p[m * LANES : (m + 1) * LANES, n * LANES : (n + 1) * LANES] = jnp.where(
                hit, 1.0, 0.0
            ).astype(BF16)
    pad = 8
    for g in range(groups):
        normed_buf[g, :pad] = jnp.zeros((pad, LANES), F32)
        d_short_buf[g, total:] = jnp.zeros((pad, LANES), F32)

    pl.semaphore_wait(barrier, ranks - 1)
    loop(1, n_resp, lambda step: comp_copy(step).start())

    @pl.when(me == 0)
    def _():
        loop(1, ranks, lambda step: pool_copy(step).start())

    def start_vectors(step):
        weight_copy(0, step).start()
        weight_copy(1, step).start()

    loop(1, sections, start_vectors)

    load_taps.wait()
    upright = jnp.transpose(taps_full[...])
    mirror = jnp.where(lax.rem(tile_row + tile_lane, LANES) == 0, 1.0, 0.0)
    taps_src[:, :LANES] = jnp.dot(
        upright, mirror, preferred_element_type=F32, precision=lax.Precision.HIGHEST
    )
    taps_src[:, LANES:] = upright
    loop(1, sections, lambda step: weight_copy(2, step).start())
    taps_in[me] = taps_src[groups_of(rank), :]

    ones = jnp.ones((16, 2 * LANES), BF16)

    def split(values):
        high = values.astype(BF16)
        return high, (values - high.astype(F32)).astype(BF16)

    def lane_sums(acc, weights):
        both = jnp.concatenate(split(acc), axis=1)
        if both.shape[0] < LANES:
            both = jnp.concatenate([both, jnp.zeros_like(both)], axis=0)
        return lax.dot_general(
            weights, both, (((1,), (1,)), ((), ())), preferred_element_type=F32
        )[:8]

    def square_rows(ref):
        def step(block, acc):
            values = ref[:, pl.ds(pl.multiple_of(block * LANES, LANES), LANES)].astype(F32)
            return acc + values * values

        return lax.fori_loop(
            0, width // LANES, step, jnp.zeros((ref.shape[0], LANES), F32), unroll=2
        )

    load_comp.wait()
    comp_line = lane_sums(square_rows(comp_full), ones)
    load_prompt.wait()
    prompt_line = lane_sums(square_rows(prompt_full), ones)
    eight_row = lax.broadcasted_iota(jnp.int32, (8, LANES), 0)
    eight_lane = lax.broadcasted_iota(jnp.int32, (8, LANES), 1)
    message = jnp.where(eight_row == 0, comp_line, prompt_line)
    for m in range(micro):
        count = jnp.full((8, LANES), length_ref[0, m], jnp.int32).astype(F32)
        message = jnp.where(eight_row == 2 + m, count, message)
    first_out[...] = message
    loop(1, ranks, lambda step: first_copy(step).start())
    first_in[rank] = message

    @pl.when(me != 0)
    def _():
        loop(1, ranks, lambda step: pool_copy(step).start())

    own_gain.wait()
    own_short.wait()
    load_head.wait()

    def weights_arrive(step):
        for kind in range(3):
            weight_wait(kind, step)

    loop(1, sections, weights_arrive)

    def tile_lanes(values, n):
        out = pltpu.roll(values, (LANES - n * per_group) % LANES, 1)
        out = jnp.where(eight_lane < per_group, out, 0.0)
        span = per_group
        while span < LANES:
            out = out + pltpu.roll(out, span, 1)
            span *= 2
        return out

    t_row = lax.broadcasted_iota(jnp.int32, (length, LANES), 0)
    s_lane = lax.broadcasted_iota(jnp.int32, (length, LANES), 1)
    keep = s_lane <= length + t_row
    keep_t = tile_row <= length + tile_lane

    def spread_params(s):
        for b in range(blocks):
            lanes = slice(b * LANES, (b + 1) * LANES)
            rows = jnp.concatenate(
                [gain_in[s, :, lanes]] + [short_in[s, j, :, lanes] for j in range(tap_count)],
                axis=0,
            )
            for n in range(per_block):
                params[s, b * per_block + n] = tile_lanes(rows, n)

    loop(0, sections, spread_params)
    for b in range(blocks):
        rows = jnp.broadcast_to(head_own[:, b * LANES : (b + 1) * LANES], (8, LANES))
        for n in range(per_block):
            heads[b * per_block + n] = tile_lanes(rows, n)

    def build(index):
        s, g = index // groups, lax.rem(index, groups)
        line = taps_in[s, pl.ds(g, 1), :]
        wide = jnp.broadcast_to(line[:, :LANES], (length, LANES))
        wide = pltpu.roll(wide, length, 1, stride=1, stride_axis=0)
        wide = jnp.where(keep, wide, 0.0)
        high = wide.astype(BF16).astype(F32)
        low = pltpu.roll(wide - high, length, 1)
        swapped = pltpu.roll(high, length, 1)
        first = s_lane < length
        toep_p[s, g] = jnp.where(first, high, low).astype(BF16)
        low = wide - high
        toep[s, g] = jnp.where(first, swapped, low).astype(BF16)
        wide = jnp.broadcast_to(line[:, LANES:], (total, LANES))
        wide = pltpu.roll(wide, length, 1, stride=1, stride_axis=0)
        toep_t[s, g] = jnp.where(keep_t, wide, 0.0).astype(BF16)

    loop(0, sections * groups, build)

    def spread_rows(lines):
        tall = jnp.concatenate(
            [jnp.broadcast_to(lines[c : c + 1], (per_group, LANES)) for c in range(comps)],
            axis=0,
        )
        return jnp.transpose(tall)[:length]

    def to_factor(sums):
        return lax.rsqrt(sums * (1.0 / width) + 1e-06)

    loop(1, ranks, first_wait)
    own_lines = jnp.concatenate(
        [first_in[r * sections + me, 0:1] for r in range(n_resp)], axis=0
    )
    own_lines = jnp.concatenate(
        [
            own_lines if m == 0 else pltpu.roll(own_lines, LANES - m * length, 1)
            for m in range(micro)
        ],
        axis=0,
    )
    fac_c[0] = spread_rows(to_factor(own_lines))

    def prompt_factor(s):
        lines = []
        for m in range(micro):
            owner = jnp.full((8, LANES), owner_ref[m], jnp.int32)
            line = jnp.zeros((8, LANES), F32)
            for r in range(n_resp):
                line = jnp.where(owner == r, first_in[r * sections + s], line)
            lines += [line[1:2]] * n_resp
        fac_p[s] = spread_rows(to_factor(jnp.concatenate(lines, axis=0)))

    loop(0, sections, prompt_factor)

    def conv_short(ref, g, start, taps):
        out = ref[g, pl.ds(start, length)] * taps[1:2]
        for j in range(1, tap_count):
            out = out + ref[g, pl.ds(start - j, length)] * taps[1 + j : 2 + j]
        return out

    def conv_long(matrix, high, low):
        left = jnp.concatenate([matrix, matrix], axis=1)
        right = jnp.concatenate([high, high, low, low], axis=0)
        return jnp.dot(left, right, preferred_element_type=F32)

    def prepare(s):
        pool_wait(s)
        sides = []
        for b in range(blocks):
            lanes = slice(b * LANES, (b + 1) * LANES)
            row = []
            for m in range(micro):
                owner = jnp.full((length, LANES), owner_ref[m], jnp.int32)
                picked = pool[s, 0, :, lanes].astype(F32)
                for r in range(1, n_resp):
                    picked = jnp.where(owner == r, pool[s, r, :, lanes].astype(F32), picked)
                row.append(picked.astype(BF16))
            sides.append(jnp.concatenate(row, axis=1))
        side = jnp.concatenate(sides, axis=0)
        step = 2 * LANES
        for n in range(per_block // 2):
            part = jnp.dot(
                side, order_p[:, n * step : (n + 1) * step], preferred_element_type=F32
            ).astype(BF16)
            for b in range(blocks):
                for k in range(2):
                    prompt_rows[s, b * per_block + 2 * n + k] = part[
                        b * length : (b + 1) * length, k * LANES : (k + 1) * LANES
                    ]
        factor = fac_p[s]

        def each(g):
            taps = params[s, g]
            normed = prompt_rows[s, g].astype(F32) * factor * taps[0:1]
            normed_buf[g, pl.ds(pad, length)] = normed
            shorter = conv_short(normed_buf, g, pad, taps)
            high, low = split(shorter)
            short_out[s, g, :length] = high
            long_out[s, g] = conv_long(toep_p[s, g], high, low)

        loop(0, groups, each)

    loop(1, n_resp, comp_wait)
    own_comp.wait()
    for b in range(blocks):
        lanes = slice(b * LANES, (b + 1) * LANES)
        for m in range(micro):
            for r in range(n_resp):
                c = m * n_resp + r
                lined[b * length : (b + 1) * length, c * LANES : (c + 1) * LANES] = comp_in[
                    r, m * length : (m + 1) * length, lanes
                ]
    for n in range(per_block // 2):
        step = 2 * LANES
        part = jnp.dot(
            lined[...], order_c[:, n * step : (n + 1) * step], preferred_element_type=F32
        ).astype(BF16)
        for b in range(blocks):
            for k in range(2):
                rows_in[0, b * per_block + 2 * n + k] = part[
                    b * length : (b + 1) * length, k * LANES : (k + 1) * LANES
                ]
    prepare(0)

    fold_row = lax.broadcasted_iota(jnp.int32, (16, 2 * LANES), 0)
    fold_lane = lax.broadcasted_iota(jnp.int32, (16, 2 * LANES), 1)
    fold = jnp.where((fold_lane % LANES) // per_group == fold_row, 1.0, 0.0).astype(BF16)

    def forward(s, last):
        acc_ref[...] = jnp.zeros_like(acc_ref)
        factor = fac_c[s]

        def each(g):
            taps = params[s, g]
            rows = rows_in[s, g].astype(F32)
            normed = rows * factor * taps[0:1]
            normed_buf[g, pl.ds(pad + length, length)] = normed
            shorter = conv_short(normed_buf, g, pad + length, taps)
            high, low = split(shorter)
            short_out[s, g, length:] = high
            longer = long_out[s, g] + conv_long(toep[s, g], high, low)
            long_out[s, g] = longer
            mixed = (rows + normed * longer).astype(BF16)
            if not last:
                rows_in[s + 1, g] = mixed
            mixed = mixed.astype(F32)
            acc_ref[...] += mixed * (heads[g, 0:1] if last else mixed)

        loop(0, groups, each)

    def forward_step(s):
        forward(s, False)
        stat_start(s, lane_sums(acc_ref[...], fold))
        prepare(s + 1)
        fac_c[s + 1] = spread_rows(to_factor(stat_finish(s)))

    loop(0, sections - 1, forward_step)
    forward(sections - 1, True)

    comp_lane = eight_lane // per_group
    counts = jnp.zeros((8, LANES), F32)
    for m in range(micro):
        for r in range(n_resp):
            row = first_in[r * sections + me, 2 + m : 3 + m]
            counts = jnp.where(comp_lane == m * n_resp + r, row, counts)
    alive = t_row.astype(F32) < counts[0:1]
    live = jnp.where(alive, 1.0, 0.0) / jnp.sqrt(counts[0:1])
    score_slot = sections - 1
    line = jnp.sum(acc_ref[...] * live, axis=0, keepdims=True)
    stat_start(score_slot, jnp.broadcast_to(line, (8, LANES)))
    winner = jnp.full((8, LANES), -1, jnp.int32)
    loser = winner
    for m in range(micro):
        for p in range(pair_ref.shape[2]):
            here = (eight_row == m) & (eight_lane == p)
            winner = jnp.where(here, pair_ref[m, 0, p], winner)
            loser = jnp.where(here, pair_ref[m, 1, p], loser)
    signs = [
        jnp.where(winner == r, 1.0, 0.0) - jnp.where(loser == r, 1.0, 0.0)
        for r in range(n_resp)
    ]
    partials = stat_finish(score_slot)
    masks = [comp_lane == eight_row * n_resp + r for r in range(n_resp)]
    scores = [
        jnp.sum(jnp.where(masks[r], partials, 0.0), axis=1, keepdims=True)
        for r in range(n_resp)
    ]
    own_score = scores[0]
    margin = jnp.zeros((8, LANES), F32)
    for r in range(n_resp):
        margin = margin + scores[r] * signs[r]
        own_score = jnp.where(me_resp == r, scores[r], own_score)
    score_ref[...] = jnp.broadcast_to(own_score, (8, LANES))
    weight = 1.0 / (1.0 + jnp.exp(margin))
    slopes = jnp.zeros((8, LANES), F32)
    for r in range(n_resp):
        slope = -jnp.sum(signs[r] * weight, axis=1, keepdims=True)
        slopes = jnp.where(masks[r], slope, slopes)
    seeds = live * jnp.sum(slopes, axis=0, keepdims=True)

    def seed(g):
        upstream[g] = seeds * heads[g, 0:1]

    loop(0, groups, seed)

    def backward(s, last):
        acc_ref[...] = jnp.zeros_like(acc_ref)
        factor = fac_c[s]

        def each(g):
            taps = params[s, g]
            rows = rows_in[s, g].astype(F32)
            above = upstream[g]
            d_long = (above * (rows * factor * taps[0:1])).astype(BF16)
            d_long_buf[g] = d_long
            d_short_buf[g, pl.ds(0, total)] = jnp.dot(
                toep_t[s, g][:, :length], d_long, preferred_element_type=F32
            )
            if last:
                return
            d_normed = above * long_out[s, g]
            for j in range(tap_count):
                d_normed = d_normed + d_short_buf[g, pl.ds(length + j, length)] * taps[1 + j : 2 + j]
            inner = d_normed * taps[0:1]
            inner_buf[g] = inner
            acc_ref[...] += inner * rows

        loop(0, groups, each)

    keep_pair = total - 1 - s_lane <= length + t_row
    reverse = jnp.where(tile_row + tile_lane == total - 1, 1.0, 0.0).astype(BF16)

    def gradients(s):
        factor_c = fac_c[s]
        factor_p = fac_p[s]

        def each(g):
            taps = params[s, g]
            scaled_p = prompt_rows[s, g].astype(F32) * factor_p
            scaled_c = rows_in[s, g].astype(F32) * factor_c
            lines = [
                jnp.sum(upstream[g] * long_out[s, g] * scaled_c, axis=0, keepdims=True)
            ]
            for j in range(tap_count):
                part = (
                    d_short_buf[g, pl.ds(j, length)] * scaled_p
                    + d_short_buf[g, pl.ds(length + j, length)] * scaled_c
                )
                lines.append(jnp.sum(part, axis=0, keepdims=True))
            tile = jnp.concatenate(lines, axis=0)
            span = per_group
            while span < LANES:
                tile = tile + pltpu.roll(tile, span, 1)
                span *= 2
            top = tile + jnp.sum(
                jnp.where(eight_row > 0, tile * taps, 0.0), axis=0, keepdims=True
            )
            tile = jnp.where(eight_row == 0, top, tile * taps[0:1])
            b, n = g // per_block, lax.rem(g, per_block)
            tiles_own[s, b] = jnp.where(comp_lane == n, tile, tiles_own[s, b])
            turned = jnp.dot(reverse, short_out[s, g], preferred_element_type=F32)
            pairs = lax.dot_general(
                d_long_buf[g],
                turned.astype(BF16),
                (((1,), (1,)), ((), ())),
                preferred_element_type=F32,
            )
            pairs = jnp.where(keep_pair, pairs, 0.0)
            pairs = pltpu.roll(pairs, LANES + 1 - length, 1, stride=1, stride_axis=0)
            tiles_own[s, blocks + g // 8, pl.ds(lax.rem(g, 8), 1)] = jnp.sum(
                pairs, axis=0, keepdims=True
            )

        for b in range(blocks):
            tiles_own[s, b] = jnp.zeros((8, LANES), F32)
        loop(0, groups, each)

        @pl.when(s == me)
        def _():
            tiles_all[rank] = tiles_own[s]

        tile_steps(s, lambda copy: copy.start())

    def backward_step(step):
        s = sections - 1 - step
        slot = sections + step
        backward(s, False)
        stat_start(slot, lane_sums(acc_ref[...], fold))
        gradients(s)
        factor = fac_c[s]
        pull = spread_rows(stat_finish(slot) * (1.0 / width)) * factor * factor * factor

        def finish(g):
            grad = upstream[g] + factor * inner_buf[g] - rows_in[s, g].astype(F32) * pull
            upstream[g] = grad.astype(BF16).astype(F32)

        loop(0, groups, finish)

    loop(0, sections - 1, backward_step)
    backward(0, True)
    gradients(0)

    loop(1, n_resp, lambda step: comp_copy(step).wait_send())

    def weights_sent(step):
        for kind in range(3):
            weight_copy(kind, step).wait_send()

    loop(1, sections, weights_sent)

    def ranks_sent(step):
        pool_copy(step).wait_send()
        first_copy(step).wait_send()

    loop(1, ranks, ranks_sent)

    def stats_sent(index):
        slot, step = index // (ranks - 1), 1 + lax.rem(index, ranks - 1)
        remote(
            stat_out.at[slot],
            stat_in.at[slot, rank],
            stat_send.at[slot, step],
            stat_recv.at[slot, rank],
            place(lax.rem(rank + step, ranks)),
        ).wait_send()

    loop(0, (2 * sections - 1) * (ranks - 1), stats_sent)
    loop(0, sections, lambda s: tile_steps(s, lambda copy: copy.wait_send()))

    def arrive(step):
        source = lax.rem(rank + step, ranks)
        remote(
            tiles_own.at[0],
            tiles_all.at[source],
            tile_send.at[0, 0],
            tile_recv.at[source],
            place(source),
        ).wait_recv()

    loop(1, ranks, arrive)
    lines = []
    for q in range(ranks):
        for b in range(blocks):
            lanes = slice((q * blocks + b) * LANES, (q * blocks + b + 1) * LANES)
            tile = tiles_all[q, b]
            gain_out[:, lanes] = tile[0:1]
            for j in range(tap_count):
                taps_short_out[j, :, lanes] = tile[1 + j : 2 + j]
        lines += [tiles_all[q, blocks + k] for k in range(groups // 8)]
    taps_long_out[...] = jnp.transpose(jnp.concatenate(lines, axis=0))


def run_wide(dims, *arrays):
    sections, n_resp, micro, length, chans, per_group, width = dims
    comps = micro * n_resp
    ranks = sections * n_resp
    groups = chans // per_group
    blocks = chans // LANES
    total = 2 * length
    tap_count = arrays[3].shape[0]
    group_all = width // per_group
    tile = (8, LANES)
    tiles = blocks + groups // 8
    vmem = pl.BlockSpec(memory_space=pltpu.VMEM)
    hbm = pl.BlockSpec(memory_space=pl.ANY)
    smem = pl.BlockSpec(memory_space=pltpu.SMEM)
    slots = 2 * sections - 1
    per = (sections, groups)
    dma = pltpu.SemaphoreType.DMA
    return pl.pallas_call(
        functools.partial(wide_kernel, dims),
        out_shape=(
            jax.ShapeDtypeStruct(tile, F32),
            jax.ShapeDtypeStruct((1, width), F32),
            jax.ShapeDtypeStruct((tap_count, 1, width), F32),
            jax.ShapeDtypeStruct((LANES, group_all), F32),
        ),
        in_specs=[hbm] * 6 + [smem] * 3,
        out_specs=(vmem,) * 4,
        scratch_shapes=[
            pltpu.VMEM((micro * length, width), BF16),
            pltpu.VMEM((length, width), BF16),
            pltpu.VMEM((LANES, group_all), F32),
            pltpu.VMEM((1, chans), F32),
            pltpu.VMEM((n_resp, micro * length, chans), BF16),
            pltpu.VMEM((sections, n_resp, length, chans), BF16),
            pltpu.VMEM((sections, 1, chans), F32),
            pltpu.VMEM((sections, tap_count, 1, chans), F32),
            pltpu.VMEM((group_all, 2 * LANES), F32),
            pltpu.VMEM((sections, groups, 2 * LANES), F32),
            pltpu.VMEM((comps * LANES, (LANES // per_group) * LANES), BF16),
            pltpu.VMEM((micro * LANES, (LANES // per_group) * LANES), BF16),
            pltpu.VMEM((blocks * length, comps * LANES), BF16),
            pltpu.VMEM(tile, F32),
            pltpu.VMEM((ranks,) + tile, F32),
            pltpu.VMEM((slots,) + tile, F32),
            pltpu.VMEM((slots, ranks) + tile, F32),
            pltpu.VMEM(per + (length, LANES), BF16),
            pltpu.VMEM(per + (length, LANES), BF16),
            pltpu.VMEM(per + (length, LANES), F32),
            pltpu.VMEM(per + (total, LANES), BF16),
            pltpu.VMEM(per + (length, LANES), BF16),
            pltpu.VMEM(per + (length, LANES), BF16),
            pltpu.VMEM(per + (total, LANES), BF16),
            pltpu.VMEM(per + tile, F32),
            pltpu.VMEM((groups,) + tile, F32),
            pltpu.VMEM((sections, length, LANES), F32),
            pltpu.VMEM((sections, length, LANES), F32),
            pltpu.VMEM((groups, 8 + total, LANES), F32),
            pltpu.VMEM((groups, total + 8, LANES), F32),
            pltpu.VMEM((groups, length, LANES), F32),
            pltpu.VMEM((groups, length, LANES), F32),
            pltpu.VMEM((groups, length, LANES), BF16),
            pltpu.VMEM((length, LANES), F32),
            pltpu.VMEM((sections, tiles) + tile, F32),
            pltpu.VMEM((ranks, tiles) + tile, F32),
            dma((8,)),
            dma((n_resp,)),
            dma((n_resp,)),
            dma((3, sections)),
            dma((3, sections)),
            dma((ranks,)),
            dma((ranks,)),
            dma((ranks,)),
            dma((ranks,)),
            dma((slots, ranks)),
            dma((slots, ranks)),
            dma((sections, n_resp)),
            dma((ranks,)),
        ],
        compiler_params=pltpu.CompilerParams(
            collective_id=1, has_side_effects=True, vmem_limit_bytes=56 * 1024 * 1024
        ),
    )(*arrays)


def wide_body(
    completion_rows,
    prompt_pool,
    norm_gain,
    short_taps,
    long_taps,
    score_head,
    live_lengths,
    prompt_owner,
    pair_index,
):
    sections = lax.axis_size("section")
    n_resp = lax.axis_size("resp")
    micro, _, length, width = completion_rows.shape
    chans = width // (sections * n_resp)
    per_group = width // long_taps.shape[2]
    scores, gain_grad, short_grad, long_grad = run_wide(
        (sections, n_resp, micro, length, chans, per_group, width),
        completion_rows.reshape(micro * length, width),
        prompt_pool[0, 0],
        norm_gain,
        short_taps.transpose(1, 0, 2),
        long_taps[0],
        score_head[None],
        prompt_owner,
        pair_index.transpose(0, 2, 1),
        live_lengths.T,
    )
    return (
        scores[:micro, :1].astype(BF16),
        gain_grad,
        short_grad.transpose(1, 0, 2),
        long_grad[None],
    )


def is_wide(
    completion_rows,
    prompt_pool,
    norm_gain,
    short_taps,
    long_taps,
    score_head,
    live_lengths,
    prompt_owner,
    pair_index,
):
    sections = lax.axis_size("section")
    n_resp = lax.axis_size("resp")
    micro, _, length, width = completion_rows.shape
    per_group = width // long_taps.shape[2]
    return (
        micro * n_resp * per_group == LANES
        and micro * n_resp == 8
        and width % (sections * n_resp * LANES) == 0
        and prompt_pool.shape[2] == length
        and long_taps.shape[1] == 2 * length == LANES
        and micro * length == LANES
        and short_taps.shape[1] == 7
    )


def either(*arrays):
    return wide_body(*arrays) if is_wide(*arrays) else body(*arrays)


def solution(mesh):
    placed = (
        P(None, ("groups", "resp"), None, None),
        P("section", ("groups", "resp"), None, None),
        P("section", None),
        P("section", None, None),
        P("section", None, None),
        P(),
        P(None, ("groups", "resp")),
        P("groups"),
        P(None, "groups", None),
    )
    return jax.shard_map(
        either,
        mesh=mesh,
        in_specs=placed,
        out_specs=(
            P(None, ("groups", "resp")),
            P("section", "groups"),
            P("section", "groups", None),
            P("section", "groups", None),
        ),
        check_vma=False,
    )
```

```python
import functools

import jax
import jax.numpy as jnp
from jax import lax
from jax.experimental import pallas as pl
from jax.experimental.pallas import tpu as pltpu
from jax.sharding import PartitionSpec as P

LANES = 128
MESH = pl.DeviceIdType.MESH
F32 = jnp.float32
BF16 = jnp.bfloat16


def rows_to_line(block):
    line = jnp.sum(jnp.transpose(block), axis=0, keepdims=True)
    return jnp.broadcast_to(line, (8, LANES))


def line_to_rows(tile):
    return jnp.transpose(jnp.broadcast_to(tile[0:1], (LANES, LANES)))


def kernel(
    dims,
    direct,
    comp_ref,
    prompt_ref,
    gain_hbm,
    short_hbm,
    taps_hbm,
    owner_ref,
    head_ref,
    ends_ref,
    length_ref,
    score_ref,
    *rest,
):
    sections, n_resp, micro, length, prompt_len, chans, per_group, width = dims
    outs, rest = (rest[:3], rest[3:]) if direct else (rest[:1], rest[1:])
    (
        toep,
        toep_t,
        pool,
        chosen_rows,
        gain_ref,
        short_ref,
        taps_ref,
        rows_in,
        short_out,
        long_out,
        fac_p,
        fac_c,
        upstream,
        partial,
        stat_acc,
        score_acc,
        prompt_acc,
        stat_out,
        stat_in,
        resp_out,
        resp_in,
        tiles_own,
        tiles_in,
        tiles_sum,
        tiles_all,
        local_sem,
        weight_sems,
        spread_sems,
        pool_sems,
        stat_sems,
        resp_sems,
        part_sems,
        tile_send,
        tile_recv,
    ) = rest
    groups = LANES // per_group
    blocks = chans // LANES
    group_rows = blocks * groups
    total = prompt_len + length
    me = lax.axis_index("section")
    me_resp = lax.axis_index("resp")
    own_lanes = pl.ds(pl.multiple_of(me * chans, chans), chans)

    def lane_slice(block):
        return pl.ds(pl.multiple_of(block * LANES, LANES), LANES)

    def head_slice(block):
        return pl.ds(pl.multiple_of(me * chans + block * LANES, LANES), LANES)

    def wide_slice(block):
        return pl.ds(pl.multiple_of(block * micro * LANES, LANES), micro * LANES)

    def loop(low, high, step_of):
        def run(index, carry):
            step_of(index)
            return carry

        lax.fori_loop(low, high, run, 0)

    def swap(axis, count, mine, out_ref, in_ref, sems):
        def copy(step):
            return pltpu.make_async_remote_copy(
                src_ref=out_ref,
                dst_ref=in_ref.at[mine],
                send_sem=sems.at[0, step],
                recv_sem=sems.at[1, step],
                device_id={axis: lax.rem(mine + step, count)},
                device_id_type=MESH,
            )

        loop(1, count, lambda step: copy(step).start())
        in_ref[mine] = out_ref[...]
        return lambda: loop(1, count, lambda step: copy(step).wait())

    def start_stats(slot, first, second):
        stat_out[slot, 0] = first
        stat_out[slot, 1] = second
        wait = swap(
            "section", sections, me, stat_out.at[slot], stat_in.at[slot], stat_sems.at[slot]
        )

        def finish():
            wait()
            return jnp.sum(stat_in[slot], axis=0)

        return finish

    def weight_copies(step):
        peer = lax.rem(me + step, sections)
        lanes = pl.ds(pl.multiple_of(peer * chans, chans), chans)
        rows = pl.ds(pl.multiple_of(peer * group_rows, group_rows), group_rows)
        return [
            pltpu.make_async_remote_copy(
                src_ref=source,
                dst_ref=target,
                send_sem=weight_sems.at[0, kind, step],
                recv_sem=weight_sems.at[1, kind, step],
                device_id={"section": peer},
                device_id_type=MESH,
            )
            for kind, source, target in (
                (0, gain_hbm.at[:, lanes], gain_ref.at[me]),
                (2, short_hbm.at[:, lanes], short_ref.at[me]),
                (1, taps_hbm.at[rows, :], taps_ref.at[me]),
            )
        ]

    def start_weights(step):
        for copy in weight_copies(step):
            copy.start()

    def wait_weights(step):
        for copy in weight_copies(step):
            copy.wait()

    own_rows = pl.ds(pl.multiple_of(me * group_rows, group_rows), group_rows)
    local_copies = [
        pltpu.make_async_copy(comp_ref.at[:, own_lanes], rows_in.at[0], local_sem.at[0]),
        pltpu.make_async_copy(gain_hbm.at[:, own_lanes], gain_ref.at[me], local_sem.at[1]),
        pltpu.make_async_copy(short_hbm.at[:, own_lanes], short_ref.at[me], local_sem.at[3]),
        pltpu.make_async_copy(taps_hbm.at[own_rows, :], taps_ref.at[me], local_sem.at[2]),
    ]

    def spread_copy(step):
        peer = lax.rem(me + step, sections)
        lanes = pl.ds(pl.multiple_of(peer * chans, chans), chans)
        return pltpu.make_async_remote_copy(
            src_ref=prompt_ref.at[:, lanes],
            dst_ref=pool.at[me, me_resp],
            send_sem=spread_sems.at[0, step],
            recv_sem=spread_sems.at[1, step],
            device_id={"section": peer},
            device_id_type=MESH,
        )

    def pool_copy(s, step):
        return pltpu.make_async_remote_copy(
            src_ref=pool.at[s, me_resp],
            dst_ref=pool.at[s, me_resp],
            send_sem=pool_sems.at[0, s, step],
            recv_sem=pool_sems.at[1, s, step],
            device_id={"resp": lax.rem(me_resp + step, n_resp)},
            device_id_type=MESH,
        )

    def own_pool():
        return pltpu.make_async_copy(
            prompt_ref.at[:, own_lanes], pool.at[me, me_resp], local_sem.at[4]
        )

    def start_pool(s):
        step = lax.rem(me - s + sections, sections)

        @pl.when(step == 0)
        def _():
            own_pool().wait()

        @pl.when(step > 0)
        def _():
            spread_copy(step).wait()

        loop(1, n_resp, lambda d: pool_copy(s, d).start())

    def wait_pool(s):
        loop(1, n_resp, lambda d: pool_copy(s, d).wait())

    if direct:
        own_pool().start()
        loop(1, sections, lambda step: spread_copy(step).start())
    for copy in local_copies:
        copy.start()
    loop(1, sections, start_weights)
    if direct:
        start_pool(0)
    for copy in local_copies:
        copy.wait()

    def first_stats(block):
        wide = rows_in[0, :, lane_slice(block)].astype(F32)
        stat_acc[...] += wide * wide

    stat_acc[...] = jnp.zeros_like(stat_acc)
    loop(0, blocks, first_stats)
    loop(1, sections, wait_weights)

    t_row = lax.broadcasted_iota(jnp.int32, (length, LANES), 0)
    s_lane = lax.broadcasted_iota(jnp.int32, (length, LANES), 1)
    keep = s_lane <= prompt_len + t_row
    s_row = lax.broadcasted_iota(jnp.int32, (total, LANES), 0)
    t_lane = lax.broadcasted_iota(jnp.int32, (total, LANES), 1)
    keep_t = s_row <= prompt_len + t_lane

    def build(s, block):
        rows = pl.ds(pl.multiple_of(block * groups, groups), groups)
        both = taps_ref[s, rows, :]
        flipped, plain = both[:, :LANES], both[:, LANES:]
        for g in range(groups):
            base = pl.multiple_of((block * groups + g) * length, length)
            wide = jnp.broadcast_to(flipped[g : g + 1], (length, LANES))
            wide = pltpu.roll(wide, prompt_len, 1, stride=1, stride_axis=0)
            wide = jnp.where(keep, wide, 0.0)
            high = wide.astype(BF16)
            low = (wide - high.astype(F32)).astype(BF16)
            toep[s, pl.ds(base, length), :] = jnp.concatenate([high, high, low], axis=1)
            base = pl.multiple_of((block * groups + g) * total, total)
            wide = jnp.broadcast_to(plain[g : g + 1], (total, LANES))
            wide = pltpu.roll(wide, prompt_len, 1, stride=1, stride_axis=0)
            toep_t[s, pl.ds(base, total), :] = jnp.where(keep_t, wide, 0.0).astype(BF16)

    def choose(s, block):
        lanes = lane_slice(block)
        for m in range(micro):
            rows = slice(m * prompt_len, (m + 1) * prompt_len)
            if direct:
                picked = jnp.zeros((prompt_len, LANES), F32)
                for r in range(n_resp):
                    flag = jnp.full((prompt_len, LANES), owner_ref[m], jnp.int32) == r
                    picked = jnp.where(flag, pool[s, r, :, lanes].astype(F32), picked)
                chosen_rows[s, rows, lanes] = picked.astype(BF16)
            else:
                picked = prompt_ref[s, rows, lanes].astype(F32)
                chosen_rows[s, rows, lanes] = prompt_ref[s, rows, lanes]
            prompt_acc[rows, :] += picked * picked

    row_id = lax.broadcasted_iota(jnp.int32, (total, LANES), 0)
    wide_group = (
        lax.broadcasted_iota(jnp.int32, (1, micro * LANES), 1) % LANES
    ) // per_group
    tap_count = short_ref.shape[1]

    def pick(stacked, rows):
        out = stacked[0:rows]
        for g in range(1, groups):
            out = jnp.where(wide_group == g, stacked[g * rows : (g + 1) * rows], out)
        return out

    def joined_rows(s, m, lanes):
        rows_p = slice(m * prompt_len, (m + 1) * prompt_len)
        rows_c = slice(m * length, (m + 1) * length)
        joined = jnp.concatenate(
            [chosen_rows[s, rows_p, lanes].astype(F32), rows_in[s, rows_c, lanes].astype(F32)],
            axis=0,
        )
        factor = jnp.concatenate([fac_p[s, rows_p, :], fac_c[s, rows_c, :]], axis=0)
        return joined, factor

    def forward(s, carry):
        if direct:
            wait_pool(s)

            @pl.when(s + 1 < sections)
            def _():
                start_pool(s + 1)

        prompt_acc[...] = jnp.zeros_like(prompt_acc)
        loop(0, blocks, lambda block: choose(s, block))
        finish = start_stats(s, rows_to_line(stat_acc[...]), rows_to_line(prompt_acc[...]))
        loop(0, blocks, lambda block: build(s, block))
        sums = finish()
        fac_c[s] = lax.rsqrt(line_to_rows(sums[0]) * (1.0 / width) + 1e-06)
        fac_p[s] = lax.rsqrt(line_to_rows(sums[1]) * (1.0 / width) + 1e-06)
        stat_acc[...] = jnp.zeros_like(stat_acc)
        score_acc[...] = jnp.zeros_like(score_acc)

        def run(block, carry):
            lanes = lane_slice(block)
            wide = wide_slice(block)
            gain = gain_ref[s, :, lanes]
            short = short_ref[s, :, lanes]
            parts, lows, saved = [], [], []
            for m in range(micro):
                joined, factor = joined_rows(s, m, lanes)
                normed = joined * factor * gain
                shorter = normed * short[0:1]
                for j in range(1, tap_count):
                    moved = jnp.where(row_id >= j, pltpu.roll(normed, j, 0), 0.0)
                    shorter = shorter + moved * short[j : j + 1]
                high = shorter.astype(BF16)
                parts.append(high)
                lows.append((shorter - high.astype(F32)).astype(BF16))
                saved.append((joined[prompt_len:], normed[prompt_len:]))
            high = jnp.concatenate(parts, axis=1)
            short_out[s, :, wide] = high
            rhs = jnp.concatenate([high, jnp.concatenate(lows, axis=1), high], axis=0)
            base = pl.multiple_of(block * groups * length, groups * length)
            stacked = jnp.dot(
                toep[s, pl.ds(base, groups * length), :], rhs, preferred_element_type=F32
            )
            longer_all = pick(stacked, length)
            for m in range(micro):
                rows = slice(m * length, (m + 1) * length)
                longer = longer_all[:, m * LANES : (m + 1) * LANES]
                long_out[s, rows, lanes] = longer
                mixed = (saved[m][0] + saved[m][1] * longer).astype(BF16)
                rows_in[s + 1, rows, lanes] = mixed
                mixed = mixed.astype(F32)
                stat_acc[rows, :] += mixed * mixed
                score_acc[rows, :] += mixed * head_ref[0:1, head_slice(block)]
            return carry

        lax.fori_loop(0, blocks, run, 0)

        return carry

    lax.fori_loop(0, sections, forward, 0)

    live = []
    for m in range(micro):
        count = jnp.full((length, LANES), length_ref[m, 0], jnp.int32)
        live.append(jnp.where(t_row < count, 1.0, 0.0) / jnp.sqrt(count.astype(F32)))
    tile_rows = []
    for m in range(micro):
        rows = slice(m * length, (m + 1) * length)
        line = jnp.sum(score_acc[rows, :] * live[m], axis=0, keepdims=True)
        tile_rows.append(jnp.broadcast_to(jnp.sum(line, axis=1, keepdims=True), (1, LANES)))
    tile_rows.append(jnp.zeros((8 - micro, LANES), F32))
    score_tile = jnp.concatenate(tile_rows, axis=0)
    own_score = start_stats(sections, score_tile, score_tile)()[0]
    score_ref[...] = own_score
    resp_out[...] = own_score
    swap("resp", n_resp, me_resp, resp_out, resp_in, resp_sems)()
    winner, loser = ends_ref[0], ends_ref[1]

    def signs(r):
        return jnp.where(winner == r, 1.0, 0.0) - jnp.where(loser == r, 1.0, 0.0)

    margin = lax.fori_loop(
        0, n_resp, lambda r, acc: acc + resp_in[r] * signs(r), jnp.zeros((8, LANES), F32)
    )
    weight = 1.0 / (1.0 + jnp.exp(margin))
    slopes = -jnp.sum(signs(me_resp) * weight, axis=1, keepdims=True)

    def seed(block, carry):
        lanes = lane_slice(block)
        for m in range(micro):
            rows = slice(m * length, (m + 1) * length)
            upstream[rows, lanes] = live[m] * slopes[m : m + 1] * head_ref[0:1, head_slice(block)]
        return carry

    lax.fori_loop(0, blocks, seed, 0)

    keep_pair = total - 1 - s_lane <= prompt_len + t_row
    reverse = (
        lax.broadcasted_iota(jnp.int32, (total, total), 0)
        + lax.broadcasted_iota(jnp.int32, (total, total), 1)
        == total - 1
    )
    reverse = jnp.where(reverse, 1.0, 0.0).astype(BF16)

    share = 2 * blocks // n_resp

    def part_slice(r):
        return pl.ds(r * share, share)

    def part_steps(s, action):
        def each(step):
            peer = lax.rem(me_resp + step, n_resp)
            action(
                pltpu.make_async_remote_copy(
                    src_ref=tiles_own.at[s, part_slice(peer)],
                    dst_ref=tiles_in.at[s, me_resp],
                    send_sem=part_sems.at[0, s, step],
                    recv_sem=part_sems.at[1, s, step],
                    device_id={"resp": peer},
                    device_id_type=MESH,
                )
            )

        loop(1, n_resp, each)

    def tile_copy(s, step, k, r):
        return pltpu.make_async_remote_copy(
            src_ref=tiles_sum.at[s],
            dst_ref=tiles_all.at[k, r],
            send_sem=tile_send.at[s, step],
            recv_sem=tile_recv.at[k, r],
            device_id={"section": s, "resp": lax.rem(me_resp + step, n_resp)},
            device_id_type=MESH,
        )

    def tile_steps(s, action):
        def each(step):
            @pl.when(jnp.logical_not((s == me) & (step == 0)))
            def _():
                action(tile_copy(s, step, me, me_resp))

        loop(0, n_resp, each)

    def backward(step, carry):
        s = sections - 1 - step
        stat_acc[...] = jnp.zeros_like(stat_acc)

        def run(block, carry):
            lanes = lane_slice(block)
            wide = wide_slice(block)
            gain = gain_ref[s, :, lanes]
            short = short_ref[s, :, lanes]
            parts, saved = [], []
            for m in range(micro):
                rows = slice(m * length, (m + 1) * length)
                joined, factor = joined_rows(s, m, lanes)
                scaled = joined * factor
                normed = scaled * gain
                above = upstream[rows, lanes]
                parts.append((above * normed[prompt_len:]).astype(BF16))
                saved.append((joined[prompt_len:], scaled, normed, above))
            d_long = jnp.concatenate(parts, axis=1)
            base = pl.multiple_of(block * groups * total, groups * total)
            stacked = jnp.dot(
                toep_t[s, pl.ds(base, groups * total), :][:, :length],
                d_long,
                preferred_element_type=F32,
            )
            d_short_all = pick(stacked, total)
            turned = jnp.dot(reverse, short_out[s, :, wide], preferred_element_type=F32)
            d_wide = d_long.astype(F32)
            masked = jnp.concatenate(
                [
                    jnp.where(wide_group == g, d_wide, 0.0).astype(BF16)
                    for g in range(groups)
                ],
                axis=0,
            )
            pairs = lax.dot_general(
                masked,
                turned.astype(BF16),
                (((1,), (1,)), ((), ())),
                preferred_element_type=F32,
            )
            lines = []
            for g in range(groups):
                one = jnp.where(keep_pair, pairs[g * length : (g + 1) * length], 0.0)
                one = pltpu.roll(one, LANES + 1 - length, 1, stride=1, stride_axis=0)
                lines.append(jnp.sum(one, axis=0, keepdims=True))
            tiles_own[s, 2 * block + 1] = jnp.concatenate(lines, axis=0)
            grads = [jnp.zeros((1, LANES), F32)] * (tap_count + 1)
            for m in range(micro):
                rows = slice(m * length, (m + 1) * length)
                joined_c, scaled, normed, above = saved[m]
                d_short = d_short_all[:, m * LANES : (m + 1) * LANES]
                d_normed = d_short * short[0:1]
                grads[1] = grads[1] + jnp.sum(d_short * normed, axis=0, keepdims=True)
                for j in range(1, tap_count):
                    moved = jnp.where(
                        row_id < total - j, pltpu.roll(d_short, total - j, 0), 0.0
                    )
                    d_normed = d_normed + moved * short[j : j + 1]
                    grads[1 + j] = grads[1 + j] + jnp.sum(
                        moved * normed, axis=0, keepdims=True
                    )
                direct = above * long_out[s, rows, lanes]
                d_normed = jnp.concatenate(
                    [d_normed[:prompt_len], d_normed[prompt_len:] + direct], axis=0
                )
                grads[0] = grads[0] + jnp.sum(d_normed * scaled, axis=0, keepdims=True)
                inner = d_normed[prompt_len:] * gain
                partial[rows, lanes] = inner
                stat_acc[rows, :] += inner * joined_c
            tiles_own[s, 2 * block] = jnp.concatenate(grads, axis=0)
            return carry

        lax.fori_loop(0, blocks, run, 0)

        if direct:
            part_steps(s, lambda copy: copy.start())
            parts_in = tiles_in.at[s]
            parts_in[me_resp] = tiles_own[s, part_slice(me_resp)]

        @pl.when(s > 0)
        def _():
            line = rows_to_line(stat_acc[...])
            all_sums = start_stats(sections + 1 + step, line, line)()[0]
            factor = fac_c[s]
            pull = line_to_rows(all_sums) * (1.0 / width) * factor * factor * factor

            def finish(block, carry):
                lanes = lane_slice(block)
                grad = (
                    upstream[:, lanes]
                    + factor * partial[:, lanes]
                    - rows_in[s, :, lanes].astype(F32) * pull
                )
                upstream[:, lanes] = grad.astype(BF16).astype(F32)
                return carry

            lax.fori_loop(0, blocks, finish, 0)

        if direct:
            part_steps(s, lambda copy: copy.wait())
            tiles_sum[s] = jnp.sum(tiles_in[s], axis=0)

            @pl.when(s == me)
            def _():
                tiles_all[me, me_resp] = tiles_sum[s]

            tile_steps(s, lambda copy: copy.start())

        return carry

    lax.fori_loop(0, sections, backward, 0)

    if direct:
        loop(0, sections, lambda s: tile_steps(s, lambda copy: copy.wait_send()))

        def arrive(step):
            k, r = step // n_resp, step % n_resp

            @pl.when(jnp.logical_not((k == me) & (r == me_resp)))
            def _():
                tile_copy(0, 0, k, r).wait_recv()

        loop(0, sections * n_resp, arrive)
        gain_out, taps_short_out, taps_long_out = outs
        per_line = LANES // groups
        for line in range(sections * blocks // per_line):
            lines = []
            for place in range(per_line):
                block = line * per_line + place
                lanes = slice(block * LANES, (block + 1) * LANES)
                owner, local = divmod(2 * block, 2 * blocks)
                first, second = (divmod(local + kind, share) for kind in range(2))
                tile = tiles_all[owner, first[0], first[1]]
                gain_out[:, lanes] = tile[0:1]
                taps_short_out[:, lanes] = tile[1:]
                lines.append(tiles_all[owner, second[0], second[1]])
            lanes = slice(line * LANES, (line + 1) * LANES)
            taps_long_out[:, lanes] = jnp.transpose(jnp.concatenate(lines, axis=0))
    else:
        outs[0][...] = tiles_own[...]


def run_kernel(dims, direct, *arrays):
    sections, n_resp, micro, length, prompt_len, chans, per_group, width = dims
    rows = micro * length
    total = prompt_len + length
    group_total = chans // per_group
    tile = (8, LANES)
    tiles = 2 * chans // LANES
    share = tiles // n_resp if direct else 1
    ranks = n_resp if direct else 1
    vmem = pl.BlockSpec(memory_space=pltpu.VMEM)
    hbm = pl.BlockSpec(memory_space=pl.ANY)
    smem = pl.BlockSpec(memory_space=pltpu.SMEM)
    tap_count = arrays[3].shape[0]
    if direct:
        out_shapes = [(1, width), (tap_count, width), (LANES, width // per_group)]
    else:
        out_shapes = [(sections, tiles) + tile]
    return pl.pallas_call(
        functools.partial(kernel, dims, direct),
        out_shape=(
            jax.ShapeDtypeStruct(tile, F32),
            *(jax.ShapeDtypeStruct(shape, F32) for shape in out_shapes),
        ),
        in_specs=[hbm, hbm if direct else vmem, hbm, hbm, hbm, smem, vmem, vmem, smem],
        out_specs=(vmem,) * (1 + len(out_shapes)),
        scratch_shapes=[
            pltpu.VMEM((sections, group_total * length, 3 * LANES), BF16),
            pltpu.VMEM((sections, group_total * total, LANES), BF16),
            pltpu.VMEM((sections, ranks, prompt_len, chans), BF16),
            pltpu.VMEM((sections, micro * prompt_len, chans), BF16),
            pltpu.VMEM((sections, 1, chans), F32),
            pltpu.VMEM((sections, tap_count, chans), F32),
            pltpu.VMEM((sections, group_total, 2 * LANES), F32),
            pltpu.VMEM((sections + 1, rows, chans), BF16),
            pltpu.VMEM((sections, total, micro * chans), BF16),
            pltpu.VMEM((sections, rows, chans), F32),
            pltpu.VMEM((sections, micro * prompt_len, LANES), F32),
            pltpu.VMEM((sections, rows, LANES), F32),
            pltpu.VMEM((rows, chans), F32),
            pltpu.VMEM((rows, chans), F32),
            pltpu.VMEM((rows, LANES), F32),
            pltpu.VMEM((rows, LANES), F32),
            pltpu.VMEM((micro * prompt_len, LANES), F32),
            pltpu.VMEM((2 * sections, 2) + tile, F32),
            pltpu.VMEM((2 * sections, sections, 2) + tile, F32),
            pltpu.VMEM(tile, F32),
            pltpu.VMEM((n_resp,) + tile, F32),
            pltpu.VMEM((sections, tiles) + tile, F32),
            pltpu.VMEM((sections, ranks, share) + tile, F32),
            pltpu.VMEM((sections, share) + tile, F32),
            pltpu.VMEM((sections, ranks, share) + tile, F32),
            pltpu.SemaphoreType.DMA((5,)),
            pltpu.SemaphoreType.DMA((2, 3, sections)),
            pltpu.SemaphoreType.DMA((2, sections)),
            pltpu.SemaphoreType.DMA((2, sections, ranks)),
            pltpu.SemaphoreType.DMA((2 * sections, 2, sections)),
            pltpu.SemaphoreType.DMA((2, n_resp)),
            pltpu.SemaphoreType.DMA((2, sections, ranks)),
            pltpu.SemaphoreType.DMA((sections, ranks)),
            pltpu.SemaphoreType.DMA((sections, ranks)),
        ],
        compiler_params=pltpu.CompilerParams(
            has_side_effects=True, vmem_limit_bytes=56 * 1024 * 1024
        ),
    )(*arrays)


def body(
    completion_rows,
    prompt_pool,
    norm_gain,
    short_taps,
    long_taps,
    score_head,
    live_lengths,
    prompt_owner,
    pair_index,
):
    sections = lax.axis_size("section")
    n_resp = lax.axis_size("resp")
    me_resp = lax.axis_index("resp")
    micro, _, length, width = completion_rows.shape
    prompt_len = prompt_pool.shape[2]
    chans = width // sections
    tap_len, group_all = long_taps.shape[1:]
    per_group = width // group_all
    dims = (sections, n_resp, micro, length, prompt_len, chans, per_group, width)

    tiles = 2 * chans // LANES
    direct = n_resp <= 8 and tiles % n_resp == 0

    taps = long_taps[0].T
    flipped = jnp.concatenate([taps[:, :1], taps[:, :0:-1]], axis=1)
    taps = jnp.concatenate([flipped, taps], axis=1)
    prompts = prompt_pool[0, 0]
    if not direct:
        split = prompts.reshape(prompt_len, sections, chans).transpose(1, 0, 2)
        split = lax.all_to_all(split, "section", 0, 0, tiled=True)
        here = (prompt_owner == me_resp)[None, :, None, None]
        split = lax.psum(jnp.where(here, split[:, None], jnp.zeros((), BF16)), "resp")
        prompts = split.reshape(sections, micro * prompt_len, chans)
    rows = completion_rows.reshape(micro * length, width)
    head = score_head[None]

    ends = jnp.pad(
        pair_index.transpose(2, 0, 1),
        ((0, 0), (0, 8 - micro), (0, LANES - pair_index.shape[1])),
        constant_values=-1,
    )
    scores, *grads = run_kernel(
        dims,
        direct,
        rows,
        prompts,
        norm_gain,
        short_taps[0],
        taps,
        prompt_owner,
        head,
        ends,
        live_lengths,
    )
    scores = scores[:micro, :1].astype(BF16)
    if direct:
        return (scores, grads[0], grads[1][None], grads[2][None])
    grads = lax.psum(grads[0], "resp")
    grads = lax.all_to_all(grads, "section", 0, 0, tiled=True)
    grads = grads.reshape(sections * tiles // 2, 2, 8, LANES)
    gs_grad = grads[:, 0].transpose(1, 0, 2).reshape(8, width)
    taps_grad = grads[:, 1].reshape(group_all, tap_len).T
    return (
        scores,
        gs_grad[:1],
        gs_grad[None, 1:],
        taps_grad[None],
    )


SIDE = 8


def wide_kernel(
    dims,
    comp_hbm,
    prompt_hbm,
    gain_hbm,
    short_hbm,
    taps_hbm,
    head_hbm,
    owner_ref,
    pair_ref,
    length_ref,
    score_ref,
    gain_out,
    taps_short_out,
    taps_long_out,
    comp_full,
    prompt_full,
    taps_full,
    head_own,
    comp_in,
    pool,
    gain_in,
    short_in,
    taps_src,
    taps_in,
    order_c,
    order_p,
    lined,
    first_out,
    first_in,
    stat_out,
    stat_in,
    rows_in,
    prompt_rows,
    long_out,
    short_out,
    toep,
    toep_p,
    toep_t,
    params,
    heads,
    fac_c,
    fac_p,
    normed_buf,
    d_short_buf,
    upstream,
    inner_buf,
    d_long_buf,
    acc_ref,
    scales,
    tiles_own,
    tiles_all,
    local_sem,
    comp_send,
    comp_recv,
    weight_send,
    weight_recv,
    pool_send,
    pool_recv,
    first_send,
    first_recv,
    stat_send,
    stat_recv,
    tile_send,
    tile_recv,
):
    sections, n_resp, micro, length, chans, per_group, width = dims
    comps = micro * n_resp
    ranks = sections * n_resp
    blocks = chans // LANES
    per_block = LANES // per_group
    groups = blocks * per_block
    tap_count = short_in.shape[1]
    total = 2 * length
    me = lax.axis_index("section")
    me_resp = lax.axis_index("resp")
    rank = me_resp * sections + me

    def loop(low, high, step_of):
        def run(index, carry):
            step_of(index)
            return carry

        lax.fori_loop(low, high, run, 0)

    def lockstep(low, high, count, step_of):
        def run(index, carry):
            live = [step_of(index * count + k, k) for k in range(count)]
            while live:
                live = [step for step in live if next(step, 0) is None]
            return carry

        lax.fori_loop(low // count, high // count, run, 0)

    def add_up(values):
        while len(values) > 1:
            values = [a + b for a, b in zip(values[::2], values[1::2])] + (
                values[-1:] if len(values) % 2 else []
            )
        return values[0]

    def place(peer):
        return {"section": lax.rem(peer, sections), "resp": peer // sections}

    def lanes_of(peer):
        return pl.ds(pl.multiple_of(peer * chans, chans), chans)

    def groups_of(peer):
        return pl.ds(pl.multiple_of(peer * groups, groups), groups)

    def remote(src, dst, send_sem, recv_sem, device):
        return pltpu.make_async_remote_copy(
            src_ref=src,
            dst_ref=dst,
            send_sem=send_sem,
            recv_sem=recv_sem,
            device_id=device,
            device_id_type=MESH,
        )

    load_comp = pltpu.make_async_copy(comp_hbm, comp_full, local_sem.at[0])
    load_prompt = pltpu.make_async_copy(prompt_hbm, prompt_full, local_sem.at[1])
    load_taps = pltpu.make_async_copy(taps_hbm, taps_full, local_sem.at[2])
    load_head = pltpu.make_async_copy(head_hbm.at[:, lanes_of(rank)], head_own, local_sem.at[3])
    own_comp = pltpu.make_async_copy(
        comp_hbm.at[:, lanes_of(rank)], comp_in.at[me_resp], local_sem.at[4]
    )
    own_pool = pltpu.make_async_copy(
        prompt_hbm.at[:, lanes_of(rank)], pool.at[me, me_resp], local_sem.at[5]
    )
    own_gain = pltpu.make_async_copy(
        gain_hbm.at[:, lanes_of(rank)], gain_in.at[me], local_sem.at[6]
    )
    own_short = pltpu.make_async_copy(
        short_hbm.at[:, :, lanes_of(rank)], short_in.at[me], local_sem.at[7]
    )

    def comp_copy(step):
        peer_resp = lax.rem(me_resp + step, n_resp)
        return remote(
            comp_hbm.at[:, lanes_of(peer_resp * sections + me)],
            comp_in.at[me_resp],
            comp_send.at[step],
            comp_recv.at[me_resp],
            {"resp": peer_resp},
        )

    def comp_wait(step):
        source = lax.rem(me_resp + step, n_resp)
        remote(
            comp_hbm.at[:, lanes_of(rank)],
            comp_in.at[source],
            comp_send.at[step],
            comp_recv.at[source],
            {"resp": source},
        ).wait_recv()

    def weight_parts(peer_rank, source):
        return (
            (gain_hbm.at[:, lanes_of(peer_rank)], gain_in.at[source]),
            (short_hbm.at[:, :, lanes_of(peer_rank)], short_in.at[source]),
            (taps_src.at[groups_of(peer_rank), :], taps_in.at[source]),
        )

    def weight_copy(kind, step):
        peer = lax.rem(me + step, sections)
        src, dst = weight_parts(me_resp * sections + peer, me)[kind]
        return remote(
            src, dst, weight_send.at[kind, step], weight_recv.at[kind, me], {"section": peer}
        )

    def weight_wait(kind, step):
        source = lax.rem(me + step, sections)
        src, dst = weight_parts(rank, source)[kind]
        remote(
            src,
            dst,
            weight_send.at[kind, step],
            weight_recv.at[kind, source],
            {"section": source},
        ).wait_recv()

    def pool_copy(step):
        peer = lax.rem(rank + step, ranks)
        return remote(
            prompt_hbm.at[:, lanes_of(peer)],
            pool.at[me, me_resp],
            pool_send.at[step],
            pool_recv.at[rank],
            place(peer),
        )

    def pool_wait(s):
        def each(r):
            source = r * sections + s

            @pl.when(source != rank)
            def _():
                remote(
                    prompt_hbm.at[:, lanes_of(rank)],
                    pool.at[s, r],
                    pool_send.at[0],
                    pool_recv.at[source],
                    place(source),
                ).wait_recv()

            @pl.when(source == rank)
            def _():
                own_pool.wait()

        loop(0, n_resp, each)

    def first_copy(step):
        peer = lax.rem(rank + step, ranks)
        return remote(
            first_out, first_in.at[rank], first_send.at[step], first_recv.at[rank], place(peer)
        )

    def first_wait(step):
        source = lax.rem(rank + step, ranks)
        remote(
            first_out,
            first_in.at[source],
            first_send.at[step],
            first_recv.at[source],
            place(source),
        ).wait_recv()

    peers = []
    for j in range(1, n_resp):
        hop = jnp.where(me_resp * 2 < n_resp, n_resp - j, j)
        peer_resp = lax.rem(me_resp + hop, n_resp)
        peers += [(lax.rem(me + k, sections), peer_resp) for k in range(sections)]
    peers += [(lax.rem(me + k, sections), me_resp) for k in range(1, sections)]

    def stat_start(slot, tile):
        stat_out[slot] = tile
        for peer, peer_resp in peers:
            remote(
                stat_out.at[slot],
                stat_in.at[slot, rank],
                stat_send.at[slot],
                stat_recv.at[slot],
                {"section": peer, "resp": peer_resp},
            ).start()
        stat_in[slot, rank] = tile

    def stat_wait(slot, sem):
        bulk = stat_in.at[slot, pl.ds(0, ranks - 1)]
        pltpu.make_async_copy(bulk, bulk, sem.at[slot]).wait()

    def stat_finish(slot):
        stat_wait(slot, stat_recv)
        return jnp.sum(stat_in[slot], axis=0)

    def tile_copy(s, step):
        return remote(
            tiles_own.at[s],
            tiles_all.at[rank],
            tile_send.at[s, step],
            tile_recv.at[rank],
            {"section": s, "resp": lax.rem(me_resp + step, n_resp)},
        )

    def tile_steps(s, action):
        def each(step):
            @pl.when(jnp.logical_not((s == me) & (step == 0)))
            def _():
                action(tile_copy(s, step))

        loop(0, n_resp, each)

    for copy in (load_taps, load_comp, load_prompt, load_head):
        copy.start()
    for copy in (own_comp, own_pool, own_gain, own_short):
        copy.start()
    barrier = pltpu.get_barrier_semaphore()
    loop(
        1,
        ranks,
        lambda step: pl.semaphore_signal(
            barrier,
            inc=1,
            device_id=place(lax.rem(rank + step, ranks)),
            device_id_type=MESH,
        ),
    )

    tile_row = lax.broadcasted_iota(jnp.int32, (LANES, LANES), 0)
    tile_lane = lax.broadcasted_iota(jnp.int32, (LANES, LANES), 1)
    row_target = (tile_row // per_group) * LANES + tile_row % per_group
    prompt_key = (tile_lane // (n_resp * per_group)) * (n_resp * per_group) + (
        tile_lane % per_group
    )

    def fill_order(c):
        rows = pl.ds(pl.multiple_of(c * LANES, LANES), LANES)
        for n in range(per_block):
            hit = row_target + c * per_group == tile_lane + n * LANES
            order_c[rows, n * LANES : (n + 1) * LANES] = jnp.where(hit, 1.0, 0.0).astype(BF16)

    loop(0, comps, fill_order)
    for m in range(micro):
        for n in range(per_block):
            hit = row_target + m * n_resp * per_group == prompt_key + n * LANES
            order_p[m * LANES : (m + 1) * LANES, n * LANES : (n + 1) * LANES] = jnp.where(
                hit, 1.0, 0.0
            ).astype(BF16)
    pad = 8
    for g in range(groups):
        normed_buf[g, :pad] = jnp.zeros((pad, LANES), F32)
        for s in range(sections):
            d_short_buf[s, g, total:] = jnp.zeros((pad, LANES), F32)

    load_taps.wait()
    upright = jnp.transpose(taps_full[...])
    mirror = jnp.where(lax.rem(tile_row + tile_lane, LANES) == 0, 1.0, 0.0)
    taps_src[:, :LANES] = jnp.dot(
        upright, mirror, preferred_element_type=F32, precision=lax.Precision.HIGHEST
    )
    taps_src[:, LANES:] = upright

    ones = jnp.ones((16, 2 * LANES), BF16)

    def split(values):
        high = values.astype(BF16)
        return high, (values - high.astype(F32)).astype(BF16)

    def lane_sums(acc, weights, below=None):
        if acc.shape[0] < LANES:
            rest = [] if below is None else [below]
            rows = LANES - acc.shape[0] - sum(block.shape[0] for block in rest)
            acc = jnp.concatenate([acc] + rest + [jnp.zeros((rows, LANES), F32)], axis=0)
        both = jnp.concatenate(split(acc), axis=1)
        return lax.dot_general(
            weights, both, (((1,), (1,)), ((), ())), preferred_element_type=F32
        )[:8]

    def square_rows(ref):
        def step(block, acc):
            values = ref[:, pl.ds(pl.multiple_of(block * LANES, LANES), LANES)].astype(F32)
            return acc + values * values

        return lax.fori_loop(
            0, width // LANES, step, jnp.zeros((ref.shape[0], LANES), F32), unroll=2
        )

    load_comp.wait()
    comp_line = lane_sums(square_rows(comp_full), ones)
    load_prompt.wait()
    prompt_line = lane_sums(square_rows(prompt_full), ones)
    eight_row = lax.broadcasted_iota(jnp.int32, (8, LANES), 0)
    eight_lane = lax.broadcasted_iota(jnp.int32, (8, LANES), 1)
    message = jnp.where(eight_row == 0, comp_line, prompt_line)
    for m in range(micro):
        count = jnp.full((8, LANES), length_ref[0, m], jnp.int32).astype(F32)
        message = jnp.where(eight_row == 2 + m, count, message)
    first_out[...] = message

    pl.semaphore_wait(barrier, ranks - 1)
    loop(1, n_resp, lambda step: comp_copy(step).start())
    loop(1, sections, lambda step: weight_copy(2, step).start())

    def start_pool(s):
        @pl.when(me == s)
        def _():
            loop(1, ranks, lambda step: pool_copy(step).start())

    loop(1, ranks, lambda step: first_copy(step).start())
    start_pool(0)

    def start_vectors(step):
        weight_copy(0, step).start()
        weight_copy(1, step).start()

    loop(1, sections, start_vectors)
    first_in[rank] = message
    taps_in[me] = taps_src[groups_of(rank), :]

    own_gain.wait()
    own_short.wait()
    load_head.wait()

    def weights_arrive(step):
        for kind in range(3):
            weight_wait(kind, step)

    loop(1, sections, weights_arrive)

    def tile_lanes(values, n):
        out = pltpu.roll(values, (LANES - n * per_group) % LANES, 1)
        out = jnp.where(eight_lane < per_group, out, 0.0)
        span = per_group
        while span < LANES:
            out = out + pltpu.roll(out, span, 1)
            span *= 2
        return out

    t_row = lax.broadcasted_iota(jnp.int32, (length, LANES), 0)
    s_lane = lax.broadcasted_iota(jnp.int32, (length, LANES), 1)
    keep = s_lane <= length + t_row
    keep_t = tile_row <= length + tile_lane

    def spread_params(s):
        for b in range(blocks):
            lanes = slice(b * LANES, (b + 1) * LANES)
            rows = jnp.concatenate(
                [gain_in[s, :, lanes]] + [short_in[s, j, :, lanes] for j in range(tap_count)],
                axis=0,
            )
            for n in range(per_block):
                params[s, b * per_block + n] = tile_lanes(rows, n)

    loop(0, sections, spread_params)
    for b in range(blocks):
        rows = jnp.broadcast_to(head_own[:, b * LANES : (b + 1) * LANES], (8, LANES))
        for n in range(per_block):
            heads[b * per_block + n] = tile_lanes(rows, n)

    def build(index, k):
        s, g = index // groups, lax.rem(index, groups)
        line = taps_in[s, pl.ds(g, 1), :]
        wide = jnp.broadcast_to(line[:, :LANES], (length, LANES))
        wide = pltpu.roll(wide, length, 1, stride=1, stride_axis=0)
        wide_t = jnp.broadcast_to(line[:, LANES:], (total, LANES))
        wide_t = pltpu.roll(wide_t, length, 1, stride=1, stride_axis=0)
        yield
        wide = jnp.where(keep, wide, 0.0)
        high = wide.astype(BF16).astype(F32)
        low = wide - high
        low_turned = pltpu.roll(low, length, 1)
        high_turned = pltpu.roll(high, length, 1)
        toep_t[s, g] = jnp.where(keep_t, wide_t, 0.0).astype(BF16)
        yield
        first = s_lane < length
        toep_p[s, g] = jnp.where(first, high, low_turned).astype(BF16)
        toep[s, g] = jnp.where(first, high_turned, low).astype(BF16)

    lockstep(0, sections * groups, 4, build)

    def spread_rows(lines):
        tall = jnp.concatenate(
            [jnp.broadcast_to(lines[c : c + 1], (per_group, LANES)) for c in range(comps)],
            axis=0,
        )
        return jnp.transpose(tall)[:length]

    def to_factor(sums):
        return lax.rsqrt(sums * (1.0 / width) + 1e-06)

    loop(1, ranks, first_wait)
    own_lines = jnp.concatenate(
        [first_in[r * sections + me, 0:1] for r in range(n_resp)], axis=0
    )
    own_lines = jnp.concatenate(
        [
            own_lines if m == 0 else pltpu.roll(own_lines, LANES - m * length, 1)
            for m in range(micro)
        ],
        axis=0,
    )
    fac_c[0] = spread_rows(to_factor(own_lines))

    def prompt_factor(s):
        lines = []
        for m in range(micro):
            owner = jnp.full((8, LANES), owner_ref[m], jnp.int32)
            line = jnp.zeros((8, LANES), F32)
            for r in range(n_resp):
                line = jnp.where(owner == r, first_in[r * sections + s], line)
            lines += [line[1:2]] * n_resp
        fac_p[s] = spread_rows(to_factor(jnp.concatenate(lines, axis=0)))

    loop(0, sections, prompt_factor)

    def conv_short(ref, g, start, taps):
        out = ref[g, pl.ds(start, length)] * taps[1:2]
        for j in range(1, tap_count):
            out = out + ref[g, pl.ds(start - j, length)] * taps[1 + j : 2 + j]
        return out

    def conv_long(matrix, high, low):
        left = jnp.concatenate([matrix, matrix], axis=1)
        right = jnp.concatenate([high, high, low, low], axis=0)
        return jnp.dot(left, right, preferred_element_type=F32)

    def prepare(s):
        pool_wait(s)

        @pl.when(s == 0)
        def _():
            start_pool(1)

        sides = []
        for b in range(blocks):
            lanes = slice(b * LANES, (b + 1) * LANES)
            row = []
            for m in range(micro):
                owner = jnp.full((length, LANES), owner_ref[m], jnp.int32)
                picked = pool[s, 0, :, lanes].astype(F32)
                for r in range(1, n_resp):
                    picked = jnp.where(owner == r, pool[s, r, :, lanes].astype(F32), picked)
                row.append(picked.astype(BF16))
            sides.append(jnp.concatenate(row, axis=1))
        side = jnp.concatenate(sides, axis=0)
        step = 2 * LANES
        for n in range(per_block // 2):
            part = jnp.dot(
                side, order_p[:, n * step : (n + 1) * step], preferred_element_type=F32
            ).astype(BF16)
            for b in range(blocks):
                for k in range(2):
                    prompt_rows[s, b * per_block + 2 * n + k] = part[
                        b * length : (b + 1) * length, k * LANES : (k + 1) * LANES
                    ]
        factor = fac_p[s]

        def each(g, k):
            taps = params[s, g]
            normed = prompt_rows[s, g].astype(F32) * factor * taps[0:1]
            normed_buf[g, pl.ds(pad, length)] = normed
            yield
            shorter = conv_short(normed_buf, g, pad, taps)
            high, low = split(shorter)
            short_out[s, g, :length] = high
            yield
            longer = conv_long(toep_p[s, g], high, low)
            yield
            long_out[s, g] = longer

        lockstep(0, groups, SIDE, each)

    loop(1, n_resp, comp_wait)
    loop(2, sections, start_pool)
    own_comp.wait()
    for b in range(blocks):
        lanes = slice(b * LANES, (b + 1) * LANES)
        for m in range(micro):
            for r in range(n_resp):
                c = m * n_resp + r
                lined[b * length : (b + 1) * length, c * LANES : (c + 1) * LANES] = comp_in[
                    r, m * length : (m + 1) * length, lanes
                ]
    for n in range(per_block // 2):
        step = 2 * LANES
        part = jnp.dot(
            lined[...], order_c[:, n * step : (n + 1) * step], preferred_element_type=F32
        ).astype(BF16)
        for b in range(blocks):
            for k in range(2):
                rows_in[0, b * per_block + 2 * n + k] = part[
                    b * length : (b + 1) * length, k * LANES : (k + 1) * LANES
                ]
    prepare(0)

    fold_row = lax.broadcasted_iota(jnp.int32, (16, 2 * LANES), 0)
    fold_lane = lax.broadcasted_iota(jnp.int32, (16, 2 * LANES), 1)
    fold = jnp.where((fold_lane % LANES) // per_group == fold_row, 1.0, 0.0).astype(BF16)

    def forward(s, last):
        acc_ref[...] = jnp.zeros_like(acc_ref)
        factor = fac_c[s]

        sums = []

        def each(g, k):
            taps = params[s, g]
            rows = rows_in[s, g].astype(F32)
            normed = rows * factor * taps[0:1]
            normed_buf[g, pl.ds(pad + length, length)] = normed
            yield
            shorter = conv_short(normed_buf, g, pad + length, taps)
            high, low = split(shorter)
            short_out[s, g, length:] = high
            yield
            longer = conv_long(toep[s, g], high, low)
            yield
            longer = long_out[s, g] + longer
            normed = normed_buf[g, pl.ds(pad + length, length)]
            mixed = (rows_in[s, g].astype(F32) + normed * longer).astype(BF16)
            sums.append((longer, mixed))
            yield
            longer, mixed = sums[k]
            long_out[s, g] = longer
            if not last:
                rows_in[s + 1, g] = mixed
            mixed = mixed.astype(F32)
            sums[k] = mixed * (heads[g, 0:1] if last else mixed)
            yield
            if k == SIDE - 1:
                acc_ref[...] += add_up(sums)
                sums.clear()

        lockstep(0, groups, SIDE, each)

    def forward_step(s):
        forward(s, False)
        stat_start(s, lane_sums(acc_ref[...], fold))
        prepare(s + 1)
        fac_c[s + 1] = spread_rows(to_factor(stat_finish(s)))

    loop(0, sections - 1, forward_step)
    forward(sections - 1, True)

    comp_lane = eight_lane // per_group
    counts = jnp.zeros((8, LANES), F32)
    for m in range(micro):
        for r in range(n_resp):
            row = first_in[r * sections + me, 2 + m : 3 + m]
            counts = jnp.where(comp_lane == m * n_resp + r, row, counts)
    alive = t_row.astype(F32) < counts[0:1]
    live = jnp.where(alive, 1.0, 0.0) / jnp.sqrt(counts[0:1])
    score_line = jnp.sum(acc_ref[...] * live, axis=0, keepdims=True)
    score_line = jnp.where(eight_row == 0, score_line, 0.0)

    def seed(g, k):
        upstream[sections - 1, g] = live * heads[g, 0:1]
        yield

    lockstep(0, groups, SIDE, seed)

    def backward(s, last):
        acc_ref[...] = jnp.zeros_like(acc_ref)
        factor = fac_c[s]

        sums = []

        def each(g, k):
            taps = params[s, g]
            rows = rows_in[s, g].astype(F32)
            d_long = (upstream[s, g] * (rows * factor * taps[0:1])).astype(BF16)
            yield
            d_long_buf[s, g] = d_long
            d_short = jnp.dot(
                toep_t[s, g][:, :length], d_long, preferred_element_type=F32
            )
            yield
            d_short_buf[s, g, pl.ds(0, total)] = d_short
            if last:
                return
            yield
            d_normed = upstream[s, g] * long_out[s, g]
            for j in range(tap_count):
                d_normed = d_normed + d_short_buf[s, g, pl.ds(length + j, length)] * taps[1 + j : 2 + j]
            inner = d_normed * taps[0:1]
            sums.append(inner)
            yield
            inner_buf[g] = sums[k]
            sums[k] = sums[k] * rows_in[s, g].astype(F32)
            yield
            if k == SIDE - 1:
                acc_ref[...] += add_up(sums)
                sums.clear()

        lockstep(0, groups, SIDE, each)

    keep_pair = total - 1 - s_lane <= length + t_row
    reverse = jnp.where(tile_row + tile_lane == total - 1, 1.0, 0.0).astype(BF16)

    def gradients(s):
        factor_c = fac_c[s]
        factor_p = fac_p[s]
        scale = scales[s, 0:1]
        tops, longs = [], []

        def each(g, k):
            turned = jnp.dot(reverse, short_out[s, g], preferred_element_type=F32)
            yield
            pairs = lax.dot_general(
                (d_long_buf[s, g].astype(F32) * scale).astype(BF16),
                turned.astype(BF16),
                (((1,), (1,)), ((), ())),
                preferred_element_type=F32,
            )
            yield
            taps = params[s, g]
            scaled_p = prompt_rows[s, g].astype(F32) * factor_p
            scaled_c = rows_in[s, g].astype(F32) * factor_c
            lines = [
                jnp.sum(upstream[s, g] * long_out[s, g] * scaled_c, axis=0, keepdims=True)
            ]
            for j in range(tap_count):
                part = (
                    d_short_buf[s, g, pl.ds(j, length)] * scaled_p
                    + d_short_buf[s, g, pl.ds(length + j, length)] * scaled_c
                )
                lines.append(jnp.sum(part, axis=0, keepdims=True))
            tile = jnp.concatenate(lines, axis=0) * scale
            yield
            pairs = jnp.where(keep_pair, pairs, 0.0)
            pairs = pltpu.roll(pairs, LANES + 1 - length, 1, stride=1, stride_axis=0)
            yield
            span = per_group
            while span < LANES:
                tile = tile + pltpu.roll(tile, span, 1)
                span *= 2
            yield
            top = tile + jnp.sum(
                jnp.where(eight_row > 0, tile * taps, 0.0), axis=0, keepdims=True
            )
            tops.append(jnp.where(eight_row == 0, top, tile * taps[0:1]))
            longs.append(jnp.sum(pairs, axis=0, keepdims=True))
            yield
            if k < SIDE - 1:
                return
            b, n = g // per_block, lax.rem(g, per_block)
            tile = tiles_own[s, b]
            for i in range(SIDE):
                tile = jnp.where(comp_lane == n - (SIDE - 1) + i, tops[i], tile)
            tiles_own[s, b] = tile
            for i in range(SIDE):
                row = lax.rem(g, 8) - (SIDE - 1) + i
                tiles_own[s, blocks + g // 8, pl.ds(row, 1)] = longs[i]
            tops.clear()
            longs.clear()

        for b in range(blocks):
            tiles_own[s, b] = jnp.zeros((8, LANES), F32)
        lockstep(0, groups, SIDE, each)

        @pl.when(s == me)
        def _():
            tiles_all[rank] = tiles_own[s]

        tile_steps(s, lambda copy: copy.start())

    def go_down(s, sums, scale):
        factor = fac_c[s]
        pull = spread_rows(sums * (1.0 / width)) * factor * factor * factor

        def finish(g, k):
            grad = upstream[s, g] + factor * inner_buf[g] - rows_in[s, g].astype(F32) * pull
            yield
            if scale is not None:
                grad = grad * scale
            upstream[s - 1, g] = grad.astype(BF16).astype(F32)

        lockstep(0, groups, SIDE, finish)

    last = sections - 1
    backward(last, False)
    stat_start(last, lane_sums(acc_ref[...], fold, score_line))
    loop(1, n_resp, lambda step: comp_copy(step).wait_send())

    def weights_sent(step):
        for kind in range(3):
            weight_copy(kind, step).wait_send()

    loop(1, sections, weights_sent)

    def ranks_sent(step):
        pool_copy(step).wait_send()
        first_copy(step).wait_send()

    loop(1, ranks, ranks_sent)
    winner = jnp.full((8, LANES), -1, jnp.int32)
    loser = winner
    for m in range(micro):
        for p in range(pair_ref.shape[2]):
            here = (eight_row == m) & (eight_lane == p)
            winner = jnp.where(here, pair_ref[m, 0, p], winner)
            loser = jnp.where(here, pair_ref[m, 1, p], loser)
    signs = [
        jnp.where(winner == r, 1.0, 0.0) - jnp.where(loser == r, 1.0, 0.0)
        for r in range(n_resp)
    ]
    masks = [comp_lane == eight_row * n_resp + r for r in range(n_resp)]
    sums = stat_finish(last)
    totals = jnp.sum(jnp.where(eight_lane == length, sums, 0.0), axis=1, keepdims=True)
    totals = jnp.broadcast_to(totals, (8, LANES))
    scores = []
    for r in range(n_resp):
        rows = totals[r : r + 1]
        for m in range(1, micro):
            rows = jnp.where(eight_row == m, totals[m * n_resp + r : m * n_resp + r + 1], rows)
        scores.append(jnp.broadcast_to(rows, (8, LANES)))
    own_score = scores[0]
    margin = jnp.zeros((8, LANES), F32)
    for r in range(n_resp):
        margin = margin + scores[r] * signs[r]
        own_score = jnp.where(me_resp == r, scores[r], own_score)
    score_ref[...] = own_score[:micro, :1].astype(BF16)
    weight = 1.0 / (1.0 + jnp.exp(margin))
    slopes = jnp.zeros((8, LANES), F32)
    for r in range(n_resp):
        slope = -jnp.sum(signs[r] * weight, axis=1, keepdims=True)
        slopes = jnp.where(masks[r], slope, slopes)
    slopes = jnp.sum(slopes, axis=0, keepdims=True)
    for s in range(sections - 1):
        scales[s] = jnp.ones((8, LANES), F32)
    scales[last] = jnp.broadcast_to(slopes, (8, LANES))
    go_down(last, sums, slopes)

    def backward_step(step):
        s = sections - 1 - step
        slot = last + step
        backward(s, False)
        stat_start(slot, lane_sums(acc_ref[...], fold))
        loop(s, jnp.where(step == 1, s + 2, s + 1), gradients)
        go_down(s, stat_finish(slot), None)

    loop(1, sections - 1, backward_step)
    backward(0, True)
    gradients(0)

    loop(0, 2 * sections - 2, lambda slot: stat_wait(slot, stat_send))
    loop(0, sections, lambda s: tile_steps(s, lambda copy: copy.wait_send()))

    def arrive(step):
        source = lax.rem(rank + step, ranks)
        remote(
            tiles_own.at[0],
            tiles_all.at[source],
            tile_send.at[0, 0],
            tile_recv.at[source],
            place(source),
        ).wait_recv()

    loop(1, ranks, arrive)
    lines = []
    for q in range(ranks):
        for b in range(blocks):
            lanes = slice((q * blocks + b) * LANES, (q * blocks + b + 1) * LANES)
            tile = tiles_all[q, b]
            gain_out[:, lanes] = tile[0:1]
            for j in range(tap_count):
                taps_short_out[j, :, lanes] = tile[1 + j : 2 + j]
        lines += [tiles_all[q, blocks + k] for k in range(groups // 8)]
    taps_long_out[...] = jnp.transpose(jnp.concatenate(lines, axis=0))


def run_wide(dims, *arrays):
    sections, n_resp, micro, length, chans, per_group, width = dims
    comps = micro * n_resp
    ranks = sections * n_resp
    groups = chans // per_group
    blocks = chans // LANES
    total = 2 * length
    tap_count = arrays[3].shape[0]
    group_all = width // per_group
    tile = (8, LANES)
    tiles = blocks + groups // 8
    vmem = pl.BlockSpec(memory_space=pltpu.VMEM)
    hbm = pl.BlockSpec(memory_space=pl.ANY)
    smem = pl.BlockSpec(memory_space=pltpu.SMEM)
    slots = 2 * sections - 2
    per = (sections, groups)
    dma = pltpu.SemaphoreType.DMA
    return pl.pallas_call(
        functools.partial(wide_kernel, dims),
        out_shape=(
            jax.ShapeDtypeStruct((micro, 1), BF16),
            jax.ShapeDtypeStruct((1, width), F32),
            jax.ShapeDtypeStruct((tap_count, 1, width), F32),
            jax.ShapeDtypeStruct((LANES, group_all), F32),
        ),
        in_specs=[hbm] * 6 + [smem] * 3,
        out_specs=(vmem,) * 4,
        scratch_shapes=[
            pltpu.VMEM((micro * length, width), BF16),
            pltpu.VMEM((length, width), BF16),
            pltpu.VMEM((LANES, group_all), F32),
            pltpu.VMEM((1, chans), F32),
            pltpu.VMEM((n_resp, micro * length, chans), BF16),
            pltpu.VMEM((sections, n_resp, length, chans), BF16),
            pltpu.VMEM((sections, 1, chans), F32),
            pltpu.VMEM((sections, tap_count, 1, chans), F32),
            pltpu.VMEM((group_all, 2 * LANES), F32),
            pltpu.VMEM((sections, groups, 2 * LANES), F32),
            pltpu.VMEM((comps * LANES, (LANES // per_group) * LANES), BF16),
            pltpu.VMEM((micro * LANES, (LANES // per_group) * LANES), BF16),
            pltpu.VMEM((blocks * length, comps * LANES), BF16),
            pltpu.VMEM(tile, F32),
            pltpu.VMEM((ranks,) + tile, F32),
            pltpu.VMEM((slots,) + tile, F32),
            pltpu.VMEM((slots, ranks) + tile, F32),
            pltpu.VMEM(per + (length, LANES), BF16),
            pltpu.VMEM(per + (length, LANES), BF16),
            pltpu.VMEM(per + (length, LANES), F32),
            pltpu.VMEM(per + (total, LANES), BF16),
            pltpu.VMEM(per + (length, LANES), BF16),
            pltpu.VMEM(per + (length, LANES), BF16),
            pltpu.VMEM(per + (total, LANES), BF16),
            pltpu.VMEM(per + tile, F32),
            pltpu.VMEM((groups,) + tile, F32),
            pltpu.VMEM((sections, length, LANES), F32),
            pltpu.VMEM((sections, length, LANES), F32),
            pltpu.VMEM((groups, 8 + total, LANES), F32),
            pltpu.VMEM(per + (total + 8, LANES), F32),
            pltpu.VMEM(per + (length, LANES), F32),
            pltpu.VMEM((groups, length, LANES), F32),
            pltpu.VMEM(per + (length, LANES), BF16),
            pltpu.VMEM((length, LANES), F32),
            pltpu.VMEM((sections,) + tile, F32),
            pltpu.VMEM((sections, tiles) + tile, F32),
            pltpu.VMEM((ranks, tiles) + tile, F32),
            dma((8,)),
            dma((n_resp,)),
            dma((n_resp,)),
            dma((3, sections)),
            dma((3, sections)),
            dma((ranks,)),
            dma((ranks,)),
            dma((ranks,)),
            dma((ranks,)),
            dma((slots,)),
            dma((slots,)),
            dma((sections, n_resp)),
            dma((ranks,)),
        ],
        compiler_params=pltpu.CompilerParams(
            collective_id=1, has_side_effects=True, vmem_limit_bytes=56 * 1024 * 1024
        ),
    )(*arrays)


def wide_body(
    completion_rows,
    prompt_pool,
    norm_gain,
    short_taps,
    long_taps,
    score_head,
    live_lengths,
    prompt_owner,
    pair_index,
):
    sections = lax.axis_size("section")
    n_resp = lax.axis_size("resp")
    micro, _, length, width = completion_rows.shape
    chans = width // (sections * n_resp)
    per_group = width // long_taps.shape[2]
    scores, gain_grad, short_grad, long_grad = run_wide(
        (sections, n_resp, micro, length, chans, per_group, width),
        completion_rows.reshape(micro * length, width),
        prompt_pool[0, 0],
        norm_gain,
        short_taps.transpose(1, 0, 2),
        long_taps[0],
        score_head[None],
        prompt_owner,
        pair_index.transpose(0, 2, 1),
        live_lengths.T,
    )
    return (
        scores,
        gain_grad,
        short_grad.transpose(1, 0, 2),
        long_grad[None],
    )


def is_wide(
    completion_rows,
    prompt_pool,
    norm_gain,
    short_taps,
    long_taps,
    score_head,
    live_lengths,
    prompt_owner,
    pair_index,
):
    sections = lax.axis_size("section")
    n_resp = lax.axis_size("resp")
    micro, _, length, width = completion_rows.shape
    per_group = width // long_taps.shape[2]
    return (
        micro * n_resp * per_group == LANES
        and micro * n_resp == 8
        and width % (sections * n_resp * LANES) == 0
        and prompt_pool.shape[2] == length
        and long_taps.shape[1] == 2 * length == LANES
        and micro * length == LANES
        and short_taps.shape[1] == 7
        and sections >= 3
    )


def either(*arrays):
    return wide_body(*arrays) if is_wide(*arrays) else body(*arrays)


def solution(mesh):
    placed = (
        P(None, ("groups", "resp"), None, None),
        P("section", ("groups", "resp"), None, None),
        P("section", None),
        P("section", None, None),
        P("section", None, None),
        P(),
        P(None, ("groups", "resp")),
        P("groups"),
        P(None, "groups", None),
    )
    return jax.shard_map(
        either,
        mesh=mesh,
        in_specs=placed,
        out_specs=(
            P(None, ("groups", "resp")),
            P("section", "groups"),
            P("section", "groups", None),
            P("section", "groups", None),
        ),
        check_vma=False,
    )
```

```python
import functools

import jax
import jax.numpy as jnp
from jax import lax
from jax.experimental import pallas as pl
from jax.experimental.pallas import tpu as pltpu
from jax.sharding import PartitionSpec as P

LANES = 128
MESH = pl.DeviceIdType.MESH
F32 = jnp.float32
BF16 = jnp.bfloat16


def rows_to_line(block):
    line = jnp.sum(jnp.transpose(block), axis=0, keepdims=True)
    return jnp.broadcast_to(line, (8, LANES))


def line_to_rows(tile):
    return jnp.transpose(jnp.broadcast_to(tile[0:1], (LANES, LANES)))


def kernel(
    dims,
    direct,
    comp_ref,
    prompt_ref,
    gain_hbm,
    short_hbm,
    taps_hbm,
    owner_ref,
    head_ref,
    ends_ref,
    length_ref,
    score_ref,
    *rest,
):
    sections, n_resp, micro, length, prompt_len, chans, per_group, width = dims
    outs, rest = (rest[:3], rest[3:]) if direct else (rest[:1], rest[1:])
    (
        toep,
        toep_t,
        pool,
        chosen_rows,
        gain_ref,
        short_ref,
        taps_ref,
        rows_in,
        short_out,
        long_out,
        fac_p,
        fac_c,
        upstream,
        partial,
        stat_acc,
        score_acc,
        prompt_acc,
        stat_out,
        stat_in,
        resp_out,
        resp_in,
        tiles_own,
        tiles_in,
        tiles_sum,
        tiles_all,
        local_sem,
        weight_sems,
        spread_sems,
        pool_sems,
        stat_sems,
        resp_sems,
        part_sems,
        tile_send,
        tile_recv,
    ) = rest
    groups = LANES // per_group
    blocks = chans // LANES
    group_rows = blocks * groups
    total = prompt_len + length
    me = lax.axis_index("section")
    me_resp = lax.axis_index("resp")
    own_lanes = pl.ds(pl.multiple_of(me * chans, chans), chans)

    def lane_slice(block):
        return pl.ds(pl.multiple_of(block * LANES, LANES), LANES)

    def head_slice(block):
        return pl.ds(pl.multiple_of(me * chans + block * LANES, LANES), LANES)

    def wide_slice(block):
        return pl.ds(pl.multiple_of(block * micro * LANES, LANES), micro * LANES)

    def loop(low, high, step_of):
        def run(index, carry):
            step_of(index)
            return carry

        lax.fori_loop(low, high, run, 0)

    def swap(axis, count, mine, out_ref, in_ref, sems):
        def copy(step):
            return pltpu.make_async_remote_copy(
                src_ref=out_ref,
                dst_ref=in_ref.at[mine],
                send_sem=sems.at[0, step],
                recv_sem=sems.at[1, step],
                device_id={axis: lax.rem(mine + step, count)},
                device_id_type=MESH,
            )

        loop(1, count, lambda step: copy(step).start())
        in_ref[mine] = out_ref[...]
        return lambda: loop(1, count, lambda step: copy(step).wait())

    def start_stats(slot, first, second):
        stat_out[slot, 0] = first
        stat_out[slot, 1] = second
        wait = swap(
            "section", sections, me, stat_out.at[slot], stat_in.at[slot], stat_sems.at[slot]
        )

        def finish():
            wait()
            return jnp.sum(stat_in[slot], axis=0)

        return finish

    def weight_copies(step):
        peer = lax.rem(me + step, sections)
        lanes = pl.ds(pl.multiple_of(peer * chans, chans), chans)
        rows = pl.ds(pl.multiple_of(peer * group_rows, group_rows), group_rows)
        return [
            pltpu.make_async_remote_copy(
                src_ref=source,
                dst_ref=target,
                send_sem=weight_sems.at[0, kind, step],
                recv_sem=weight_sems.at[1, kind, step],
                device_id={"section": peer},
                device_id_type=MESH,
            )
            for kind, source, target in (
                (0, gain_hbm.at[:, lanes], gain_ref.at[me]),
                (2, short_hbm.at[:, lanes], short_ref.at[me]),
                (1, taps_hbm.at[rows, :], taps_ref.at[me]),
            )
        ]

    def start_weights(step):
        for copy in weight_copies(step):
            copy.start()

    def wait_weights(step):
        for copy in weight_copies(step):
            copy.wait()

    own_rows = pl.ds(pl.multiple_of(me * group_rows, group_rows), group_rows)
    local_copies = [
        pltpu.make_async_copy(comp_ref.at[:, own_lanes], rows_in.at[0], local_sem.at[0]),
        pltpu.make_async_copy(gain_hbm.at[:, own_lanes], gain_ref.at[me], local_sem.at[1]),
        pltpu.make_async_copy(short_hbm.at[:, own_lanes], short_ref.at[me], local_sem.at[3]),
        pltpu.make_async_copy(taps_hbm.at[own_rows, :], taps_ref.at[me], local_sem.at[2]),
    ]

    def spread_copy(step):
        peer = lax.rem(me + step, sections)
        lanes = pl.ds(pl.multiple_of(peer * chans, chans), chans)
        return pltpu.make_async_remote_copy(
            src_ref=prompt_ref.at[:, lanes],
            dst_ref=pool.at[me, me_resp],
            send_sem=spread_sems.at[0, step],
            recv_sem=spread_sems.at[1, step],
            device_id={"section": peer},
            device_id_type=MESH,
        )

    def pool_copy(s, step):
        return pltpu.make_async_remote_copy(
            src_ref=pool.at[s, me_resp],
            dst_ref=pool.at[s, me_resp],
            send_sem=pool_sems.at[0, s, step],
            recv_sem=pool_sems.at[1, s, step],
            device_id={"resp": lax.rem(me_resp + step, n_resp)},
            device_id_type=MESH,
        )

    def own_pool():
        return pltpu.make_async_copy(
            prompt_ref.at[:, own_lanes], pool.at[me, me_resp], local_sem.at[4]
        )

    def start_pool(s):
        step = lax.rem(me - s + sections, sections)

        @pl.when(step == 0)
        def _():
            own_pool().wait()

        @pl.when(step > 0)
        def _():
            spread_copy(step).wait()

        loop(1, n_resp, lambda d: pool_copy(s, d).start())

    def wait_pool(s):
        loop(1, n_resp, lambda d: pool_copy(s, d).wait())

    if direct:
        own_pool().start()
        loop(1, sections, lambda step: spread_copy(step).start())
    for copy in local_copies:
        copy.start()
    loop(1, sections, start_weights)
    if direct:
        start_pool(0)
    for copy in local_copies:
        copy.wait()

    def first_stats(block):
        wide = rows_in[0, :, lane_slice(block)].astype(F32)
        stat_acc[...] += wide * wide

    stat_acc[...] = jnp.zeros_like(stat_acc)
    loop(0, blocks, first_stats)
    loop(1, sections, wait_weights)

    t_row = lax.broadcasted_iota(jnp.int32, (length, LANES), 0)
    s_lane = lax.broadcasted_iota(jnp.int32, (length, LANES), 1)
    keep = s_lane <= prompt_len + t_row
    s_row = lax.broadcasted_iota(jnp.int32, (total, LANES), 0)
    t_lane = lax.broadcasted_iota(jnp.int32, (total, LANES), 1)
    keep_t = s_row <= prompt_len + t_lane

    def build(s, block):
        rows = pl.ds(pl.multiple_of(block * groups, groups), groups)
        both = taps_ref[s, rows, :]
        flipped, plain = both[:, :LANES], both[:, LANES:]
        for g in range(groups):
            base = pl.multiple_of((block * groups + g) * length, length)
            wide = jnp.broadcast_to(flipped[g : g + 1], (length, LANES))
            wide = pltpu.roll(wide, prompt_len, 1, stride=1, stride_axis=0)
            wide = jnp.where(keep, wide, 0.0)
            high = wide.astype(BF16)
            low = (wide - high.astype(F32)).astype(BF16)
            toep[s, pl.ds(base, length), :] = jnp.concatenate([high, high, low], axis=1)
            base = pl.multiple_of((block * groups + g) * total, total)
            wide = jnp.broadcast_to(plain[g : g + 1], (total, LANES))
            wide = pltpu.roll(wide, prompt_len, 1, stride=1, stride_axis=0)
            toep_t[s, pl.ds(base, total), :] = jnp.where(keep_t, wide, 0.0).astype(BF16)

    def choose(s, block):
        lanes = lane_slice(block)
        for m in range(micro):
            rows = slice(m * prompt_len, (m + 1) * prompt_len)
            if direct:
                picked = jnp.zeros((prompt_len, LANES), F32)
                for r in range(n_resp):
                    flag = jnp.full((prompt_len, LANES), owner_ref[m], jnp.int32) == r
                    picked = jnp.where(flag, pool[s, r, :, lanes].astype(F32), picked)
                chosen_rows[s, rows, lanes] = picked.astype(BF16)
            else:
                picked = prompt_ref[s, rows, lanes].astype(F32)
                chosen_rows[s, rows, lanes] = prompt_ref[s, rows, lanes]
            prompt_acc[rows, :] += picked * picked

    row_id = lax.broadcasted_iota(jnp.int32, (total, LANES), 0)
    wide_group = (
        lax.broadcasted_iota(jnp.int32, (1, micro * LANES), 1) % LANES
    ) // per_group
    tap_count = short_ref.shape[1]

    def pick(stacked, rows):
        out = stacked[0:rows]
        for g in range(1, groups):
            out = jnp.where(wide_group == g, stacked[g * rows : (g + 1) * rows], out)
        return out

    def joined_rows(s, m, lanes):
        rows_p = slice(m * prompt_len, (m + 1) * prompt_len)
        rows_c = slice(m * length, (m + 1) * length)
        joined = jnp.concatenate(
            [chosen_rows[s, rows_p, lanes].astype(F32), rows_in[s, rows_c, lanes].astype(F32)],
            axis=0,
        )
        factor = jnp.concatenate([fac_p[s, rows_p, :], fac_c[s, rows_c, :]], axis=0)
        return joined, factor

    def forward(s, carry):
        if direct:
            wait_pool(s)

            @pl.when(s + 1 < sections)
            def _():
                start_pool(s + 1)

        prompt_acc[...] = jnp.zeros_like(prompt_acc)
        loop(0, blocks, lambda block: choose(s, block))
        finish = start_stats(s, rows_to_line(stat_acc[...]), rows_to_line(prompt_acc[...]))
        loop(0, blocks, lambda block: build(s, block))
        sums = finish()
        fac_c[s] = lax.rsqrt(line_to_rows(sums[0]) * (1.0 / width) + 1e-06)
        fac_p[s] = lax.rsqrt(line_to_rows(sums[1]) * (1.0 / width) + 1e-06)
        stat_acc[...] = jnp.zeros_like(stat_acc)
        score_acc[...] = jnp.zeros_like(score_acc)

        def run(block, carry):
            lanes = lane_slice(block)
            wide = wide_slice(block)
            gain = gain_ref[s, :, lanes]
            short = short_ref[s, :, lanes]
            parts, lows, saved = [], [], []
            for m in range(micro):
                joined, factor = joined_rows(s, m, lanes)
                normed = joined * factor * gain
                shorter = normed * short[0:1]
                for j in range(1, tap_count):
                    moved = jnp.where(row_id >= j, pltpu.roll(normed, j, 0), 0.0)
                    shorter = shorter + moved * short[j : j + 1]
                high = shorter.astype(BF16)
                parts.append(high)
                lows.append((shorter - high.astype(F32)).astype(BF16))
                saved.append((joined[prompt_len:], normed[prompt_len:]))
            high = jnp.concatenate(parts, axis=1)
            short_out[s, :, wide] = high
            rhs = jnp.concatenate([high, jnp.concatenate(lows, axis=1), high], axis=0)
            base = pl.multiple_of(block * groups * length, groups * length)
            stacked = jnp.dot(
                toep[s, pl.ds(base, groups * length), :], rhs, preferred_element_type=F32
            )
            longer_all = pick(stacked, length)
            for m in range(micro):
                rows = slice(m * length, (m + 1) * length)
                longer = longer_all[:, m * LANES : (m + 1) * LANES]
                long_out[s, rows, lanes] = longer
                mixed = (saved[m][0] + saved[m][1] * longer).astype(BF16)
                rows_in[s + 1, rows, lanes] = mixed
                mixed = mixed.astype(F32)
                stat_acc[rows, :] += mixed * mixed
                score_acc[rows, :] += mixed * head_ref[0:1, head_slice(block)]
            return carry

        lax.fori_loop(0, blocks, run, 0)

        return carry

    lax.fori_loop(0, sections, forward, 0)

    live = []
    for m in range(micro):
        count = jnp.full((length, LANES), length_ref[m, 0], jnp.int32)
        live.append(jnp.where(t_row < count, 1.0, 0.0) / jnp.sqrt(count.astype(F32)))
    tile_rows = []
    for m in range(micro):
        rows = slice(m * length, (m + 1) * length)
        line = jnp.sum(score_acc[rows, :] * live[m], axis=0, keepdims=True)
        tile_rows.append(jnp.broadcast_to(jnp.sum(line, axis=1, keepdims=True), (1, LANES)))
    tile_rows.append(jnp.zeros((8 - micro, LANES), F32))
    score_tile = jnp.concatenate(tile_rows, axis=0)
    own_score = start_stats(sections, score_tile, score_tile)()[0]
    score_ref[...] = own_score
    resp_out[...] = own_score
    swap("resp", n_resp, me_resp, resp_out, resp_in, resp_sems)()
    winner, loser = ends_ref[0], ends_ref[1]

    def signs(r):
        return jnp.where(winner == r, 1.0, 0.0) - jnp.where(loser == r, 1.0, 0.0)

    margin = lax.fori_loop(
        0, n_resp, lambda r, acc: acc + resp_in[r] * signs(r), jnp.zeros((8, LANES), F32)
    )
    weight = 1.0 / (1.0 + jnp.exp(margin))
    slopes = -jnp.sum(signs(me_resp) * weight, axis=1, keepdims=True)

    def seed(block, carry):
        lanes = lane_slice(block)
        for m in range(micro):
            rows = slice(m * length, (m + 1) * length)
            upstream[rows, lanes] = live[m] * slopes[m : m + 1] * head_ref[0:1, head_slice(block)]
        return carry

    lax.fori_loop(0, blocks, seed, 0)

    keep_pair = total - 1 - s_lane <= prompt_len + t_row
    reverse = (
        lax.broadcasted_iota(jnp.int32, (total, total), 0)
        + lax.broadcasted_iota(jnp.int32, (total, total), 1)
        == total - 1
    )
    reverse = jnp.where(reverse, 1.0, 0.0).astype(BF16)

    share = 2 * blocks // n_resp

    def part_slice(r):
        return pl.ds(r * share, share)

    def part_steps(s, action):
        def each(step):
            peer = lax.rem(me_resp + step, n_resp)
            action(
                pltpu.make_async_remote_copy(
                    src_ref=tiles_own.at[s, part_slice(peer)],
                    dst_ref=tiles_in.at[s, me_resp],
                    send_sem=part_sems.at[0, s, step],
                    recv_sem=part_sems.at[1, s, step],
                    device_id={"resp": peer},
                    device_id_type=MESH,
                )
            )

        loop(1, n_resp, each)

    def tile_copy(s, step, k, r):
        return pltpu.make_async_remote_copy(
            src_ref=tiles_sum.at[s],
            dst_ref=tiles_all.at[k, r],
            send_sem=tile_send.at[s, step],
            recv_sem=tile_recv.at[k, r],
            device_id={"section": s, "resp": lax.rem(me_resp + step, n_resp)},
            device_id_type=MESH,
        )

    def tile_steps(s, action):
        def each(step):
            @pl.when(jnp.logical_not((s == me) & (step == 0)))
            def _():
                action(tile_copy(s, step, me, me_resp))

        loop(0, n_resp, each)

    def backward(step, carry):
        s = sections - 1 - step
        stat_acc[...] = jnp.zeros_like(stat_acc)

        def run(block, carry):
            lanes = lane_slice(block)
            wide = wide_slice(block)
            gain = gain_ref[s, :, lanes]
            short = short_ref[s, :, lanes]
            parts, saved = [], []
            for m in range(micro):
                rows = slice(m * length, (m + 1) * length)
                joined, factor = joined_rows(s, m, lanes)
                scaled = joined * factor
                normed = scaled * gain
                above = upstream[rows, lanes]
                parts.append((above * normed[prompt_len:]).astype(BF16))
                saved.append((joined[prompt_len:], scaled, normed, above))
            d_long = jnp.concatenate(parts, axis=1)
            base = pl.multiple_of(block * groups * total, groups * total)
            stacked = jnp.dot(
                toep_t[s, pl.ds(base, groups * total), :][:, :length],
                d_long,
                preferred_element_type=F32,
            )
            d_short_all = pick(stacked, total)
            turned = jnp.dot(reverse, short_out[s, :, wide], preferred_element_type=F32)
            d_wide = d_long.astype(F32)
            masked = jnp.concatenate(
                [
                    jnp.where(wide_group == g, d_wide, 0.0).astype(BF16)
                    for g in range(groups)
                ],
                axis=0,
            )
            pairs = lax.dot_general(
                masked,
                turned.astype(BF16),
                (((1,), (1,)), ((), ())),
                preferred_element_type=F32,
            )
            lines = []
            for g in range(groups):
                one = jnp.where(keep_pair, pairs[g * length : (g + 1) * length], 0.0)
                one = pltpu.roll(one, LANES + 1 - length, 1, stride=1, stride_axis=0)
                lines.append(jnp.sum(one, axis=0, keepdims=True))
            tiles_own[s, 2 * block + 1] = jnp.concatenate(lines, axis=0)
            grads = [jnp.zeros((1, LANES), F32)] * (tap_count + 1)
            for m in range(micro):
                rows = slice(m * length, (m + 1) * length)
                joined_c, scaled, normed, above = saved[m]
                d_short = d_short_all[:, m * LANES : (m + 1) * LANES]
                d_normed = d_short * short[0:1]
                grads[1] = grads[1] + jnp.sum(d_short * normed, axis=0, keepdims=True)
                for j in range(1, tap_count):
                    moved = jnp.where(
                        row_id < total - j, pltpu.roll(d_short, total - j, 0), 0.0
                    )
                    d_normed = d_normed + moved * short[j : j + 1]
                    grads[1 + j] = grads[1 + j] + jnp.sum(
                        moved * normed, axis=0, keepdims=True
                    )
                direct = above * long_out[s, rows, lanes]
                d_normed = jnp.concatenate(
                    [d_normed[:prompt_len], d_normed[prompt_len:] + direct], axis=0
                )
                grads[0] = grads[0] + jnp.sum(d_normed * scaled, axis=0, keepdims=True)
                inner = d_normed[prompt_len:] * gain
                partial[rows, lanes] = inner
                stat_acc[rows, :] += inner * joined_c
            tiles_own[s, 2 * block] = jnp.concatenate(grads, axis=0)
            return carry

        lax.fori_loop(0, blocks, run, 0)

        if direct:
            part_steps(s, lambda copy: copy.start())
            parts_in = tiles_in.at[s]
            parts_in[me_resp] = tiles_own[s, part_slice(me_resp)]

        @pl.when(s > 0)
        def _():
            line = rows_to_line(stat_acc[...])
            all_sums = start_stats(sections + 1 + step, line, line)()[0]
            factor = fac_c[s]
            pull = line_to_rows(all_sums) * (1.0 / width) * factor * factor * factor

            def finish(block, carry):
                lanes = lane_slice(block)
                grad = (
                    upstream[:, lanes]
                    + factor * partial[:, lanes]
                    - rows_in[s, :, lanes].astype(F32) * pull
                )
                upstream[:, lanes] = grad.astype(BF16).astype(F32)
                return carry

            lax.fori_loop(0, blocks, finish, 0)

        if direct:
            part_steps(s, lambda copy: copy.wait())
            tiles_sum[s] = jnp.sum(tiles_in[s], axis=0)

            @pl.when(s == me)
            def _():
                tiles_all[me, me_resp] = tiles_sum[s]

            tile_steps(s, lambda copy: copy.start())

        return carry

    lax.fori_loop(0, sections, backward, 0)

    if direct:
        loop(0, sections, lambda s: tile_steps(s, lambda copy: copy.wait_send()))

        def arrive(step):
            k, r = step // n_resp, step % n_resp

            @pl.when(jnp.logical_not((k == me) & (r == me_resp)))
            def _():
                tile_copy(0, 0, k, r).wait_recv()

        loop(0, sections * n_resp, arrive)
        gain_out, taps_short_out, taps_long_out = outs
        per_line = LANES // groups
        for line in range(sections * blocks // per_line):
            lines = []
            for place in range(per_line):
                block = line * per_line + place
                lanes = slice(block * LANES, (block + 1) * LANES)
                owner, local = divmod(2 * block, 2 * blocks)
                first, second = (divmod(local + kind, share) for kind in range(2))
                tile = tiles_all[owner, first[0], first[1]]
                gain_out[:, lanes] = tile[0:1]
                taps_short_out[:, lanes] = tile[1:]
                lines.append(tiles_all[owner, second[0], second[1]])
            lanes = slice(line * LANES, (line + 1) * LANES)
            taps_long_out[:, lanes] = jnp.transpose(jnp.concatenate(lines, axis=0))
    else:
        outs[0][...] = tiles_own[...]


def run_kernel(dims, direct, *arrays):
    sections, n_resp, micro, length, prompt_len, chans, per_group, width = dims
    rows = micro * length
    total = prompt_len + length
    group_total = chans // per_group
    tile = (8, LANES)
    tiles = 2 * chans // LANES
    share = tiles // n_resp if direct else 1
    ranks = n_resp if direct else 1
    vmem = pl.BlockSpec(memory_space=pltpu.VMEM)
    hbm = pl.BlockSpec(memory_space=pl.ANY)
    smem = pl.BlockSpec(memory_space=pltpu.SMEM)
    tap_count = arrays[3].shape[0]
    if direct:
        out_shapes = [(1, width), (tap_count, width), (LANES, width // per_group)]
    else:
        out_shapes = [(sections, tiles) + tile]
    return pl.pallas_call(
        functools.partial(kernel, dims, direct),
        out_shape=(
            jax.ShapeDtypeStruct(tile, F32),
            *(jax.ShapeDtypeStruct(shape, F32) for shape in out_shapes),
        ),
        in_specs=[hbm, hbm if direct else vmem, hbm, hbm, hbm, smem, vmem, vmem, smem],
        out_specs=(vmem,) * (1 + len(out_shapes)),
        scratch_shapes=[
            pltpu.VMEM((sections, group_total * length, 3 * LANES), BF16),
            pltpu.VMEM((sections, group_total * total, LANES), BF16),
            pltpu.VMEM((sections, ranks, prompt_len, chans), BF16),
            pltpu.VMEM((sections, micro * prompt_len, chans), BF16),
            pltpu.VMEM((sections, 1, chans), F32),
            pltpu.VMEM((sections, tap_count, chans), F32),
            pltpu.VMEM((sections, group_total, 2 * LANES), F32),
            pltpu.VMEM((sections + 1, rows, chans), BF16),
            pltpu.VMEM((sections, total, micro * chans), BF16),
            pltpu.VMEM((sections, rows, chans), F32),
            pltpu.VMEM((sections, micro * prompt_len, LANES), F32),
            pltpu.VMEM((sections, rows, LANES), F32),
            pltpu.VMEM((rows, chans), F32),
            pltpu.VMEM((rows, chans), F32),
            pltpu.VMEM((rows, LANES), F32),
            pltpu.VMEM((rows, LANES), F32),
            pltpu.VMEM((micro * prompt_len, LANES), F32),
            pltpu.VMEM((2 * sections, 2) + tile, F32),
            pltpu.VMEM((2 * sections, sections, 2) + tile, F32),
            pltpu.VMEM(tile, F32),
            pltpu.VMEM((n_resp,) + tile, F32),
            pltpu.VMEM((sections, tiles) + tile, F32),
            pltpu.VMEM((sections, ranks, share) + tile, F32),
            pltpu.VMEM((sections, share) + tile, F32),
            pltpu.VMEM((sections, ranks, share) + tile, F32),
            pltpu.SemaphoreType.DMA((5,)),
            pltpu.SemaphoreType.DMA((2, 3, sections)),
            pltpu.SemaphoreType.DMA((2, sections)),
            pltpu.SemaphoreType.DMA((2, sections, ranks)),
            pltpu.SemaphoreType.DMA((2 * sections, 2, sections)),
            pltpu.SemaphoreType.DMA((2, n_resp)),
            pltpu.SemaphoreType.DMA((2, sections, ranks)),
            pltpu.SemaphoreType.DMA((sections, ranks)),
            pltpu.SemaphoreType.DMA((sections, ranks)),
        ],
        compiler_params=pltpu.CompilerParams(
            has_side_effects=True, vmem_limit_bytes=56 * 1024 * 1024
        ),
    )(*arrays)


def body(
    completion_rows,
    prompt_pool,
    norm_gain,
    short_taps,
    long_taps,
    score_head,
    live_lengths,
    prompt_owner,
    pair_index,
):
    sections = lax.axis_size("section")
    n_resp = lax.axis_size("resp")
    me_resp = lax.axis_index("resp")
    micro, _, length, width = completion_rows.shape
    prompt_len = prompt_pool.shape[2]
    chans = width // sections
    tap_len, group_all = long_taps.shape[1:]
    per_group = width // group_all
    dims = (sections, n_resp, micro, length, prompt_len, chans, per_group, width)

    tiles = 2 * chans // LANES
    direct = n_resp <= 8 and tiles % n_resp == 0

    taps = long_taps[0].T
    flipped = jnp.concatenate([taps[:, :1], taps[:, :0:-1]], axis=1)
    taps = jnp.concatenate([flipped, taps], axis=1)
    prompts = prompt_pool[0, 0]
    if not direct:
        split = prompts.reshape(prompt_len, sections, chans).transpose(1, 0, 2)
        split = lax.all_to_all(split, "section", 0, 0, tiled=True)
        here = (prompt_owner == me_resp)[None, :, None, None]
        split = lax.psum(jnp.where(here, split[:, None], jnp.zeros((), BF16)), "resp")
        prompts = split.reshape(sections, micro * prompt_len, chans)
    rows = completion_rows.reshape(micro * length, width)
    head = score_head[None]

    ends = jnp.pad(
        pair_index.transpose(2, 0, 1),
        ((0, 0), (0, 8 - micro), (0, LANES - pair_index.shape[1])),
        constant_values=-1,
    )
    scores, *grads = run_kernel(
        dims,
        direct,
        rows,
        prompts,
        norm_gain,
        short_taps[0],
        taps,
        prompt_owner,
        head,
        ends,
        live_lengths,
    )
    scores = scores[:micro, :1].astype(BF16)
    if direct:
        return (scores, grads[0], grads[1][None], grads[2][None])
    grads = lax.psum(grads[0], "resp")
    grads = lax.all_to_all(grads, "section", 0, 0, tiled=True)
    grads = grads.reshape(sections * tiles // 2, 2, 8, LANES)
    gs_grad = grads[:, 0].transpose(1, 0, 2).reshape(8, width)
    taps_grad = grads[:, 1].reshape(group_all, tap_len).T
    return (
        scores,
        gs_grad[:1],
        gs_grad[None, 1:],
        taps_grad[None],
    )


SIDE = 8


def wide_kernel(
    dims,
    comp_hbm,
    prompt_hbm,
    gain_hbm,
    short_hbm,
    taps_hbm,
    head_hbm,
    owner_ref,
    pair_ref,
    length_ref,
    score_ref,
    gain_out,
    taps_short_out,
    taps_long_out,
    comp_full,
    prompt_full,
    taps_full,
    head_own,
    comp_in,
    pool,
    gain_in,
    short_in,
    taps_src,
    taps_in,
    order_c,
    order_p,
    lined,
    first_out,
    first_in,
    stat_out,
    stat_in,
    rows_in,
    prompt_rows,
    long_out,
    short_out,
    toep,
    toep_p,
    toep_t,
    params,
    heads,
    fac_c,
    fac_p,
    normed_buf,
    d_short_buf,
    upstream,
    inner_buf,
    d_long_buf,
    acc_ref,
    scales,
    tiles_own,
    tiles_all,
    local_sem,
    comp_send,
    comp_recv,
    weight_send,
    weight_recv,
    pool_send,
    pool_recv,
    first_send,
    first_recv,
    stat_send,
    stat_recv,
    tile_send,
    tile_recv,
):
    sections, n_resp, micro, length, chans, per_group, width = dims
    comps = micro * n_resp
    ranks = sections * n_resp
    blocks = chans // LANES
    per_block = LANES // per_group
    groups = blocks * per_block
    tap_count = short_in.shape[1]
    total = 2 * length
    me = lax.axis_index("section")
    me_resp = lax.axis_index("resp")
    rank = me_resp * sections + me

    def loop(low, high, step_of):
        def run(index, carry):
            step_of(index)
            return carry

        lax.fori_loop(low, high, run, 0)

    def lockstep(low, high, count, step_of):
        def run(index, carry):
            live = [step_of(index * count + k, k) for k in range(count)]
            while live:
                live = [step for step in live if next(step, 0) is None]
            return carry

        lax.fori_loop(low // count, high // count, run, 0)

    def add_up(values):
        while len(values) > 1:
            values = [a + b for a, b in zip(values[::2], values[1::2])] + (
                values[-1:] if len(values) % 2 else []
            )
        return values[0]

    def place(peer):
        return {"section": lax.rem(peer, sections), "resp": peer // sections}

    def lanes_of(peer):
        return pl.ds(pl.multiple_of(peer * chans, chans), chans)

    def groups_of(peer):
        return pl.ds(pl.multiple_of(peer * groups, groups), groups)

    def remote(src, dst, send_sem, recv_sem, device):
        return pltpu.make_async_remote_copy(
            src_ref=src,
            dst_ref=dst,
            send_sem=send_sem,
            recv_sem=recv_sem,
            device_id=device,
            device_id_type=MESH,
        )

    load_comp = pltpu.make_async_copy(comp_hbm, comp_full, local_sem.at[0])
    load_prompt = pltpu.make_async_copy(prompt_hbm, prompt_full, local_sem.at[1])
    load_taps = pltpu.make_async_copy(taps_hbm, taps_full, local_sem.at[2])
    load_head = pltpu.make_async_copy(head_hbm.at[:, lanes_of(rank)], head_own, local_sem.at[3])
    own_comp = pltpu.make_async_copy(
        comp_hbm.at[:, lanes_of(rank)], comp_in.at[me_resp], local_sem.at[4]
    )
    own_pool = pltpu.make_async_copy(
        prompt_hbm.at[:, lanes_of(rank)], pool.at[me, me_resp], local_sem.at[5]
    )
    own_gain = pltpu.make_async_copy(
        gain_hbm.at[:, lanes_of(rank)], gain_in.at[me], local_sem.at[6]
    )
    own_short = pltpu.make_async_copy(
        short_hbm.at[:, :, lanes_of(rank)], short_in.at[me], local_sem.at[7]
    )

    def comp_copy(step):
        peer_resp = lax.rem(me_resp + step, n_resp)
        return remote(
            comp_hbm.at[:, lanes_of(peer_resp * sections + me)],
            comp_in.at[me_resp],
            comp_send.at[step],
            comp_recv.at[me_resp],
            {"resp": peer_resp},
        )

    def comp_wait(step):
        source = lax.rem(me_resp + step, n_resp)
        remote(
            comp_hbm.at[:, lanes_of(rank)],
            comp_in.at[source],
            comp_send.at[step],
            comp_recv.at[source],
            {"resp": source},
        ).wait_recv()

    def weight_parts(peer_rank, source):
        return (
            (gain_hbm.at[:, lanes_of(peer_rank)], gain_in.at[source]),
            (short_hbm.at[:, :, lanes_of(peer_rank)], short_in.at[source]),
            (taps_src.at[groups_of(peer_rank), :], taps_in.at[source]),
        )

    def weight_copy(kind, step):
        peer = lax.rem(me + step, sections)
        src, dst = weight_parts(me_resp * sections + peer, me)[kind]
        return remote(
            src, dst, weight_send.at[kind, step], weight_recv.at[kind, me], {"section": peer}
        )

    def weight_wait(kind, step):
        source = lax.rem(me + step, sections)
        src, dst = weight_parts(rank, source)[kind]
        remote(
            src,
            dst,
            weight_send.at[kind, step],
            weight_recv.at[kind, source],
            {"section": source},
        ).wait_recv()

    def pool_copy(step):
        peer = lax.rem(rank + step, ranks)
        return remote(
            prompt_hbm.at[:, lanes_of(peer)],
            pool.at[me, me_resp],
            pool_send.at[step],
            pool_recv.at[rank],
            place(peer),
        )

    def pool_wait(s):
        def each(r):
            source = r * sections + s

            @pl.when(source != rank)
            def _():
                remote(
                    prompt_hbm.at[:, lanes_of(rank)],
                    pool.at[s, r],
                    pool_send.at[0],
                    pool_recv.at[source],
                    place(source),
                ).wait_recv()

            @pl.when(source == rank)
            def _():
                own_pool.wait()

        loop(0, n_resp, each)

    def first_copy(step):
        peer = lax.rem(rank + step, ranks)
        return remote(
            first_out, first_in.at[rank], first_send.at[step], first_recv.at[rank], place(peer)
        )

    def first_wait(step):
        source = lax.rem(rank + step, ranks)
        remote(
            first_out,
            first_in.at[source],
            first_send.at[step],
            first_recv.at[source],
            place(source),
        ).wait_recv()

    peers = []
    for j in range(1, n_resp):
        hop = jnp.where(me_resp * 2 < n_resp, n_resp - j, j)
        peer_resp = lax.rem(me_resp + hop, n_resp)
        peers += [(lax.rem(me + k, sections), peer_resp) for k in range(sections)]
    peers += [(lax.rem(me + k, sections), me_resp) for k in range(1, sections)]

    def stat_start(slot, tile):
        stat_out[slot] = tile
        for peer, peer_resp in peers:
            remote(
                stat_out.at[slot],
                stat_in.at[slot, rank],
                stat_send.at[slot],
                stat_recv.at[slot],
                {"section": peer, "resp": peer_resp},
            ).start()
        stat_in[slot, rank] = tile

    def stat_wait(slot, sem):
        bulk = stat_in.at[slot, pl.ds(0, ranks - 1)]
        pltpu.make_async_copy(bulk, bulk, sem.at[slot]).wait()

    def stat_finish(slot):
        stat_wait(slot, stat_recv)
        return jnp.sum(stat_in[slot], axis=0)

    def tile_copy(s, step):
        return remote(
            tiles_own.at[s],
            tiles_all.at[rank],
            tile_send.at[s, step],
            tile_recv.at[rank],
            {"section": s, "resp": lax.rem(me_resp + step, n_resp)},
        )

    def tile_steps(s, action):
        def each(step):
            @pl.when(jnp.logical_not((s == me) & (step == 0)))
            def _():
                action(tile_copy(s, step))

        loop(0, n_resp, each)

    for copy in (load_taps, load_comp, load_prompt, load_head):
        copy.start()
    for copy in (own_comp, own_pool, own_gain, own_short):
        copy.start()
    barrier = pltpu.get_barrier_semaphore()
    loop(
        1,
        ranks,
        lambda step: pl.semaphore_signal(
            barrier,
            inc=1,
            device_id=place(lax.rem(rank + step, ranks)),
            device_id_type=MESH,
        ),
    )

    tile_row = lax.broadcasted_iota(jnp.int32, (LANES, LANES), 0)
    tile_lane = lax.broadcasted_iota(jnp.int32, (LANES, LANES), 1)
    row_target = (tile_row // per_group) * LANES + tile_row % per_group
    prompt_key = (tile_lane // (n_resp * per_group)) * (n_resp * per_group) + (
        tile_lane % per_group
    )

    def fill_order(c):
        rows = pl.ds(pl.multiple_of(c * LANES, LANES), LANES)
        for n in range(per_block):
            hit = row_target + c * per_group == tile_lane + n * LANES
            order_c[rows, n * LANES : (n + 1) * LANES] = jnp.where(hit, 1.0, 0.0).astype(BF16)

    loop(0, comps, fill_order)
    for m in range(micro):
        for n in range(per_block):
            hit = row_target + m * n_resp * per_group == prompt_key + n * LANES
            order_p[m * LANES : (m + 1) * LANES, n * LANES : (n + 1) * LANES] = jnp.where(
                hit, 1.0, 0.0
            ).astype(BF16)
    pad = 8
    for g in range(groups):
        normed_buf[g, :pad] = jnp.zeros((pad, LANES), F32)
        for s in range(sections):
            d_short_buf[s, g, total:] = jnp.zeros((pad, LANES), F32)

    load_taps.wait()
    upright = jnp.transpose(taps_full[...])
    mirror = jnp.where(lax.rem(tile_row + tile_lane, LANES) == 0, 1.0, 0.0)
    taps_src[:, :LANES] = jnp.dot(
        upright, mirror, preferred_element_type=F32, precision=lax.Precision.HIGHEST
    )
    taps_src[:, LANES:] = upright

    ones = jnp.ones((16, 2 * LANES), BF16)

    def split(values):
        high = values.astype(BF16)
        return high, (values - high.astype(F32)).astype(BF16)

    def lane_sums(acc, weights, below=None):
        if acc.shape[0] < LANES:
            rest = [] if below is None else [below]
            rows = LANES - acc.shape[0] - sum(block.shape[0] for block in rest)
            acc = jnp.concatenate([acc] + rest + [jnp.zeros((rows, LANES), F32)], axis=0)
        both = jnp.concatenate(split(acc), axis=1)
        return lax.dot_general(
            weights, both, (((1,), (1,)), ((), ())), preferred_element_type=F32
        )[:8]

    def square_rows(ref):
        def step(block, acc):
            values = ref[:, pl.ds(pl.multiple_of(block * LANES, LANES), LANES)].astype(F32)
            return acc + values * values

        return lax.fori_loop(
            0, width // LANES, step, jnp.zeros((ref.shape[0], LANES), F32), unroll=2
        )

    load_comp.wait()
    comp_line = lane_sums(square_rows(comp_full), ones)
    load_prompt.wait()
    prompt_line = lane_sums(square_rows(prompt_full), ones)
    eight_row = lax.broadcasted_iota(jnp.int32, (8, LANES), 0)
    eight_lane = lax.broadcasted_iota(jnp.int32, (8, LANES), 1)
    message = jnp.where(eight_row == 0, comp_line, prompt_line)
    for m in range(micro):
        count = jnp.full((8, LANES), length_ref[0, m], jnp.int32).astype(F32)
        message = jnp.where(eight_row == 2 + m, count, message)
    first_out[...] = message

    pl.semaphore_wait(barrier, ranks - 1)
    loop(1, n_resp, lambda step: comp_copy(step).start())
    loop(1, sections, lambda step: weight_copy(2, step).start())

    def start_pools(second):
        @pl.when(lax.rem(me, 2) == second)
        def _():
            loop(1, ranks, lambda step: pool_copy(step).start())

    loop(1, ranks, lambda step: first_copy(step).start())
    start_pools(0)

    def start_vectors(step):
        weight_copy(0, step).start()
        weight_copy(1, step).start()

    loop(1, sections, start_vectors)
    first_in[rank] = message
    taps_in[me] = taps_src[groups_of(rank), :]

    own_gain.wait()
    own_short.wait()
    load_head.wait()

    def weights_arrive(step):
        for kind in range(3):
            weight_wait(kind, step)

    loop(1, sections, weights_arrive)

    def tile_lanes(values, n):
        out = pltpu.roll(values, (LANES - n * per_group) % LANES, 1)
        out = jnp.where(eight_lane < per_group, out, 0.0)
        span = per_group
        while span < LANES:
            out = out + pltpu.roll(out, span, 1)
            span *= 2
        return out

    t_row = lax.broadcasted_iota(jnp.int32, (length, LANES), 0)
    s_lane = lax.broadcasted_iota(jnp.int32, (length, LANES), 1)
    keep = s_lane <= length + t_row
    keep_t = tile_row <= length + tile_lane

    def spread_params(s):
        for b in range(blocks):
            lanes = slice(b * LANES, (b + 1) * LANES)
            rows = jnp.concatenate(
                [gain_in[s, :, lanes]] + [short_in[s, j, :, lanes] for j in range(tap_count)],
                axis=0,
            )
            for n in range(per_block):
                params[s, b * per_block + n] = tile_lanes(rows, n)

    loop(0, sections, spread_params)
    for b in range(blocks):
        rows = jnp.broadcast_to(head_own[:, b * LANES : (b + 1) * LANES], (8, LANES))
        for n in range(per_block):
            heads[b * per_block + n] = tile_lanes(rows, n)

    def build(index, k):
        s, g = index // groups, lax.rem(index, groups)
        line = taps_in[s, pl.ds(g, 1), :]
        wide = jnp.broadcast_to(line[:, :LANES], (length, LANES))
        wide = pltpu.roll(wide, length, 1, stride=1, stride_axis=0)
        wide_t = jnp.broadcast_to(line[:, LANES:], (total, LANES))
        wide_t = pltpu.roll(wide_t, length, 1, stride=1, stride_axis=0)
        yield
        wide = jnp.where(keep, wide, 0.0)
        high = wide.astype(BF16).astype(F32)
        low = wide - high
        low_turned = pltpu.roll(low, length, 1)
        high_turned = pltpu.roll(high, length, 1)
        toep_t[s, g] = jnp.where(keep_t, wide_t, 0.0).astype(BF16)
        yield
        first = s_lane < length
        toep_p[s, g] = jnp.where(first, high, low_turned).astype(BF16)
        toep[s, g] = jnp.where(first, high_turned, low).astype(BF16)

    lockstep(0, sections * groups, 4, build)

    def spread_rows(lines):
        tall = jnp.concatenate(
            [jnp.broadcast_to(lines[c : c + 1], (per_group, LANES)) for c in range(comps)],
            axis=0,
        )
        return jnp.transpose(tall)[:length]

    def to_factor(sums):
        return lax.rsqrt(sums * (1.0 / width) + 1e-06)

    loop(1, ranks, first_wait)
    own_lines = jnp.concatenate(
        [first_in[r * sections + me, 0:1] for r in range(n_resp)], axis=0
    )
    own_lines = jnp.concatenate(
        [
            own_lines if m == 0 else pltpu.roll(own_lines, LANES - m * length, 1)
            for m in range(micro)
        ],
        axis=0,
    )
    fac_c[0] = spread_rows(to_factor(own_lines))

    def prompt_factor(s):
        lines = []
        for m in range(micro):
            owner = jnp.full((8, LANES), owner_ref[m], jnp.int32)
            line = jnp.zeros((8, LANES), F32)
            for r in range(n_resp):
                line = jnp.where(owner == r, first_in[r * sections + s], line)
            lines += [line[1:2]] * n_resp
        fac_p[s] = spread_rows(to_factor(jnp.concatenate(lines, axis=0)))

    loop(0, sections, prompt_factor)

    def conv_short(ref, g, start, taps):
        out = ref[g, pl.ds(start, length)] * taps[1:2]
        for j in range(1, tap_count):
            out = out + ref[g, pl.ds(start - j, length)] * taps[1 + j : 2 + j]
        return out

    def conv_long(matrix, high, low):
        left = jnp.concatenate([matrix, matrix], axis=1)
        right = jnp.concatenate([high, high, low, low], axis=0)
        return jnp.dot(left, right, preferred_element_type=F32)

    def prepare(s):
        pool_wait(s)

        @pl.when(s == 0)
        def _():
            start_pools(1)

        sides = []
        for b in range(blocks):
            lanes = slice(b * LANES, (b + 1) * LANES)
            row = []
            for m in range(micro):
                owner = jnp.full((length, LANES), owner_ref[m], jnp.int32)
                picked = pool[s, 0, :, lanes].astype(F32)
                for r in range(1, n_resp):
                    picked = jnp.where(owner == r, pool[s, r, :, lanes].astype(F32), picked)
                row.append(picked.astype(BF16))
            sides.append(jnp.concatenate(row, axis=1))
        side = jnp.concatenate(sides, axis=0)
        step = 2 * LANES
        for n in range(per_block // 2):
            part = jnp.dot(
                side, order_p[:, n * step : (n + 1) * step], preferred_element_type=F32
            ).astype(BF16)
            for b in range(blocks):
                for k in range(2):
                    prompt_rows[s, b * per_block + 2 * n + k] = part[
                        b * length : (b + 1) * length, k * LANES : (k + 1) * LANES
                    ]
        factor = fac_p[s]

        def each(g, k):
            taps = params[s, g]
            normed = prompt_rows[s, g].astype(F32) * factor * taps[0:1]
            normed_buf[g, pl.ds(pad, length)] = normed
            yield
            shorter = conv_short(normed_buf, g, pad, taps)
            high, low = split(shorter)
            short_out[s, g, :length] = high
            yield
            longer = conv_long(toep_p[s, g], high, low)
            yield
            long_out[s, g] = longer

        lockstep(0, groups, SIDE, each)

    loop(1, n_resp, comp_wait)
    own_comp.wait()
    for b in range(blocks):
        lanes = slice(b * LANES, (b + 1) * LANES)
        for m in range(micro):
            for r in range(n_resp):
                c = m * n_resp + r
                lined[b * length : (b + 1) * length, c * LANES : (c + 1) * LANES] = comp_in[
                    r, m * length : (m + 1) * length, lanes
                ]
    for n in range(per_block // 2):
        step = 2 * LANES
        part = jnp.dot(
            lined[...], order_c[:, n * step : (n + 1) * step], preferred_element_type=F32
        ).astype(BF16)
        for b in range(blocks):
            for k in range(2):
                rows_in[0, b * per_block + 2 * n + k] = part[
                    b * length : (b + 1) * length, k * LANES : (k + 1) * LANES
                ]
    prepare(0)

    fold_row = lax.broadcasted_iota(jnp.int32, (16, 2 * LANES), 0)
    fold_lane = lax.broadcasted_iota(jnp.int32, (16, 2 * LANES), 1)
    fold = jnp.where((fold_lane % LANES) // per_group == fold_row, 1.0, 0.0).astype(BF16)

    def forward(s, last):
        acc_ref[...] = jnp.zeros_like(acc_ref)
        factor = fac_c[s]

        sums = []

        def each(g, k):
            taps = params[s, g]
            rows = rows_in[s, g].astype(F32)
            normed = rows * factor * taps[0:1]
            normed_buf[g, pl.ds(pad + length, length)] = normed
            yield
            shorter = conv_short(normed_buf, g, pad + length, taps)
            high, low = split(shorter)
            short_out[s, g, length:] = high
            yield
            longer = conv_long(toep[s, g], high, low)
            yield
            longer = long_out[s, g] + longer
            normed = normed_buf[g, pl.ds(pad + length, length)]
            mixed = (rows_in[s, g].astype(F32) + normed * longer).astype(BF16)
            sums.append((longer, mixed))
            yield
            longer, mixed = sums[k]
            long_out[s, g] = longer
            if not last:
                rows_in[s + 1, g] = mixed
            mixed = mixed.astype(F32)
            sums[k] = mixed * (heads[g, 0:1] if last else mixed)
            yield
            if k == SIDE - 1:
                acc_ref[...] += add_up(sums)
                sums.clear()

        lockstep(0, groups, SIDE, each)

    def forward_step(s):
        forward(s, False)
        stat_start(s, lane_sums(acc_ref[...], fold))
        prepare(s + 1)
        fac_c[s + 1] = spread_rows(to_factor(stat_finish(s)))

    loop(0, sections - 1, forward_step)
    forward(sections - 1, True)

    comp_lane = eight_lane // per_group
    counts = jnp.zeros((8, LANES), F32)
    for m in range(micro):
        for r in range(n_resp):
            row = first_in[r * sections + me, 2 + m : 3 + m]
            counts = jnp.where(comp_lane == m * n_resp + r, row, counts)
    alive = t_row.astype(F32) < counts[0:1]
    live = jnp.where(alive, 1.0, 0.0) / jnp.sqrt(counts[0:1])
    score_line = jnp.sum(acc_ref[...] * live, axis=0, keepdims=True)
    score_line = jnp.where(eight_row == 0, score_line, 0.0)

    def seed(g, k):
        upstream[sections - 1, g] = live * heads[g, 0:1]
        yield

    lockstep(0, groups, SIDE, seed)

    def backward(s, last):
        acc_ref[...] = jnp.zeros_like(acc_ref)
        factor = fac_c[s]

        sums = []

        def each(g, k):
            taps = params[s, g]
            rows = rows_in[s, g].astype(F32)
            d_long = (upstream[s, g] * (rows * factor * taps[0:1])).astype(BF16)
            yield
            d_long_buf[s, g] = d_long
            d_short = jnp.dot(
                toep_t[s, g][:, :length], d_long, preferred_element_type=F32
            )
            yield
            d_short_buf[s, g, pl.ds(0, total)] = d_short
            if last:
                return
            yield
            d_normed = upstream[s, g] * long_out[s, g]
            for j in range(tap_count):
                d_normed = d_normed + d_short_buf[s, g, pl.ds(length + j, length)] * taps[1 + j : 2 + j]
            inner = d_normed * taps[0:1]
            sums.append(inner)
            yield
            inner_buf[g] = sums[k]
            sums[k] = sums[k] * rows_in[s, g].astype(F32)
            yield
            if k == SIDE - 1:
                acc_ref[...] += add_up(sums)
                sums.clear()

        lockstep(0, groups, SIDE, each)

    keep_pair = total - 1 - s_lane <= length + t_row
    reverse = jnp.where(tile_row + tile_lane == total - 1, 1.0, 0.0).astype(BF16)

    def gradients(s):
        factor_c = fac_c[s]
        factor_p = fac_p[s]
        scale = scales[s, 0:1]
        tops, longs = [], []

        def each(g, k):
            turned = jnp.dot(reverse, short_out[s, g], preferred_element_type=F32)
            yield
            pairs = lax.dot_general(
                (d_long_buf[s, g].astype(F32) * scale).astype(BF16),
                turned.astype(BF16),
                (((1,), (1,)), ((), ())),
                preferred_element_type=F32,
            )
            yield
            taps = params[s, g]
            scaled_p = prompt_rows[s, g].astype(F32) * factor_p
            scaled_c = rows_in[s, g].astype(F32) * factor_c
            lines = [
                jnp.sum(upstream[s, g] * long_out[s, g] * scaled_c, axis=0, keepdims=True)
            ]
            for j in range(tap_count):
                part = (
                    d_short_buf[s, g, pl.ds(j, length)] * scaled_p
                    + d_short_buf[s, g, pl.ds(length + j, length)] * scaled_c
                )
                lines.append(jnp.sum(part, axis=0, keepdims=True))
            tile = jnp.concatenate(lines, axis=0) * scale
            yield
            pairs = jnp.where(keep_pair, pairs, 0.0)
            pairs = pltpu.roll(pairs, LANES + 1 - length, 1, stride=1, stride_axis=0)
            yield
            span = per_group
            while span < LANES:
                tile = tile + pltpu.roll(tile, span, 1)
                span *= 2
            yield
            top = tile + jnp.sum(
                jnp.where(eight_row > 0, tile * taps, 0.0), axis=0, keepdims=True
            )
            tops.append(jnp.where(eight_row == 0, top, tile * taps[0:1]))
            longs.append(jnp.sum(pairs, axis=0, keepdims=True))
            yield
            if k < SIDE - 1:
                return
            b, n = g // per_block, lax.rem(g, per_block)
            tile = tiles_own[s, b]
            for i in range(SIDE):
                tile = jnp.where(comp_lane == n - (SIDE - 1) + i, tops[i], tile)
            tiles_own[s, b] = tile
            for i in range(SIDE):
                row = lax.rem(g, 8) - (SIDE - 1) + i
                tiles_own[s, blocks + g // 8, pl.ds(row, 1)] = longs[i]
            tops.clear()
            longs.clear()

        for b in range(blocks):
            tiles_own[s, b] = jnp.zeros((8, LANES), F32)
        lockstep(0, groups, SIDE, each)

        @pl.when(s == me)
        def _():
            tiles_all[rank] = tiles_own[s]

        tile_steps(s, lambda copy: copy.start())

    def go_down(s, sums, scale):
        factor = fac_c[s]
        pull = spread_rows(sums * (1.0 / width)) * factor * factor * factor

        def finish(g, k):
            grad = upstream[s, g] + factor * inner_buf[g] - rows_in[s, g].astype(F32) * pull
            yield
            if scale is not None:
                grad = grad * scale
            upstream[s - 1, g] = grad.astype(BF16).astype(F32)

        lockstep(0, groups, SIDE, finish)

    last = sections - 1
    backward(last, False)
    stat_start(last, lane_sums(acc_ref[...], fold, score_line))
    loop(1, n_resp, lambda step: comp_copy(step).wait_send())

    def weights_sent(step):
        for kind in range(3):
            weight_copy(kind, step).wait_send()

    loop(1, sections, weights_sent)

    def ranks_sent(step):
        pool_copy(step).wait_send()
        first_copy(step).wait_send()

    loop(1, ranks, ranks_sent)
    winner = jnp.full((8, LANES), -1, jnp.int32)
    loser = winner
    for m in range(micro):
        for p in range(pair_ref.shape[2]):
            here = (eight_row == m) & (eight_lane == p)
            winner = jnp.where(here, pair_ref[m, 0, p], winner)
            loser = jnp.where(here, pair_ref[m, 1, p], loser)
    signs = [
        jnp.where(winner == r, 1.0, 0.0) - jnp.where(loser == r, 1.0, 0.0)
        for r in range(n_resp)
    ]
    masks = [comp_lane == eight_row * n_resp + r for r in range(n_resp)]
    sums = stat_finish(last)
    totals = jnp.sum(jnp.where(eight_lane == length, sums, 0.0), axis=1, keepdims=True)
    totals = jnp.broadcast_to(totals, (8, LANES))
    scores = []
    for r in range(n_resp):
        rows = totals[r : r + 1]
        for m in range(1, micro):
            rows = jnp.where(eight_row == m, totals[m * n_resp + r : m * n_resp + r + 1], rows)
        scores.append(jnp.broadcast_to(rows, (8, LANES)))
    own_score = scores[0]
    margin = jnp.zeros((8, LANES), F32)
    for r in range(n_resp):
        margin = margin + scores[r] * signs[r]
        own_score = jnp.where(me_resp == r, scores[r], own_score)
    score_ref[...] = own_score[:micro, :1].astype(BF16)
    weight = 1.0 / (1.0 + jnp.exp(margin))
    slopes = jnp.zeros((8, LANES), F32)
    for r in range(n_resp):
        slope = -jnp.sum(signs[r] * weight, axis=1, keepdims=True)
        slopes = jnp.where(masks[r], slope, slopes)
    slopes = jnp.sum(slopes, axis=0, keepdims=True)
    for s in range(sections - 1):
        scales[s] = jnp.ones((8, LANES), F32)
    scales[last] = jnp.broadcast_to(slopes, (8, LANES))
    go_down(last, sums, slopes)

    def backward_step(step):
        s = sections - 1 - step
        slot = last + step
        backward(s, False)
        stat_start(slot, lane_sums(acc_ref[...], fold))
        loop(s, jnp.where(step == 1, s + 2, s + 1), gradients)
        go_down(s, stat_finish(slot), None)

    loop(1, sections - 1, backward_step)
    backward(0, True)
    gradients(0)

    loop(0, 2 * sections - 2, lambda slot: stat_wait(slot, stat_send))
    loop(0, sections, lambda s: tile_steps(s, lambda copy: copy.wait_send()))

    def arrive(step):
        source = lax.rem(rank + step, ranks)
        remote(
            tiles_own.at[0],
            tiles_all.at[source],
            tile_send.at[0, 0],
            tile_recv.at[source],
            place(source),
        ).wait_recv()

    loop(1, ranks, arrive)
    lines = []
    for q in range(ranks):
        for b in range(blocks):
            lanes = slice((q * blocks + b) * LANES, (q * blocks + b + 1) * LANES)
            tile = tiles_all[q, b]
            gain_out[:, lanes] = tile[0:1]
            for j in range(tap_count):
                taps_short_out[j, :, lanes] = tile[1 + j : 2 + j]
        lines += [tiles_all[q, blocks + k] for k in range(groups // 8)]
    taps_long_out[...] = jnp.transpose(jnp.concatenate(lines, axis=0))


def flush_kernel(*refs):
    for source, target in zip(refs, refs[len(refs) // 2 :]):
        target[...] = source[...]


def flush(*arrays):
    vmem = pl.BlockSpec(memory_space=pltpu.VMEM)
    return pl.pallas_call(
        flush_kernel,
        out_shape=tuple(jax.ShapeDtypeStruct(array.shape, array.dtype) for array in arrays),
        in_specs=[vmem] * len(arrays),
        out_specs=(vmem,) * len(arrays),
    )(*arrays)


def run_wide(dims, *arrays):
    sections, n_resp, micro, length, chans, per_group, width = dims
    comps = micro * n_resp
    ranks = sections * n_resp
    groups = chans // per_group
    blocks = chans // LANES
    total = 2 * length
    tap_count = arrays[3].shape[0]
    group_all = width // per_group
    tile = (8, LANES)
    tiles = blocks + groups // 8
    vmem = pl.BlockSpec(memory_space=pltpu.VMEM)
    hbm = pl.BlockSpec(memory_space=pl.ANY)
    smem = pl.BlockSpec(memory_space=pltpu.SMEM)
    slots = 2 * sections - 2
    per = (sections, groups)
    dma = pltpu.SemaphoreType.DMA
    return pl.pallas_call(
        functools.partial(wide_kernel, dims),
        out_shape=(
            jax.ShapeDtypeStruct((micro, 1), BF16),
            jax.ShapeDtypeStruct((1, width), F32),
            jax.ShapeDtypeStruct((tap_count, 1, width), F32),
            jax.ShapeDtypeStruct((LANES, group_all), F32),
        ),
        in_specs=[hbm] * 6 + [smem] * 3,
        out_specs=(vmem,) * 4,
        scratch_shapes=[
            pltpu.VMEM((micro * length, width), BF16),
            pltpu.VMEM((length, width), BF16),
            pltpu.VMEM((LANES, group_all), F32),
            pltpu.VMEM((1, chans), F32),
            pltpu.VMEM((n_resp, micro * length, chans), BF16),
            pltpu.VMEM((sections, n_resp, length, chans), BF16),
            pltpu.VMEM((sections, 1, chans), F32),
            pltpu.VMEM((sections, tap_count, 1, chans), F32),
            pltpu.VMEM((group_all, 2 * LANES), F32),
            pltpu.VMEM((sections, groups, 2 * LANES), F32),
            pltpu.VMEM((comps * LANES, (LANES // per_group) * LANES), BF16),
            pltpu.VMEM((micro * LANES, (LANES // per_group) * LANES), BF16),
            pltpu.VMEM((blocks * length, comps * LANES), BF16),
            pltpu.VMEM(tile, F32),
            pltpu.VMEM((ranks,) + tile, F32),
            pltpu.VMEM((slots,) + tile, F32),
            pltpu.VMEM((slots, ranks) + tile, F32),
            pltpu.VMEM(per + (length, LANES), BF16),
            pltpu.VMEM(per + (length, LANES), BF16),
            pltpu.VMEM(per + (length, LANES), F32),
            pltpu.VMEM(per + (total, LANES), BF16),
            pltpu.VMEM(per + (length, LANES), BF16),
            pltpu.VMEM(per + (length, LANES), BF16),
            pltpu.VMEM(per + (total, LANES), BF16),
            pltpu.VMEM(per + tile, F32),
            pltpu.VMEM((groups,) + tile, F32),
            pltpu.VMEM((sections, length, LANES), F32),
            pltpu.VMEM((sections, length, LANES), F32),
            pltpu.VMEM((groups, 8 + total, LANES), F32),
            pltpu.VMEM(per + (total + 8, LANES), F32),
            pltpu.VMEM(per + (length, LANES), F32),
            pltpu.VMEM((groups, length, LANES), F32),
            pltpu.VMEM(per + (length, LANES), BF16),
            pltpu.VMEM((length, LANES), F32),
            pltpu.VMEM((sections,) + tile, F32),
            pltpu.VMEM((sections, tiles) + tile, F32),
            pltpu.VMEM((ranks, tiles) + tile, F32),
            dma((8,)),
            dma((n_resp,)),
            dma((n_resp,)),
            dma((3, sections)),
            dma((3, sections)),
            dma((ranks,)),
            dma((ranks,)),
            dma((ranks,)),
            dma((ranks,)),
            dma((slots,)),
            dma((slots,)),
            dma((sections, n_resp)),
            dma((ranks,)),
        ],
        compiler_params=pltpu.CompilerParams(
            collective_id=1, has_side_effects=True, vmem_limit_bytes=56 * 1024 * 1024
        ),
    )(*arrays)


def wide_body(
    completion_rows,
    prompt_pool,
    norm_gain,
    short_taps,
    long_taps,
    score_head,
    live_lengths,
    prompt_owner,
    pair_index,
):
    sections = lax.axis_size("section")
    n_resp = lax.axis_size("resp")
    micro, _, length, width = completion_rows.shape
    chans = width // (sections * n_resp)
    per_group = width // long_taps.shape[2]
    results = run_wide(
        (sections, n_resp, micro, length, chans, per_group, width),
        completion_rows.reshape(micro * length, width),
        prompt_pool[0, 0],
        norm_gain,
        short_taps.transpose(1, 0, 2),
        long_taps[0],
        score_head[None],
        prompt_owner,
        pair_index.transpose(0, 2, 1),
        live_lengths.T,
    )
    scores, gain_grad, short_grad, long_grad = flush(*results)
    return (
        scores,
        gain_grad,
        short_grad.transpose(1, 0, 2),
        long_grad[None],
    )


def is_wide(
    completion_rows,
    prompt_pool,
    norm_gain,
    short_taps,
    long_taps,
    score_head,
    live_lengths,
    prompt_owner,
    pair_index,
):
    sections = lax.axis_size("section")
    n_resp = lax.axis_size("resp")
    micro, _, length, width = completion_rows.shape
    per_group = width // long_taps.shape[2]
    return (
        micro * n_resp * per_group == LANES
        and micro * n_resp == 8
        and width % (sections * n_resp * LANES) == 0
        and prompt_pool.shape[2] == length
        and long_taps.shape[1] == 2 * length == LANES
        and micro * length == LANES
        and short_taps.shape[1] == 7
        and sections >= 3
    )


def either(*arrays):
    return wide_body(*arrays) if is_wide(*arrays) else body(*arrays)


def solution(mesh):
    placed = (
        P(None, ("groups", "resp"), None, None),
        P("section", ("groups", "resp"), None, None),
        P("section", None),
        P("section", None, None),
        P("section", None, None),
        P(),
        P(None, ("groups", "resp")),
        P("groups"),
        P(None, "groups", None),
    )
    return jax.shard_map(
        either,
        mesh=mesh,
        in_specs=placed,
        out_specs=(
            P(None, ("groups", "resp")),
            P("section", "groups"),
            P("section", "groups", None),
            P("section", "groups", None),
        ),
        check_vma=False,
    )
```

```python
import functools

import jax
import jax.numpy as jnp
from jax import lax
from jax.experimental import pallas as pl
from jax.experimental.pallas import tpu as pltpu
from jax.sharding import PartitionSpec as P

LANES = 128
MESH = pl.DeviceIdType.MESH
F32 = jnp.float32
BF16 = jnp.bfloat16


def rows_to_line(block):
    line = jnp.sum(jnp.transpose(block), axis=0, keepdims=True)
    return jnp.broadcast_to(line, (8, LANES))


def line_to_rows(tile):
    return jnp.transpose(jnp.broadcast_to(tile[0:1], (LANES, LANES)))


def kernel(
    dims,
    direct,
    comp_ref,
    prompt_ref,
    gain_hbm,
    short_hbm,
    taps_hbm,
    owner_ref,
    head_ref,
    ends_ref,
    length_ref,
    score_ref,
    *rest,
):
    sections, n_resp, micro, length, prompt_len, chans, per_group, width = dims
    outs, rest = (rest[:3], rest[3:]) if direct else (rest[:1], rest[1:])
    (
        toep,
        toep_t,
        pool,
        chosen_rows,
        gain_ref,
        short_ref,
        taps_ref,
        rows_in,
        short_out,
        long_out,
        fac_p,
        fac_c,
        upstream,
        partial,
        stat_acc,
        score_acc,
        prompt_acc,
        stat_out,
        stat_in,
        resp_out,
        resp_in,
        tiles_own,
        tiles_in,
        tiles_sum,
        tiles_all,
        local_sem,
        weight_sems,
        spread_sems,
        pool_sems,
        stat_sems,
        resp_sems,
        part_sems,
        tile_send,
        tile_recv,
    ) = rest
    groups = LANES // per_group
    blocks = chans // LANES
    group_rows = blocks * groups
    total = prompt_len + length
    me = lax.axis_index("section")
    me_resp = lax.axis_index("resp")
    own_lanes = pl.ds(pl.multiple_of(me * chans, chans), chans)

    def lane_slice(block):
        return pl.ds(pl.multiple_of(block * LANES, LANES), LANES)

    def head_slice(block):
        return pl.ds(pl.multiple_of(me * chans + block * LANES, LANES), LANES)

    def wide_slice(block):
        return pl.ds(pl.multiple_of(block * micro * LANES, LANES), micro * LANES)

    def loop(low, high, step_of):
        def run(index, carry):
            step_of(index)
            return carry

        lax.fori_loop(low, high, run, 0)

    def swap(axis, count, mine, out_ref, in_ref, sems):
        def copy(step):
            return pltpu.make_async_remote_copy(
                src_ref=out_ref,
                dst_ref=in_ref.at[mine],
                send_sem=sems.at[0, step],
                recv_sem=sems.at[1, step],
                device_id={axis: lax.rem(mine + step, count)},
                device_id_type=MESH,
            )

        loop(1, count, lambda step: copy(step).start())
        in_ref[mine] = out_ref[...]
        return lambda: loop(1, count, lambda step: copy(step).wait())

    def start_stats(slot, first, second):
        stat_out[slot, 0] = first
        stat_out[slot, 1] = second
        wait = swap(
            "section", sections, me, stat_out.at[slot], stat_in.at[slot], stat_sems.at[slot]
        )

        def finish():
            wait()
            return jnp.sum(stat_in[slot], axis=0)

        return finish

    def weight_copies(step):
        peer = lax.rem(me + step, sections)
        lanes = pl.ds(pl.multiple_of(peer * chans, chans), chans)
        rows = pl.ds(pl.multiple_of(peer * group_rows, group_rows), group_rows)
        return [
            pltpu.make_async_remote_copy(
                src_ref=source,
                dst_ref=target,
                send_sem=weight_sems.at[0, kind, step],
                recv_sem=weight_sems.at[1, kind, step],
                device_id={"section": peer},
                device_id_type=MESH,
            )
            for kind, source, target in (
                (0, gain_hbm.at[:, lanes], gain_ref.at[me]),
                (2, short_hbm.at[:, lanes], short_ref.at[me]),
                (1, taps_hbm.at[rows, :], taps_ref.at[me]),
            )
        ]

    def start_weights(step):
        for copy in weight_copies(step):
            copy.start()

    def wait_weights(step):
        for copy in weight_copies(step):
            copy.wait()

    own_rows = pl.ds(pl.multiple_of(me * group_rows, group_rows), group_rows)
    local_copies = [
        pltpu.make_async_copy(comp_ref.at[:, own_lanes], rows_in.at[0], local_sem.at[0]),
        pltpu.make_async_copy(gain_hbm.at[:, own_lanes], gain_ref.at[me], local_sem.at[1]),
        pltpu.make_async_copy(short_hbm.at[:, own_lanes], short_ref.at[me], local_sem.at[3]),
        pltpu.make_async_copy(taps_hbm.at[own_rows, :], taps_ref.at[me], local_sem.at[2]),
    ]

    def spread_copy(step):
        peer = lax.rem(me + step, sections)
        lanes = pl.ds(pl.multiple_of(peer * chans, chans), chans)
        return pltpu.make_async_remote_copy(
            src_ref=prompt_ref.at[:, lanes],
            dst_ref=pool.at[me, me_resp],
            send_sem=spread_sems.at[0, step],
            recv_sem=spread_sems.at[1, step],
            device_id={"section": peer},
            device_id_type=MESH,
        )

    def pool_copy(s, step):
        return pltpu.make_async_remote_copy(
            src_ref=pool.at[s, me_resp],
            dst_ref=pool.at[s, me_resp],
            send_sem=pool_sems.at[0, s, step],
            recv_sem=pool_sems.at[1, s, step],
            device_id={"resp": lax.rem(me_resp + step, n_resp)},
            device_id_type=MESH,
        )

    def own_pool():
        return pltpu.make_async_copy(
            prompt_ref.at[:, own_lanes], pool.at[me, me_resp], local_sem.at[4]
        )

    def start_pool(s):
        step = lax.rem(me - s + sections, sections)

        @pl.when(step == 0)
        def _():
            own_pool().wait()

        @pl.when(step > 0)
        def _():
            spread_copy(step).wait()

        loop(1, n_resp, lambda d: pool_copy(s, d).start())

    def wait_pool(s):
        loop(1, n_resp, lambda d: pool_copy(s, d).wait())

    if direct:
        own_pool().start()
        loop(1, sections, lambda step: spread_copy(step).start())
    for copy in local_copies:
        copy.start()
    loop(1, sections, start_weights)
    if direct:
        start_pool(0)
    for copy in local_copies:
        copy.wait()

    def first_stats(block):
        wide = rows_in[0, :, lane_slice(block)].astype(F32)
        stat_acc[...] += wide * wide

    stat_acc[...] = jnp.zeros_like(stat_acc)
    loop(0, blocks, first_stats)
    loop(1, sections, wait_weights)

    t_row = lax.broadcasted_iota(jnp.int32, (length, LANES), 0)
    s_lane = lax.broadcasted_iota(jnp.int32, (length, LANES), 1)
    keep = s_lane <= prompt_len + t_row
    s_row = lax.broadcasted_iota(jnp.int32, (total, LANES), 0)
    t_lane = lax.broadcasted_iota(jnp.int32, (total, LANES), 1)
    keep_t = s_row <= prompt_len + t_lane

    def build(s, block):
        rows = pl.ds(pl.multiple_of(block * groups, groups), groups)
        both = taps_ref[s, rows, :]
        flipped, plain = both[:, :LANES], both[:, LANES:]
        for g in range(groups):
            base = pl.multiple_of((block * groups + g) * length, length)
            wide = jnp.broadcast_to(flipped[g : g + 1], (length, LANES))
            wide = pltpu.roll(wide, prompt_len, 1, stride=1, stride_axis=0)
            wide = jnp.where(keep, wide, 0.0)
            high = wide.astype(BF16)
            low = (wide - high.astype(F32)).astype(BF16)
            toep[s, pl.ds(base, length), :] = jnp.concatenate([high, high, low], axis=1)
            base = pl.multiple_of((block * groups + g) * total, total)
            wide = jnp.broadcast_to(plain[g : g + 1], (total, LANES))
            wide = pltpu.roll(wide, prompt_len, 1, stride=1, stride_axis=0)
            toep_t[s, pl.ds(base, total), :] = jnp.where(keep_t, wide, 0.0).astype(BF16)

    def choose(s, block):
        lanes = lane_slice(block)
        for m in range(micro):
            rows = slice(m * prompt_len, (m + 1) * prompt_len)
            if direct:
                picked = jnp.zeros((prompt_len, LANES), F32)
                for r in range(n_resp):
                    flag = jnp.full((prompt_len, LANES), owner_ref[m], jnp.int32) == r
                    picked = jnp.where(flag, pool[s, r, :, lanes].astype(F32), picked)
                chosen_rows[s, rows, lanes] = picked.astype(BF16)
            else:
                picked = prompt_ref[s, rows, lanes].astype(F32)
                chosen_rows[s, rows, lanes] = prompt_ref[s, rows, lanes]
            prompt_acc[rows, :] += picked * picked

    row_id = lax.broadcasted_iota(jnp.int32, (total, LANES), 0)
    wide_group = (
        lax.broadcasted_iota(jnp.int32, (1, micro * LANES), 1) % LANES
    ) // per_group
    tap_count = short_ref.shape[1]

    def pick(stacked, rows):
        out = stacked[0:rows]
        for g in range(1, groups):
            out = jnp.where(wide_group == g, stacked[g * rows : (g + 1) * rows], out)
        return out

    def joined_rows(s, m, lanes):
        rows_p = slice(m * prompt_len, (m + 1) * prompt_len)
        rows_c = slice(m * length, (m + 1) * length)
        joined = jnp.concatenate(
            [chosen_rows[s, rows_p, lanes].astype(F32), rows_in[s, rows_c, lanes].astype(F32)],
            axis=0,
        )
        factor = jnp.concatenate([fac_p[s, rows_p, :], fac_c[s, rows_c, :]], axis=0)
        return joined, factor

    def forward(s, carry):
        if direct:
            wait_pool(s)

            @pl.when(s + 1 < sections)
            def _():
                start_pool(s + 1)

        prompt_acc[...] = jnp.zeros_like(prompt_acc)
        loop(0, blocks, lambda block: choose(s, block))
        finish = start_stats(s, rows_to_line(stat_acc[...]), rows_to_line(prompt_acc[...]))
        loop(0, blocks, lambda block: build(s, block))
        sums = finish()
        fac_c[s] = lax.rsqrt(line_to_rows(sums[0]) * (1.0 / width) + 1e-06)
        fac_p[s] = lax.rsqrt(line_to_rows(sums[1]) * (1.0 / width) + 1e-06)
        stat_acc[...] = jnp.zeros_like(stat_acc)
        score_acc[...] = jnp.zeros_like(score_acc)

        def run(block, carry):
            lanes = lane_slice(block)
            wide = wide_slice(block)
            gain = gain_ref[s, :, lanes]
            short = short_ref[s, :, lanes]
            parts, lows, saved = [], [], []
            for m in range(micro):
                joined, factor = joined_rows(s, m, lanes)
                normed = joined * factor * gain
                shorter = normed * short[0:1]
                for j in range(1, tap_count):
                    moved = jnp.where(row_id >= j, pltpu.roll(normed, j, 0), 0.0)
                    shorter = shorter + moved * short[j : j + 1]
                high = shorter.astype(BF16)
                parts.append(high)
                lows.append((shorter - high.astype(F32)).astype(BF16))
                saved.append((joined[prompt_len:], normed[prompt_len:]))
            high = jnp.concatenate(parts, axis=1)
            short_out[s, :, wide] = high
            rhs = jnp.concatenate([high, jnp.concatenate(lows, axis=1), high], axis=0)
            base = pl.multiple_of(block * groups * length, groups * length)
            stacked = jnp.dot(
                toep[s, pl.ds(base, groups * length), :], rhs, preferred_element_type=F32
            )
            longer_all = pick(stacked, length)
            for m in range(micro):
                rows = slice(m * length, (m + 1) * length)
                longer = longer_all[:, m * LANES : (m + 1) * LANES]
                long_out[s, rows, lanes] = longer
                mixed = (saved[m][0] + saved[m][1] * longer).astype(BF16)
                rows_in[s + 1, rows, lanes] = mixed
                mixed = mixed.astype(F32)
                stat_acc[rows, :] += mixed * mixed
                score_acc[rows, :] += mixed * head_ref[0:1, head_slice(block)]
            return carry

        lax.fori_loop(0, blocks, run, 0)

        return carry

    lax.fori_loop(0, sections, forward, 0)

    live = []
    for m in range(micro):
        count = jnp.full((length, LANES), length_ref[m, 0], jnp.int32)
        live.append(jnp.where(t_row < count, 1.0, 0.0) / jnp.sqrt(count.astype(F32)))
    tile_rows = []
    for m in range(micro):
        rows = slice(m * length, (m + 1) * length)
        line = jnp.sum(score_acc[rows, :] * live[m], axis=0, keepdims=True)
        tile_rows.append(jnp.broadcast_to(jnp.sum(line, axis=1, keepdims=True), (1, LANES)))
    tile_rows.append(jnp.zeros((8 - micro, LANES), F32))
    score_tile = jnp.concatenate(tile_rows, axis=0)
    own_score = start_stats(sections, score_tile, score_tile)()[0]
    score_ref[...] = own_score
    resp_out[...] = own_score
    swap("resp", n_resp, me_resp, resp_out, resp_in, resp_sems)()
    winner, loser = ends_ref[0], ends_ref[1]

    def signs(r):
        return jnp.where(winner == r, 1.0, 0.0) - jnp.where(loser == r, 1.0, 0.0)

    margin = lax.fori_loop(
        0, n_resp, lambda r, acc: acc + resp_in[r] * signs(r), jnp.zeros((8, LANES), F32)
    )
    weight = 1.0 / (1.0 + jnp.exp(margin))
    slopes = -jnp.sum(signs(me_resp) * weight, axis=1, keepdims=True)

    def seed(block, carry):
        lanes = lane_slice(block)
        for m in range(micro):
            rows = slice(m * length, (m + 1) * length)
            upstream[rows, lanes] = live[m] * slopes[m : m + 1] * head_ref[0:1, head_slice(block)]
        return carry

    lax.fori_loop(0, blocks, seed, 0)

    keep_pair = total - 1 - s_lane <= prompt_len + t_row
    reverse = (
        lax.broadcasted_iota(jnp.int32, (total, total), 0)
        + lax.broadcasted_iota(jnp.int32, (total, total), 1)
        == total - 1
    )
    reverse = jnp.where(reverse, 1.0, 0.0).astype(BF16)

    share = 2 * blocks // n_resp

    def part_slice(r):
        return pl.ds(r * share, share)

    def part_steps(s, action):
        def each(step):
            peer = lax.rem(me_resp + step, n_resp)
            action(
                pltpu.make_async_remote_copy(
                    src_ref=tiles_own.at[s, part_slice(peer)],
                    dst_ref=tiles_in.at[s, me_resp],
                    send_sem=part_sems.at[0, s, step],
                    recv_sem=part_sems.at[1, s, step],
                    device_id={"resp": peer},
                    device_id_type=MESH,
                )
            )

        loop(1, n_resp, each)

    def tile_copy(s, step, k, r):
        return pltpu.make_async_remote_copy(
            src_ref=tiles_sum.at[s],
            dst_ref=tiles_all.at[k, r],
            send_sem=tile_send.at[s, step],
            recv_sem=tile_recv.at[k, r],
            device_id={"section": s, "resp": lax.rem(me_resp + step, n_resp)},
            device_id_type=MESH,
        )

    def tile_steps(s, action):
        def each(step):
            @pl.when(jnp.logical_not((s == me) & (step == 0)))
            def _():
                action(tile_copy(s, step, me, me_resp))

        loop(0, n_resp, each)

    def backward(step, carry):
        s = sections - 1 - step
        stat_acc[...] = jnp.zeros_like(stat_acc)

        def run(block, carry):
            lanes = lane_slice(block)
            wide = wide_slice(block)
            gain = gain_ref[s, :, lanes]
            short = short_ref[s, :, lanes]
            parts, saved = [], []
            for m in range(micro):
                rows = slice(m * length, (m + 1) * length)
                joined, factor = joined_rows(s, m, lanes)
                scaled = joined * factor
                normed = scaled * gain
                above = upstream[rows, lanes]
                parts.append((above * normed[prompt_len:]).astype(BF16))
                saved.append((joined[prompt_len:], scaled, normed, above))
            d_long = jnp.concatenate(parts, axis=1)
            base = pl.multiple_of(block * groups * total, groups * total)
            stacked = jnp.dot(
                toep_t[s, pl.ds(base, groups * total), :][:, :length],
                d_long,
                preferred_element_type=F32,
            )
            d_short_all = pick(stacked, total)
            turned = jnp.dot(reverse, short_out[s, :, wide], preferred_element_type=F32)
            d_wide = d_long.astype(F32)
            masked = jnp.concatenate(
                [
                    jnp.where(wide_group == g, d_wide, 0.0).astype(BF16)
                    for g in range(groups)
                ],
                axis=0,
            )
            pairs = lax.dot_general(
                masked,
                turned.astype(BF16),
                (((1,), (1,)), ((), ())),
                preferred_element_type=F32,
            )
            lines = []
            for g in range(groups):
                one = jnp.where(keep_pair, pairs[g * length : (g + 1) * length], 0.0)
                one = pltpu.roll(one, LANES + 1 - length, 1, stride=1, stride_axis=0)
                lines.append(jnp.sum(one, axis=0, keepdims=True))
            tiles_own[s, 2 * block + 1] = jnp.concatenate(lines, axis=0)
            grads = [jnp.zeros((1, LANES), F32)] * (tap_count + 1)
            for m in range(micro):
                rows = slice(m * length, (m + 1) * length)
                joined_c, scaled, normed, above = saved[m]
                d_short = d_short_all[:, m * LANES : (m + 1) * LANES]
                d_normed = d_short * short[0:1]
                grads[1] = grads[1] + jnp.sum(d_short * normed, axis=0, keepdims=True)
                for j in range(1, tap_count):
                    moved = jnp.where(
                        row_id < total - j, pltpu.roll(d_short, total - j, 0), 0.0
                    )
                    d_normed = d_normed + moved * short[j : j + 1]
                    grads[1 + j] = grads[1 + j] + jnp.sum(
                        moved * normed, axis=0, keepdims=True
                    )
                direct = above * long_out[s, rows, lanes]
                d_normed = jnp.concatenate(
                    [d_normed[:prompt_len], d_normed[prompt_len:] + direct], axis=0
                )
                grads[0] = grads[0] + jnp.sum(d_normed * scaled, axis=0, keepdims=True)
                inner = d_normed[prompt_len:] * gain
                partial[rows, lanes] = inner
                stat_acc[rows, :] += inner * joined_c
            tiles_own[s, 2 * block] = jnp.concatenate(grads, axis=0)
            return carry

        lax.fori_loop(0, blocks, run, 0)

        if direct:
            part_steps(s, lambda copy: copy.start())
            parts_in = tiles_in.at[s]
            parts_in[me_resp] = tiles_own[s, part_slice(me_resp)]

        @pl.when(s > 0)
        def _():
            line = rows_to_line(stat_acc[...])
            all_sums = start_stats(sections + 1 + step, line, line)()[0]
            factor = fac_c[s]
            pull = line_to_rows(all_sums) * (1.0 / width) * factor * factor * factor

            def finish(block, carry):
                lanes = lane_slice(block)
                grad = (
                    upstream[:, lanes]
                    + factor * partial[:, lanes]
                    - rows_in[s, :, lanes].astype(F32) * pull
                )
                upstream[:, lanes] = grad.astype(BF16).astype(F32)
                return carry

            lax.fori_loop(0, blocks, finish, 0)

        if direct:
            part_steps(s, lambda copy: copy.wait())
            tiles_sum[s] = jnp.sum(tiles_in[s], axis=0)

            @pl.when(s == me)
            def _():
                tiles_all[me, me_resp] = tiles_sum[s]

            tile_steps(s, lambda copy: copy.start())

        return carry

    lax.fori_loop(0, sections, backward, 0)

    if direct:
        loop(0, sections, lambda s: tile_steps(s, lambda copy: copy.wait_send()))

        def arrive(step):
            k, r = step // n_resp, step % n_resp

            @pl.when(jnp.logical_not((k == me) & (r == me_resp)))
            def _():
                tile_copy(0, 0, k, r).wait_recv()

        loop(0, sections * n_resp, arrive)
        gain_out, taps_short_out, taps_long_out = outs
        per_line = LANES // groups
        for line in range(sections * blocks // per_line):
            lines = []
            for place in range(per_line):
                block = line * per_line + place
                lanes = slice(block * LANES, (block + 1) * LANES)
                owner, local = divmod(2 * block, 2 * blocks)
                first, second = (divmod(local + kind, share) for kind in range(2))
                tile = tiles_all[owner, first[0], first[1]]
                gain_out[:, lanes] = tile[0:1]
                taps_short_out[:, lanes] = tile[1:]
                lines.append(tiles_all[owner, second[0], second[1]])
            lanes = slice(line * LANES, (line + 1) * LANES)
            taps_long_out[:, lanes] = jnp.transpose(jnp.concatenate(lines, axis=0))
    else:
        outs[0][...] = tiles_own[...]


def run_kernel(dims, direct, *arrays):
    sections, n_resp, micro, length, prompt_len, chans, per_group, width = dims
    rows = micro * length
    total = prompt_len + length
    group_total = chans // per_group
    tile = (8, LANES)
    tiles = 2 * chans // LANES
    share = tiles // n_resp if direct else 1
    ranks = n_resp if direct else 1
    vmem = pl.BlockSpec(memory_space=pltpu.VMEM)
    hbm = pl.BlockSpec(memory_space=pl.ANY)
    smem = pl.BlockSpec(memory_space=pltpu.SMEM)
    tap_count = arrays[3].shape[0]
    if direct:
        out_shapes = [(1, width), (tap_count, width), (LANES, width // per_group)]
    else:
        out_shapes = [(sections, tiles) + tile]
    return pl.pallas_call(
        functools.partial(kernel, dims, direct),
        out_shape=(
            jax.ShapeDtypeStruct(tile, F32),
            *(jax.ShapeDtypeStruct(shape, F32) for shape in out_shapes),
        ),
        in_specs=[hbm, hbm if direct else vmem, hbm, hbm, hbm, smem, vmem, vmem, smem],
        out_specs=(vmem,) * (1 + len(out_shapes)),
        scratch_shapes=[
            pltpu.VMEM((sections, group_total * length, 3 * LANES), BF16),
            pltpu.VMEM((sections, group_total * total, LANES), BF16),
            pltpu.VMEM((sections, ranks, prompt_len, chans), BF16),
            pltpu.VMEM((sections, micro * prompt_len, chans), BF16),
            pltpu.VMEM((sections, 1, chans), F32),
            pltpu.VMEM((sections, tap_count, chans), F32),
            pltpu.VMEM((sections, group_total, 2 * LANES), F32),
            pltpu.VMEM((sections + 1, rows, chans), BF16),
            pltpu.VMEM((sections, total, micro * chans), BF16),
            pltpu.VMEM((sections, rows, chans), F32),
            pltpu.VMEM((sections, micro * prompt_len, LANES), F32),
            pltpu.VMEM((sections, rows, LANES), F32),
            pltpu.VMEM((rows, chans), F32),
            pltpu.VMEM((rows, chans), F32),
            pltpu.VMEM((rows, LANES), F32),
            pltpu.VMEM((rows, LANES), F32),
            pltpu.VMEM((micro * prompt_len, LANES), F32),
            pltpu.VMEM((2 * sections, 2) + tile, F32),
            pltpu.VMEM((2 * sections, sections, 2) + tile, F32),
            pltpu.VMEM(tile, F32),
            pltpu.VMEM((n_resp,) + tile, F32),
            pltpu.VMEM((sections, tiles) + tile, F32),
            pltpu.VMEM((sections, ranks, share) + tile, F32),
            pltpu.VMEM((sections, share) + tile, F32),
            pltpu.VMEM((sections, ranks, share) + tile, F32),
            pltpu.SemaphoreType.DMA((5,)),
            pltpu.SemaphoreType.DMA((2, 3, sections)),
            pltpu.SemaphoreType.DMA((2, sections)),
            pltpu.SemaphoreType.DMA((2, sections, ranks)),
            pltpu.SemaphoreType.DMA((2 * sections, 2, sections)),
            pltpu.SemaphoreType.DMA((2, n_resp)),
            pltpu.SemaphoreType.DMA((2, sections, ranks)),
            pltpu.SemaphoreType.DMA((sections, ranks)),
            pltpu.SemaphoreType.DMA((sections, ranks)),
        ],
        compiler_params=pltpu.CompilerParams(
            has_side_effects=True, vmem_limit_bytes=56 * 1024 * 1024
        ),
    )(*arrays)


def body(
    completion_rows,
    prompt_pool,
    norm_gain,
    short_taps,
    long_taps,
    score_head,
    live_lengths,
    prompt_owner,
    pair_index,
):
    sections = lax.axis_size("section")
    n_resp = lax.axis_size("resp")
    me_resp = lax.axis_index("resp")
    micro, _, length, width = completion_rows.shape
    prompt_len = prompt_pool.shape[2]
    chans = width // sections
    tap_len, group_all = long_taps.shape[1:]
    per_group = width // group_all
    dims = (sections, n_resp, micro, length, prompt_len, chans, per_group, width)

    tiles = 2 * chans // LANES
    direct = n_resp <= 8 and tiles % n_resp == 0

    taps = long_taps[0].T
    flipped = jnp.concatenate([taps[:, :1], taps[:, :0:-1]], axis=1)
    taps = jnp.concatenate([flipped, taps], axis=1)
    prompts = prompt_pool[0, 0]
    if not direct:
        split = prompts.reshape(prompt_len, sections, chans).transpose(1, 0, 2)
        split = lax.all_to_all(split, "section", 0, 0, tiled=True)
        here = (prompt_owner == me_resp)[None, :, None, None]
        split = lax.psum(jnp.where(here, split[:, None], jnp.zeros((), BF16)), "resp")
        prompts = split.reshape(sections, micro * prompt_len, chans)
    rows = completion_rows.reshape(micro * length, width)
    head = score_head[None]

    ends = jnp.pad(
        pair_index.transpose(2, 0, 1),
        ((0, 0), (0, 8 - micro), (0, LANES - pair_index.shape[1])),
        constant_values=-1,
    )
    scores, *grads = run_kernel(
        dims,
        direct,
        rows,
        prompts,
        norm_gain,
        short_taps[0],
        taps,
        prompt_owner,
        head,
        ends,
        live_lengths,
    )
    scores = scores[:micro, :1].astype(BF16)
    if direct:
        return (scores, grads[0], grads[1][None], grads[2][None])
    grads = lax.psum(grads[0], "resp")
    grads = lax.all_to_all(grads, "section", 0, 0, tiled=True)
    grads = grads.reshape(sections * tiles // 2, 2, 8, LANES)
    gs_grad = grads[:, 0].transpose(1, 0, 2).reshape(8, width)
    taps_grad = grads[:, 1].reshape(group_all, tap_len).T
    return (
        scores,
        gs_grad[:1],
        gs_grad[None, 1:],
        taps_grad[None],
    )


SIDE = 8


def wide_kernel(
    dims,
    comp_hbm,
    prompt_hbm,
    gain_hbm,
    short_hbm,
    taps_hbm,
    head_hbm,
    owner_ref,
    pair_ref,
    length_ref,
    score_ref,
    short_grad_out,
    long_grad_out,
    comp_full,
    prompt_full,
    taps_full,
    head_own,
    comp_in,
    staged,
    pool,
    gain_in,
    short_in,
    taps_src,
    taps_in,
    order_c,
    order_p,
    lined,
    first_out,
    first_in,
    stat_out,
    stat_in,
    rows_in,
    prompt_rows,
    long_out,
    short_out,
    toep,
    toep_p,
    toep_t,
    params,
    heads,
    fac_c,
    fac_p,
    normed_buf,
    d_short_buf,
    upstream,
    inner_buf,
    d_long_buf,
    acc_ref,
    scales,
    tiles_own,
    short_own,
    long_own,
    local_sem,
    comp_send,
    comp_recv,
    weight_send,
    weight_recv,
    pool_send,
    pool_recv,
    pool_own,
    spread_send,
    spread_recv,
    first_send,
    first_recv,
    stat_send,
    stat_recv,
    part_send,
    part_recv,
):
    sections, n_resp, micro, length, chans, per_group, width = dims
    comps = micro * n_resp
    ranks = sections * n_resp
    blocks = chans // LANES
    per_block = LANES // per_group
    groups = blocks * per_block
    tap_count = short_in.shape[1]
    total = 2 * length
    me = lax.axis_index("section")
    me_resp = lax.axis_index("resp")
    rank = me * n_resp + me_resp

    def loop(low, high, step_of):
        def run(index, carry):
            step_of(index)
            return carry

        lax.fori_loop(low, high, run, 0)

    def lockstep(low, high, count, step_of):
        def run(index, carry):
            live = [step_of(index * count + k, k) for k in range(count)]
            while live:
                live = [step for step in live if next(step, 0) is None]
            return carry

        lax.fori_loop(low // count, high // count, run, 0)

    def add_up(values):
        while len(values) > 1:
            values = [a + b for a, b in zip(values[::2], values[1::2])] + (
                values[-1:] if len(values) % 2 else []
            )
        return values[0]

    def place(peer):
        return {"section": peer // n_resp, "resp": lax.rem(peer, n_resp)}

    def lanes_of(peer):
        return pl.ds(pl.multiple_of(peer * chans, chans), chans)

    def groups_of(peer):
        return pl.ds(pl.multiple_of(peer * groups, groups), groups)

    def remote(src, dst, send_sem, recv_sem, device):
        return pltpu.make_async_remote_copy(
            src_ref=src,
            dst_ref=dst,
            send_sem=send_sem,
            recv_sem=recv_sem,
            device_id=device,
            device_id_type=MESH,
        )

    load_comp = pltpu.make_async_copy(comp_hbm, comp_full, local_sem.at[0])
    load_prompt = pltpu.make_async_copy(prompt_hbm, prompt_full, local_sem.at[1])
    load_taps = pltpu.make_async_copy(taps_hbm, taps_full, local_sem.at[2])
    load_head = pltpu.make_async_copy(head_hbm.at[:, lanes_of(rank)], head_own, local_sem.at[3])
    own_comp = pltpu.make_async_copy(
        comp_hbm.at[:, lanes_of(rank)], comp_in.at[me_resp], local_sem.at[4]
    )
    own_stage = pltpu.make_async_copy(
        prompt_hbm.at[:, pl.ds(pl.multiple_of(me * n_resp * chans, n_resp * chans), n_resp * chans)],
        staged.at[me],
        local_sem.at[5],
    )
    own_gain = pltpu.make_async_copy(
        gain_hbm.at[:, lanes_of(rank)], gain_in.at[me], local_sem.at[6]
    )
    own_short = pltpu.make_async_copy(
        short_hbm.at[:, :, lanes_of(rank)], short_in.at[me], local_sem.at[7]
    )

    def comp_copy(step):
        peer_resp = lax.rem(me_resp + step, n_resp)
        return remote(
            comp_hbm.at[:, lanes_of(me * n_resp + peer_resp)],
            comp_in.at[me_resp],
            comp_send.at[step],
            comp_recv.at[me_resp],
            {"resp": peer_resp},
        )

    def comp_wait(step):
        source = lax.rem(me_resp + step, n_resp)
        remote(
            comp_hbm.at[:, lanes_of(rank)],
            comp_in.at[source],
            comp_send.at[step],
            comp_recv.at[source],
            {"resp": source},
        ).wait_recv()

    def weight_parts(peer_rank, source):
        return (
            (gain_hbm.at[:, lanes_of(peer_rank)], gain_in.at[source]),
            (short_hbm.at[:, :, lanes_of(peer_rank)], short_in.at[source]),
            (taps_src.at[groups_of(peer_rank), :], taps_in.at[source]),
        )

    def weight_copy(kind, step):
        peer = lax.rem(me + step, sections)
        src, dst = weight_parts(peer * n_resp + me_resp, me)[kind]
        return remote(
            src, dst, weight_send.at[kind, step], weight_recv.at[kind, me], {"section": peer}
        )

    def weight_wait(kind, step):
        source = lax.rem(me + step, sections)
        src, dst = weight_parts(rank, source)[kind]
        remote(
            src,
            dst,
            weight_send.at[kind, step],
            weight_recv.at[kind, source],
            {"section": source},
        ).wait_recv()

    def far_lanes(peer):
        span = n_resp * chans
        return pl.ds(pl.multiple_of(peer * span, span), span)

    def spread_copy(step):
        peer = lax.rem(me + step, sections)
        return remote(
            prompt_hbm.at[:, far_lanes(peer)],
            staged.at[me],
            spread_send.at[step],
            spread_recv.at[me],
            {"section": peer},
        )

    def spread_wait(s):
        remote(
            prompt_hbm.at[:, far_lanes(me)],
            staged.at[s],
            spread_send.at[0],
            spread_recv.at[s],
            {"section": s},
        ).wait_recv()

    def pool_copy(s, step):
        peer = lax.rem(me_resp + step, n_resp)
        return remote(
            staged.at[s, :, pl.ds(pl.multiple_of(peer * chans, chans), chans)],
            pool.at[s, me_resp],
            pool_send.at[s, step],
            pool_recv.at[s, me_resp],
            {"resp": peer},
        )

    def own_pool(s):
        return pltpu.make_async_copy(
            staged.at[s, :, pl.ds(pl.multiple_of(me_resp * chans, chans), chans)],
            pool.at[s, me_resp],
            pool_own.at[s],
        )

    def start_pool(s):
        @pl.when(s == me)
        def _():
            own_stage.wait()

        @pl.when(s != me)
        def _():
            spread_wait(s)

        loop(1, n_resp, lambda step: pool_copy(s, step).start())
        own_pool(s).start()

    def pool_wait(s):
        def each(step):
            source = lax.rem(me_resp + step, n_resp)
            remote(
                pool.at[s, source],
                pool.at[s, source],
                pool_send.at[s, step],
                pool_recv.at[s, source],
                {"resp": source},
            ).wait_recv()

        loop(1, n_resp, each)
        own_pool(s).wait()

    def first_copy(step):
        peer = lax.rem(rank + step, ranks)
        return remote(
            first_out, first_in.at[rank], first_send.at[step], first_recv.at[rank], place(peer)
        )

    def first_wait(step):
        source = lax.rem(rank + step, ranks)
        remote(
            first_out,
            first_in.at[source],
            first_send.at[step],
            first_recv.at[source],
            place(source),
        ).wait_recv()

    peers = []
    for j in range(1, n_resp):
        hop = jnp.where(me_resp * 2 < n_resp, n_resp - j, j)
        peer_resp = lax.rem(me_resp + hop, n_resp)
        peers += [(lax.rem(me + k, sections), peer_resp) for k in range(sections)]
    peers += [(lax.rem(me + k, sections), me_resp) for k in range(1, sections)]

    def stat_start(slot, tile):
        stat_out[slot] = tile
        for peer, peer_resp in peers:
            remote(
                stat_out.at[slot],
                stat_in.at[slot, rank],
                stat_send.at[slot],
                stat_recv.at[slot],
                {"section": peer, "resp": peer_resp},
            ).start()
        stat_in[slot, rank] = tile

    def stat_wait(slot, sem):
        bulk = stat_in.at[slot, pl.ds(0, ranks - 1)]
        pltpu.make_async_copy(bulk, bulk, sem.at[slot]).wait()

    def stat_finish(slot):
        stat_wait(slot, stat_recv)
        return jnp.sum(stat_in[slot], axis=0)

    def result_parts(s):
        return (
            (short_own.at[s], short_grad_out.at[:, :, lanes_of(rank)]),
            (long_own.at[s], long_grad_out.at[groups_of(rank), :]),
        )

    def result_own(s, kind):
        src, dst = result_parts(s)[kind]
        return pltpu.make_async_copy(src, dst, local_sem.at[8 + kind])

    def result_start(s):
        def each(step):
            @pl.when(jnp.logical_not((s == me) & (step == 0)))
            def _():
                for kind, (src, dst) in enumerate(result_parts(s)):
                    remote(
                        src,
                        dst,
                        part_send.at[kind],
                        part_recv.at[kind],
                        {"section": s, "resp": lax.rem(me_resp + step, n_resp)},
                    ).start()

        loop(0, n_resp, each)

        @pl.when(s == me)
        def _():
            for kind in range(2):
                result_own(s, kind).start()

    def result_wait(sem):
        for kind, bulk in enumerate(
            (
                short_grad_out.at[:, :, pl.ds(0, (ranks - 1) * chans)],
                long_grad_out.at[pl.ds(0, (ranks - 1) * groups), :],
            )
        ):
            pltpu.make_async_copy(bulk, bulk, sem.at[kind]).wait()

    for copy in (load_taps, load_comp, load_prompt, load_head):
        copy.start()
    for copy in (own_comp, own_stage, own_gain, own_short):
        copy.start()
    barrier = pltpu.get_barrier_semaphore()
    loop(
        1,
        ranks,
        lambda step: pl.semaphore_signal(
            barrier,
            inc=1,
            device_id=place(lax.rem(rank + step, ranks)),
            device_id_type=MESH,
        ),
    )

    tile_row = lax.broadcasted_iota(jnp.int32, (LANES, LANES), 0)
    tile_lane = lax.broadcasted_iota(jnp.int32, (LANES, LANES), 1)
    row_target = (tile_row // per_group) * LANES + tile_row % per_group
    prompt_key = (tile_lane // (n_resp * per_group)) * (n_resp * per_group) + (
        tile_lane % per_group
    )

    def fill_order(c):
        rows = pl.ds(pl.multiple_of(c * LANES, LANES), LANES)
        for n in range(per_block):
            hit = row_target + c * per_group == tile_lane + n * LANES
            order_c[rows, n * LANES : (n + 1) * LANES] = jnp.where(hit, 1.0, 0.0).astype(BF16)

    loop(0, comps, fill_order)
    for m in range(micro):
        for n in range(per_block):
            hit = row_target + m * n_resp * per_group == prompt_key + n * LANES
            order_p[m * LANES : (m + 1) * LANES, n * LANES : (n + 1) * LANES] = jnp.where(
                hit, 1.0, 0.0
            ).astype(BF16)
    pad = 8
    for g in range(groups):
        normed_buf[g, :pad] = jnp.zeros((pad, LANES), F32)
        for s in range(sections):
            d_short_buf[s, g, total:] = jnp.zeros((pad, LANES), F32)

    load_taps.wait()
    upright = jnp.transpose(taps_full[...])
    mirror = jnp.where(lax.rem(tile_row + tile_lane, LANES) == 0, 1.0, 0.0)
    taps_src[:, :LANES] = jnp.dot(
        upright, mirror, preferred_element_type=F32, precision=lax.Precision.HIGHEST
    )
    taps_src[:, LANES:] = upright

    ones = jnp.ones((16, 2 * LANES), BF16)

    def split(values):
        high = values.astype(BF16)
        return high, (values - high.astype(F32)).astype(BF16)

    def lane_sums(acc, weights, below=None):
        if acc.shape[0] < LANES:
            rest = [] if below is None else [below]
            rows = LANES - acc.shape[0] - sum(block.shape[0] for block in rest)
            acc = jnp.concatenate([acc] + rest + [jnp.zeros((rows, LANES), F32)], axis=0)
        both = jnp.concatenate(split(acc), axis=1)
        return lax.dot_general(
            weights, both, (((1,), (1,)), ((), ())), preferred_element_type=F32
        )[:8]

    def square_rows(ref):
        def step(block, acc):
            values = ref[:, pl.ds(pl.multiple_of(block * LANES, LANES), LANES)].astype(F32)
            return acc + values * values

        return lax.fori_loop(
            0, width // LANES, step, jnp.zeros((ref.shape[0], LANES), F32), unroll=2
        )

    load_comp.wait()
    comp_line = lane_sums(square_rows(comp_full), ones)
    load_prompt.wait()
    prompt_line = lane_sums(square_rows(prompt_full), ones)
    eight_row = lax.broadcasted_iota(jnp.int32, (8, LANES), 0)
    eight_lane = lax.broadcasted_iota(jnp.int32, (8, LANES), 1)
    message = jnp.where(eight_row == 0, comp_line, prompt_line)
    for m in range(micro):
        count = jnp.full((8, LANES), length_ref[0, m], jnp.int32).astype(F32)
        message = jnp.where(eight_row == 2 + m, count, message)
    first_out[...] = message

    pl.semaphore_wait(barrier, ranks - 1)
    @pl.when(me == 0)
    def _():
        loop(1, sections, lambda step: spread_copy(step).start())

    loop(1, n_resp, lambda step: comp_copy(step).start())
    loop(1, sections, lambda step: weight_copy(2, step).start())

    loop(1, ranks, lambda step: first_copy(step).start())

    def start_vectors(step):
        weight_copy(0, step).start()
        weight_copy(1, step).start()

    loop(1, sections, start_vectors)
    @pl.when(me != 0)
    def _():
        loop(1, sections, lambda step: spread_copy(step).start())

    first_in[rank] = message
    taps_in[me] = taps_src[groups_of(rank), :]

    own_gain.wait()
    own_short.wait()
    load_head.wait()

    def weights_arrive(step):
        for kind in range(3):
            weight_wait(kind, step)

    loop(1, sections, weights_arrive)

    def tile_lanes(values, n):
        out = pltpu.roll(values, (LANES - n * per_group) % LANES, 1)
        out = jnp.where(eight_lane < per_group, out, 0.0)
        span = per_group
        while span < LANES:
            out = out + pltpu.roll(out, span, 1)
            span *= 2
        return out

    t_row = lax.broadcasted_iota(jnp.int32, (length, LANES), 0)
    s_lane = lax.broadcasted_iota(jnp.int32, (length, LANES), 1)
    keep = s_lane <= length + t_row
    keep_t = tile_row <= length + tile_lane

    def spread_params(s):
        for b in range(blocks):
            lanes = slice(b * LANES, (b + 1) * LANES)
            rows = jnp.concatenate(
                [gain_in[s, :, lanes]] + [short_in[s, j, :, lanes] for j in range(tap_count)],
                axis=0,
            )
            for n in range(per_block):
                params[s, b * per_block + n] = tile_lanes(rows, n)

    loop(0, sections, spread_params)
    for b in range(blocks):
        rows = jnp.broadcast_to(head_own[:, b * LANES : (b + 1) * LANES], (8, LANES))
        for n in range(per_block):
            heads[b * per_block + n] = tile_lanes(rows, n)

    def build(s, g, k):
        line = taps_in[s, pl.ds(g, 1), :]
        wide = jnp.broadcast_to(line[:, :LANES], (length, LANES))
        wide = pltpu.roll(wide, length, 1, stride=1, stride_axis=0)
        wide_t = jnp.broadcast_to(line[:, LANES:], (total, LANES))
        wide_t = pltpu.roll(wide_t, length, 1, stride=1, stride_axis=0)
        yield
        wide = jnp.where(keep, wide, 0.0)
        high = wide.astype(BF16).astype(F32)
        low = wide - high
        low_turned = pltpu.roll(low, length, 1)
        high_turned = pltpu.roll(high, length, 1)
        toep_t[s, g] = jnp.where(keep_t, wide_t, 0.0).astype(BF16)
        yield
        first = s_lane < length
        toep_p[s, g] = jnp.where(first, high, low_turned).astype(BF16)
        toep[s, g] = jnp.where(first, high_turned, low).astype(BF16)

    start_pool(0)
    def build_section(s):
        lockstep(0, groups, 4, lambda g, k: build(s, g, k))

    build_section(0)

    def spread_rows(lines):
        tall = jnp.concatenate(
            [jnp.broadcast_to(lines[c : c + 1], (per_group, LANES)) for c in range(comps)],
            axis=0,
        )
        return jnp.transpose(tall)[:length]

    def to_factor(sums):
        return lax.rsqrt(sums * (1.0 / width) + 1e-06)

    loop(1, ranks, first_wait)
    own_lines = jnp.concatenate(
        [first_in[me * n_resp + r, 0:1] for r in range(n_resp)], axis=0
    )
    own_lines = jnp.concatenate(
        [
            own_lines if m == 0 else pltpu.roll(own_lines, LANES - m * length, 1)
            for m in range(micro)
        ],
        axis=0,
    )
    fac_c[0] = spread_rows(to_factor(own_lines))

    def prompt_factor(s):
        lines = []
        for m in range(micro):
            owner = jnp.full((8, LANES), owner_ref[m], jnp.int32)
            line = jnp.zeros((8, LANES), F32)
            for r in range(n_resp):
                line = jnp.where(owner == r, first_in[s * n_resp + r], line)
            lines += [line[1:2]] * n_resp
        fac_p[s] = spread_rows(to_factor(jnp.concatenate(lines, axis=0)))

    loop(0, sections, prompt_factor)

    def conv_short(ref, g, start, taps):
        out = ref[g, pl.ds(start, length)] * taps[1:2]
        for j in range(1, tap_count):
            out = out + ref[g, pl.ds(start - j, length)] * taps[1 + j : 2 + j]
        return out

    def conv_long(matrix, high, low):
        left = jnp.concatenate([matrix, matrix], axis=1)
        right = jnp.concatenate([high, high, low, low], axis=0)
        return jnp.dot(left, right, preferred_element_type=F32)

    def prepare(s):
        pool_wait(s)

        sides = []
        for b in range(blocks):
            lanes = slice(b * LANES, (b + 1) * LANES)
            row = []
            for m in range(micro):
                owner = jnp.full((length, LANES), owner_ref[m], jnp.int32)
                picked = pool[s, 0, :, lanes].astype(F32)
                for r in range(1, n_resp):
                    picked = jnp.where(owner == r, pool[s, r, :, lanes].astype(F32), picked)
                row.append(picked.astype(BF16))
            sides.append(jnp.concatenate(row, axis=1))
        side = jnp.concatenate(sides, axis=0)
        step = 2 * LANES
        for n in range(per_block // 2):
            part = jnp.dot(
                side, order_p[:, n * step : (n + 1) * step], preferred_element_type=F32
            ).astype(BF16)
            for b in range(blocks):
                for k in range(2):
                    prompt_rows[s, b * per_block + 2 * n + k] = part[
                        b * length : (b + 1) * length, k * LANES : (k + 1) * LANES
                    ]
        factor = fac_p[s]

        def each(g, k):
            taps = params[s, g]
            normed = prompt_rows[s, g].astype(F32) * factor * taps[0:1]
            normed_buf[g, pl.ds(pad, length)] = normed
            yield
            shorter = conv_short(normed_buf, g, pad, taps)
            high, low = split(shorter)
            short_out[s, g, :length] = high
            yield
            longer = conv_long(toep_p[s, g], high, low)
            yield
            long_out[s, g] = longer

        lockstep(0, groups, SIDE, each)

    loop(1, n_resp, comp_wait)
    start_pool(1)
    own_comp.wait()
    for b in range(blocks):
        lanes = slice(b * LANES, (b + 1) * LANES)
        for m in range(micro):
            for r in range(n_resp):
                c = m * n_resp + r
                lined[b * length : (b + 1) * length, c * LANES : (c + 1) * LANES] = comp_in[
                    r, m * length : (m + 1) * length, lanes
                ]
    for n in range(per_block // 2):
        step = 2 * LANES
        part = jnp.dot(
            lined[...], order_c[:, n * step : (n + 1) * step], preferred_element_type=F32
        ).astype(BF16)
        for b in range(blocks):
            for k in range(2):
                rows_in[0, b * per_block + 2 * n + k] = part[
                    b * length : (b + 1) * length, k * LANES : (k + 1) * LANES
                ]
    prepare(0)

    fold_row = lax.broadcasted_iota(jnp.int32, (16, 2 * LANES), 0)
    fold_lane = lax.broadcasted_iota(jnp.int32, (16, 2 * LANES), 1)
    fold = jnp.where((fold_lane % LANES) // per_group == fold_row, 1.0, 0.0).astype(BF16)

    def forward(s, last):
        acc_ref[...] = jnp.zeros_like(acc_ref)
        factor = fac_c[s]

        sums = []

        def each(g, k):
            taps = params[s, g]
            rows = rows_in[s, g].astype(F32)
            normed = rows * factor * taps[0:1]
            normed_buf[g, pl.ds(pad + length, length)] = normed
            yield
            shorter = conv_short(normed_buf, g, pad + length, taps)
            high, low = split(shorter)
            short_out[s, g, length:] = high
            yield
            longer = conv_long(toep[s, g], high, low)
            yield
            longer = long_out[s, g] + longer
            normed = normed_buf[g, pl.ds(pad + length, length)]
            mixed = (rows_in[s, g].astype(F32) + normed * longer).astype(BF16)
            sums.append((longer, mixed))
            yield
            longer, mixed = sums[k]
            long_out[s, g] = longer
            if not last:
                rows_in[s + 1, g] = mixed
            mixed = mixed.astype(F32)
            sums[k] = mixed * (heads[g, 0:1] if last else mixed)
            yield
            if k == SIDE - 1:
                acc_ref[...] += add_up(sums)
                sums.clear()

        lockstep(0, groups, SIDE, each)

    def forward_step(s):
        forward(s, False)
        stat_start(s, lane_sums(acc_ref[...], fold))
        build_section(s + 1)
        prepare(s + 1)

        @pl.when(s + 2 < sections)
        def _():
            start_pool(s + 2)

        fac_c[s + 1] = spread_rows(to_factor(stat_finish(s)))

    loop(0, sections - 1, forward_step)
    forward(sections - 1, True)

    comp_lane = eight_lane // per_group
    counts = jnp.zeros((8, LANES), F32)
    for m in range(micro):
        for r in range(n_resp):
            row = first_in[me * n_resp + r, 2 + m : 3 + m]
            counts = jnp.where(comp_lane == m * n_resp + r, row, counts)
    alive = t_row.astype(F32) < counts[0:1]
    live = jnp.where(alive, 1.0, 0.0) / jnp.sqrt(counts[0:1])
    score_line = jnp.sum(acc_ref[...] * live, axis=0, keepdims=True)
    score_line = jnp.where(eight_row == 0, score_line, 0.0)

    def seed(g, k):
        upstream[sections - 1, g] = live * heads[g, 0:1]
        yield

    lockstep(0, groups, SIDE, seed)

    def backward(s, last):
        acc_ref[...] = jnp.zeros_like(acc_ref)
        factor = fac_c[s]

        sums = []

        def each(g, k):
            taps = params[s, g]
            rows = rows_in[s, g].astype(F32)
            d_long = (upstream[s, g] * (rows * factor * taps[0:1])).astype(BF16)
            yield
            d_long_buf[s, g] = d_long
            d_short = jnp.dot(
                toep_t[s, g][:, :length], d_long, preferred_element_type=F32
            )
            yield
            d_short_buf[s, g, pl.ds(0, total)] = d_short
            if last:
                return
            yield
            d_normed = upstream[s, g] * long_out[s, g]
            for j in range(tap_count):
                d_normed = d_normed + d_short_buf[s, g, pl.ds(length + j, length)] * taps[1 + j : 2 + j]
            inner = d_normed * taps[0:1]
            sums.append(inner)
            yield
            inner_buf[g] = sums[k]
            sums[k] = sums[k] * rows_in[s, g].astype(F32)
            yield
            if k == SIDE - 1:
                acc_ref[...] += add_up(sums)
                sums.clear()

        lockstep(0, groups, SIDE, each)

    keep_pair = total - 1 - s_lane <= length + t_row
    reverse = jnp.where(tile_row + tile_lane == total - 1, 1.0, 0.0).astype(BF16)

    def gradients(s):
        factor_c = fac_c[s]
        factor_p = fac_p[s]
        scale = scales[s, 0:1]
        tops, longs = [], []

        def each(g, k):
            turned = jnp.dot(reverse, short_out[s, g], preferred_element_type=F32)
            yield
            pairs = lax.dot_general(
                (d_long_buf[s, g].astype(F32) * scale).astype(BF16),
                turned.astype(BF16),
                (((1,), (1,)), ((), ())),
                preferred_element_type=F32,
            )
            yield
            taps = params[s, g]
            scaled_p = prompt_rows[s, g].astype(F32) * factor_p
            scaled_c = rows_in[s, g].astype(F32) * factor_c
            lines = [
                jnp.sum(upstream[s, g] * long_out[s, g] * scaled_c, axis=0, keepdims=True)
            ]
            for j in range(tap_count):
                part = (
                    d_short_buf[s, g, pl.ds(j, length)] * scaled_p
                    + d_short_buf[s, g, pl.ds(length + j, length)] * scaled_c
                )
                lines.append(jnp.sum(part, axis=0, keepdims=True))
            tile = jnp.concatenate(lines, axis=0) * scale
            yield
            pairs = jnp.where(keep_pair, pairs, 0.0)
            pairs = pltpu.roll(pairs, LANES + 1 - length, 1, stride=1, stride_axis=0)
            yield
            span = per_group
            while span < LANES:
                tile = tile + pltpu.roll(tile, span, 1)
                span *= 2
            yield
            top = tile + jnp.sum(
                jnp.where(eight_row > 0, tile * taps, 0.0), axis=0, keepdims=True
            )
            tops.append(jnp.where(eight_row == 0, top, tile * taps[0:1]))
            longs.append(jnp.sum(pairs, axis=0, keepdims=True))
            yield
            if k < SIDE - 1:
                return
            b, n = g // per_block, lax.rem(g, per_block)
            tile = tiles_own[b]
            for i in range(SIDE):
                tile = jnp.where(comp_lane == n - (SIDE - 1) + i, tops[i], tile)
            tiles_own[b] = tile
            long_own[s, pl.ds(pl.multiple_of(g - (SIDE - 1), SIDE), SIDE)] = jnp.concatenate(
                longs, axis=0
            )
            tops.clear()
            longs.clear()

        for b in range(blocks):
            tiles_own[b] = jnp.zeros((8, LANES), F32)
        lockstep(0, groups, SIDE, each)
        for b in range(blocks):
            tile = tiles_own[b]
            for j in range(1 + tap_count):
                short_own[s, j, :, b * LANES : (b + 1) * LANES] = tile[j : j + 1]
        result_start(s)

    def go_down(s, sums, scale):
        factor = fac_c[s]
        pull = spread_rows(sums * (1.0 / width)) * factor * factor * factor

        def finish(g, k):
            grad = upstream[s, g] + factor * inner_buf[g] - rows_in[s, g].astype(F32) * pull
            yield
            if scale is not None:
                grad = grad * scale
            upstream[s - 1, g] = grad.astype(BF16).astype(F32)

        lockstep(0, groups, SIDE, finish)

    last = sections - 1
    backward(last, False)
    stat_start(last, lane_sums(acc_ref[...], fold, score_line))
    loop(1, n_resp, lambda step: comp_copy(step).wait_send())

    def weights_sent(step):
        for kind in range(3):
            weight_copy(kind, step).wait_send()

    loop(1, sections, weights_sent)

    loop(1, ranks, lambda step: first_copy(step).wait_send())
    loop(1, sections, lambda step: spread_copy(step).wait_send())

    def pools_sent(s):
        loop(1, n_resp, lambda step: pool_copy(s, step).wait_send())

    loop(0, sections, pools_sent)
    winner = jnp.full((8, LANES), -1, jnp.int32)
    loser = winner
    for m in range(micro):
        for p in range(pair_ref.shape[2]):
            here = (eight_row == m) & (eight_lane == p)
            winner = jnp.where(here, pair_ref[m, 0, p], winner)
            loser = jnp.where(here, pair_ref[m, 1, p], loser)
    signs = [
        jnp.where(winner == r, 1.0, 0.0) - jnp.where(loser == r, 1.0, 0.0)
        for r in range(n_resp)
    ]
    masks = [comp_lane == eight_row * n_resp + r for r in range(n_resp)]
    sums = stat_finish(last)
    totals = jnp.sum(jnp.where(eight_lane == length, sums, 0.0), axis=1, keepdims=True)
    totals = jnp.broadcast_to(totals, (8, LANES))
    scores = []
    for r in range(n_resp):
        rows = totals[r : r + 1]
        for m in range(1, micro):
            rows = jnp.where(eight_row == m, totals[m * n_resp + r : m * n_resp + r + 1], rows)
        scores.append(jnp.broadcast_to(rows, (8, LANES)))
    own_score = scores[0]
    margin = jnp.zeros((8, LANES), F32)
    for r in range(n_resp):
        margin = margin + scores[r] * signs[r]
        own_score = jnp.where(me_resp == r, scores[r], own_score)
    score_ref[...] = own_score[:micro, :1].astype(BF16)
    weight = 1.0 / (1.0 + jnp.exp(margin))
    slopes = jnp.zeros((8, LANES), F32)
    for r in range(n_resp):
        slope = -jnp.sum(signs[r] * weight, axis=1, keepdims=True)
        slopes = jnp.where(masks[r], slope, slopes)
    slopes = jnp.sum(slopes, axis=0, keepdims=True)
    for s in range(sections - 1):
        scales[s] = jnp.ones((8, LANES), F32)
    scales[last] = jnp.broadcast_to(slopes, (8, LANES))
    go_down(last, sums, slopes)

    def backward_step(step):
        s = sections - 1 - step
        slot = last + step
        backward(s, False)
        stat_start(slot, lane_sums(acc_ref[...], fold))
        loop(s, jnp.where(step == 1, s + 2, s + 1), gradients)
        go_down(s, stat_finish(slot), None)

    loop(1, sections - 1, backward_step)
    backward(0, True)
    gradients(0)

    loop(0, 2 * sections - 2, lambda slot: stat_wait(slot, stat_send))
    for kind in range(2):
        result_own(me, kind).wait()
    result_wait(part_send)
    result_wait(part_recv)


def flush_kernel(score_in, short_in, long_in, score_ref, gain_ref, short_ref, long_ref):
    score_ref[...] = score_in[...]
    gain_ref[...] = short_in[0]
    short_ref[...] = short_in[1:]
    long_ref[...] = jnp.transpose(long_in[...])


def flush(scores, short_grad, long_grad):
    vmem = pl.BlockSpec(memory_space=pltpu.VMEM)
    rows, _, width = short_grad.shape
    return pl.pallas_call(
        flush_kernel,
        out_shape=(
            jax.ShapeDtypeStruct(scores.shape, BF16),
            jax.ShapeDtypeStruct((1, width), F32),
            jax.ShapeDtypeStruct((rows - 1, 1, width), F32),
            jax.ShapeDtypeStruct(long_grad.shape[::-1], F32),
        ),
        in_specs=[vmem] * 3,
        out_specs=(vmem,) * 4,
    )(scores, short_grad, long_grad)


def run_wide(dims, *arrays):
    sections, n_resp, micro, length, chans, per_group, width = dims
    comps = micro * n_resp
    ranks = sections * n_resp
    groups = chans // per_group
    blocks = chans // LANES
    total = 2 * length
    tap_count = arrays[3].shape[0]
    group_all = width // per_group
    tile = (8, LANES)
    vmem = pl.BlockSpec(memory_space=pltpu.VMEM)
    hbm = pl.BlockSpec(memory_space=pl.ANY)
    smem = pl.BlockSpec(memory_space=pltpu.SMEM)
    slots = 2 * sections - 2
    per = (sections, groups)
    dma = pltpu.SemaphoreType.DMA
    return pl.pallas_call(
        functools.partial(wide_kernel, dims),
        out_shape=(
            jax.ShapeDtypeStruct((micro, 1), BF16),
            jax.ShapeDtypeStruct((1 + tap_count, 1, width), F32),
            jax.ShapeDtypeStruct((group_all, LANES), F32),
        ),
        in_specs=[hbm] * 6 + [smem] * 3,
        out_specs=(vmem,) * 3,
        scratch_shapes=[
            pltpu.VMEM((micro * length, width), BF16),
            pltpu.VMEM((length, width), BF16),
            pltpu.VMEM((LANES, group_all), F32),
            pltpu.VMEM((1, chans), F32),
            pltpu.VMEM((n_resp, micro * length, chans), BF16),
            pltpu.VMEM((sections, length, n_resp * chans), BF16),
            pltpu.VMEM((sections, n_resp, length, chans), BF16),
            pltpu.VMEM((sections, 1, chans), F32),
            pltpu.VMEM((sections, tap_count, 1, chans), F32),
            pltpu.VMEM((group_all, 2 * LANES), F32),
            pltpu.VMEM((sections, groups, 2 * LANES), F32),
            pltpu.VMEM((comps * LANES, (LANES // per_group) * LANES), BF16),
            pltpu.VMEM((micro * LANES, (LANES // per_group) * LANES), BF16),
            pltpu.VMEM((blocks * length, comps * LANES), BF16),
            pltpu.VMEM(tile, F32),
            pltpu.VMEM((ranks,) + tile, F32),
            pltpu.VMEM((slots,) + tile, F32),
            pltpu.VMEM((slots, ranks) + tile, F32),
            pltpu.VMEM(per + (length, LANES), BF16),
            pltpu.VMEM(per + (length, LANES), BF16),
            pltpu.VMEM(per + (length, LANES), F32),
            pltpu.VMEM(per + (total, LANES), BF16),
            pltpu.VMEM(per + (length, LANES), BF16),
            pltpu.VMEM(per + (length, LANES), BF16),
            pltpu.VMEM(per + (total, LANES), BF16),
            pltpu.VMEM(per + tile, F32),
            pltpu.VMEM((groups,) + tile, F32),
            pltpu.VMEM((sections, length, LANES), F32),
            pltpu.VMEM((sections, length, LANES), F32),
            pltpu.VMEM((groups, 8 + total, LANES), F32),
            pltpu.VMEM(per + (total + 8, LANES), F32),
            pltpu.VMEM(per + (length, LANES), F32),
            pltpu.VMEM((groups, length, LANES), F32),
            pltpu.VMEM(per + (length, LANES), BF16),
            pltpu.VMEM((length, LANES), F32),
            pltpu.VMEM((sections,) + tile, F32),
            pltpu.VMEM((blocks,) + tile, F32),
            pltpu.VMEM((sections, 1 + tap_count, 1, chans), F32),
            pltpu.VMEM((sections, groups, LANES), F32),
            dma((10,)),
            dma((n_resp,)),
            dma((n_resp,)),
            dma((3, sections)),
            dma((3, sections)),
            dma((sections, n_resp)),
            dma((sections, n_resp)),
            dma((sections,)),
            dma((sections,)),
            dma((sections,)),
            dma((ranks,)),
            dma((ranks,)),
            dma((slots,)),
            dma((slots,)),
            dma((2,)),
            dma((2,)),
        ],
        compiler_params=pltpu.CompilerParams(
            collective_id=1, has_side_effects=True, vmem_limit_bytes=56 * 1024 * 1024
        ),
    )(*arrays)


def wide_body(
    completion_rows,
    prompt_pool,
    norm_gain,
    short_taps,
    long_taps,
    score_head,
    live_lengths,
    prompt_owner,
    pair_index,
):
    sections = lax.axis_size("section")
    n_resp = lax.axis_size("resp")
    micro, _, length, width = completion_rows.shape
    chans = width // (sections * n_resp)
    per_group = width // long_taps.shape[2]
    results = run_wide(
        (sections, n_resp, micro, length, chans, per_group, width),
        completion_rows.reshape(micro * length, width),
        prompt_pool[0, 0],
        norm_gain,
        short_taps.transpose(1, 0, 2),
        long_taps[0],
        score_head[None],
        prompt_owner,
        pair_index.transpose(0, 2, 1),
        live_lengths.T,
    )
    scores, gain_grad, short_grad, long_grad = flush(*results)
    return (
        scores,
        gain_grad,
        short_grad.transpose(1, 0, 2),
        long_grad[None],
    )


def is_wide(
    completion_rows,
    prompt_pool,
    norm_gain,
    short_taps,
    long_taps,
    score_head,
    live_lengths,
    prompt_owner,
    pair_index,
):
    sections = lax.axis_size("section")
    n_resp = lax.axis_size("resp")
    micro, _, length, width = completion_rows.shape
    per_group = width // long_taps.shape[2]
    return (
        micro * n_resp * per_group == LANES
        and micro * n_resp == 8
        and width % (sections * n_resp * LANES) == 0
        and prompt_pool.shape[2] == length
        and long_taps.shape[1] == 2 * length == LANES
        and micro * length == LANES
        and short_taps.shape[1] == 7
        and sections >= 3
    )


def either(*arrays):
    return wide_body(*arrays) if is_wide(*arrays) else body(*arrays)


def solution(mesh):
    placed = (
        P(None, ("groups", "resp"), None, None),
        P("section", ("groups", "resp"), None, None),
        P("section", None),
        P("section", None, None),
        P("section", None, None),
        P(),
        P(None, ("groups", "resp")),
        P("groups"),
        P(None, "groups", None),
    )
    return jax.shard_map(
        either,
        mesh=mesh,
        in_specs=placed,
        out_specs=(
            P(None, ("groups", "resp")),
            P("section", "groups"),
            P("section", "groups", None),
            P("section", "groups", None),
        ),
        check_vma=False,
    )
```

```python
import functools

import jax
import jax.numpy as jnp
from jax import lax
from jax.experimental import pallas as pl
from jax.experimental.pallas import tpu as pltpu
from jax.sharding import PartitionSpec as P

LANES = 128
MESH = pl.DeviceIdType.MESH
F32 = jnp.float32
BF16 = jnp.bfloat16


def rows_to_line(block):
    line = jnp.sum(jnp.transpose(block), axis=0, keepdims=True)
    return jnp.broadcast_to(line, (8, LANES))


def line_to_rows(tile):
    return jnp.transpose(jnp.broadcast_to(tile[0:1], (LANES, LANES)))


def kernel(
    dims,
    direct,
    comp_ref,
    prompt_ref,
    gain_hbm,
    short_hbm,
    taps_hbm,
    owner_ref,
    head_ref,
    ends_ref,
    length_ref,
    score_ref,
    *rest,
):
    sections, n_resp, micro, length, prompt_len, chans, per_group, width = dims
    outs, rest = (rest[:3], rest[3:]) if direct else (rest[:1], rest[1:])
    (
        toep,
        toep_t,
        pool,
        chosen_rows,
        gain_ref,
        short_ref,
        taps_ref,
        rows_in,
        short_out,
        long_out,
        fac_p,
        fac_c,
        upstream,
        partial,
        stat_acc,
        score_acc,
        prompt_acc,
        stat_out,
        stat_in,
        resp_out,
        resp_in,
        tiles_own,
        tiles_in,
        tiles_sum,
        tiles_all,
        local_sem,
        weight_sems,
        spread_sems,
        pool_sems,
        stat_sems,
        resp_sems,
        part_sems,
        tile_send,
        tile_recv,
    ) = rest
    groups = LANES // per_group
    blocks = chans // LANES
    group_rows = blocks * groups
    total = prompt_len + length
    me = lax.axis_index("section")
    me_resp = lax.axis_index("resp")
    own_lanes = pl.ds(pl.multiple_of(me * chans, chans), chans)

    def lane_slice(block):
        return pl.ds(pl.multiple_of(block * LANES, LANES), LANES)

    def head_slice(block):
        return pl.ds(pl.multiple_of(me * chans + block * LANES, LANES), LANES)

    def wide_slice(block):
        return pl.ds(pl.multiple_of(block * micro * LANES, LANES), micro * LANES)

    def loop(low, high, step_of):
        def run(index, carry):
            step_of(index)
            return carry

        lax.fori_loop(low, high, run, 0)

    def swap(axis, count, mine, out_ref, in_ref, sems):
        def copy(step):
            return pltpu.make_async_remote_copy(
                src_ref=out_ref,
                dst_ref=in_ref.at[mine],
                send_sem=sems.at[0, step],
                recv_sem=sems.at[1, step],
                device_id={axis: lax.rem(mine + step, count)},
                device_id_type=MESH,
            )

        loop(1, count, lambda step: copy(step).start())
        in_ref[mine] = out_ref[...]
        return lambda: loop(1, count, lambda step: copy(step).wait())

    def start_stats(slot, first, second):
        stat_out[slot, 0] = first
        stat_out[slot, 1] = second
        wait = swap(
            "section", sections, me, stat_out.at[slot], stat_in.at[slot], stat_sems.at[slot]
        )

        def finish():
            wait()
            return jnp.sum(stat_in[slot], axis=0)

        return finish

    def weight_copies(step):
        peer = lax.rem(me + step, sections)
        lanes = pl.ds(pl.multiple_of(peer * chans, chans), chans)
        rows = pl.ds(pl.multiple_of(peer * group_rows, group_rows), group_rows)
        return [
            pltpu.make_async_remote_copy(
                src_ref=source,
                dst_ref=target,
                send_sem=weight_sems.at[0, kind, step],
                recv_sem=weight_sems.at[1, kind, step],
                device_id={"section": peer},
                device_id_type=MESH,
            )
            for kind, source, target in (
                (0, gain_hbm.at[:, lanes], gain_ref.at[me]),
                (2, short_hbm.at[:, lanes], short_ref.at[me]),
                (1, taps_hbm.at[rows, :], taps_ref.at[me]),
            )
        ]

    def start_weights(step):
        for copy in weight_copies(step):
            copy.start()

    def wait_weights(step):
        for copy in weight_copies(step):
            copy.wait()

    own_rows = pl.ds(pl.multiple_of(me * group_rows, group_rows), group_rows)
    local_copies = [
        pltpu.make_async_copy(comp_ref.at[:, own_lanes], rows_in.at[0], local_sem.at[0]),
        pltpu.make_async_copy(gain_hbm.at[:, own_lanes], gain_ref.at[me], local_sem.at[1]),
        pltpu.make_async_copy(short_hbm.at[:, own_lanes], short_ref.at[me], local_sem.at[3]),
        pltpu.make_async_copy(taps_hbm.at[own_rows, :], taps_ref.at[me], local_sem.at[2]),
    ]

    def spread_copy(step):
        peer = lax.rem(me + step, sections)
        lanes = pl.ds(pl.multiple_of(peer * chans, chans), chans)
        return pltpu.make_async_remote_copy(
            src_ref=prompt_ref.at[:, lanes],
            dst_ref=pool.at[me, me_resp],
            send_sem=spread_sems.at[0, step],
            recv_sem=spread_sems.at[1, step],
            device_id={"section": peer},
            device_id_type=MESH,
        )

    def pool_copy(s, step):
        return pltpu.make_async_remote_copy(
            src_ref=pool.at[s, me_resp],
            dst_ref=pool.at[s, me_resp],
            send_sem=pool_sems.at[0, s, step],
            recv_sem=pool_sems.at[1, s, step],
            device_id={"resp": lax.rem(me_resp + step, n_resp)},
            device_id_type=MESH,
        )

    def own_pool():
        return pltpu.make_async_copy(
            prompt_ref.at[:, own_lanes], pool.at[me, me_resp], local_sem.at[4]
        )

    def start_pool(s):
        step = lax.rem(me - s + sections, sections)

        @pl.when(step == 0)
        def _():
            own_pool().wait()

        @pl.when(step > 0)
        def _():
            spread_copy(step).wait()

        loop(1, n_resp, lambda d: pool_copy(s, d).start())

    def wait_pool(s):
        loop(1, n_resp, lambda d: pool_copy(s, d).wait())

    if direct:
        own_pool().start()
        loop(1, sections, lambda step: spread_copy(step).start())
    for copy in local_copies:
        copy.start()
    loop(1, sections, start_weights)
    if direct:
        start_pool(0)
    for copy in local_copies:
        copy.wait()

    def first_stats(block):
        wide = rows_in[0, :, lane_slice(block)].astype(F32)
        stat_acc[...] += wide * wide

    stat_acc[...] = jnp.zeros_like(stat_acc)
    loop(0, blocks, first_stats)
    loop(1, sections, wait_weights)

    t_row = lax.broadcasted_iota(jnp.int32, (length, LANES), 0)
    s_lane = lax.broadcasted_iota(jnp.int32, (length, LANES), 1)
    keep = s_lane <= prompt_len + t_row
    s_row = lax.broadcasted_iota(jnp.int32, (total, LANES), 0)
    t_lane = lax.broadcasted_iota(jnp.int32, (total, LANES), 1)
    keep_t = s_row <= prompt_len + t_lane

    def build(s, block):
        rows = pl.ds(pl.multiple_of(block * groups, groups), groups)
        both = taps_ref[s, rows, :]
        flipped, plain = both[:, :LANES], both[:, LANES:]
        for g in range(groups):
            base = pl.multiple_of((block * groups + g) * length, length)
            wide = jnp.broadcast_to(flipped[g : g + 1], (length, LANES))
            wide = pltpu.roll(wide, prompt_len, 1, stride=1, stride_axis=0)
            wide = jnp.where(keep, wide, 0.0)
            high = wide.astype(BF16)
            low = (wide - high.astype(F32)).astype(BF16)
            toep[s, pl.ds(base, length), :] = jnp.concatenate([high, high, low], axis=1)
            base = pl.multiple_of((block * groups + g) * total, total)
            wide = jnp.broadcast_to(plain[g : g + 1], (total, LANES))
            wide = pltpu.roll(wide, prompt_len, 1, stride=1, stride_axis=0)
            toep_t[s, pl.ds(base, total), :] = jnp.where(keep_t, wide, 0.0).astype(BF16)

    def choose(s, block):
        lanes = lane_slice(block)
        for m in range(micro):
            rows = slice(m * prompt_len, (m + 1) * prompt_len)
            if direct:
                picked = jnp.zeros((prompt_len, LANES), F32)
                for r in range(n_resp):
                    flag = jnp.full((prompt_len, LANES), owner_ref[m], jnp.int32) == r
                    picked = jnp.where(flag, pool[s, r, :, lanes].astype(F32), picked)
                chosen_rows[s, rows, lanes] = picked.astype(BF16)
            else:
                picked = prompt_ref[s, rows, lanes].astype(F32)
                chosen_rows[s, rows, lanes] = prompt_ref[s, rows, lanes]
            prompt_acc[rows, :] += picked * picked

    row_id = lax.broadcasted_iota(jnp.int32, (total, LANES), 0)
    wide_group = (
        lax.broadcasted_iota(jnp.int32, (1, micro * LANES), 1) % LANES
    ) // per_group
    tap_count = short_ref.shape[1]

    def pick(stacked, rows):
        out = stacked[0:rows]
        for g in range(1, groups):
            out = jnp.where(wide_group == g, stacked[g * rows : (g + 1) * rows], out)
        return out

    def joined_rows(s, m, lanes):
        rows_p = slice(m * prompt_len, (m + 1) * prompt_len)
        rows_c = slice(m * length, (m + 1) * length)
        joined = jnp.concatenate(
            [chosen_rows[s, rows_p, lanes].astype(F32), rows_in[s, rows_c, lanes].astype(F32)],
            axis=0,
        )
        factor = jnp.concatenate([fac_p[s, rows_p, :], fac_c[s, rows_c, :]], axis=0)
        return joined, factor

    def forward(s, carry):
        if direct:
            wait_pool(s)

            @pl.when(s + 1 < sections)
            def _():
                start_pool(s + 1)

        prompt_acc[...] = jnp.zeros_like(prompt_acc)
        loop(0, blocks, lambda block: choose(s, block))
        finish = start_stats(s, rows_to_line(stat_acc[...]), rows_to_line(prompt_acc[...]))
        loop(0, blocks, lambda block: build(s, block))
        sums = finish()
        fac_c[s] = lax.rsqrt(line_to_rows(sums[0]) * (1.0 / width) + 1e-06)
        fac_p[s] = lax.rsqrt(line_to_rows(sums[1]) * (1.0 / width) + 1e-06)
        stat_acc[...] = jnp.zeros_like(stat_acc)
        score_acc[...] = jnp.zeros_like(score_acc)

        def run(block, carry):
            lanes = lane_slice(block)
            wide = wide_slice(block)
            gain = gain_ref[s, :, lanes]
            short = short_ref[s, :, lanes]
            parts, lows, saved = [], [], []
            for m in range(micro):
                joined, factor = joined_rows(s, m, lanes)
                normed = joined * factor * gain
                shorter = normed * short[0:1]
                for j in range(1, tap_count):
                    moved = jnp.where(row_id >= j, pltpu.roll(normed, j, 0), 0.0)
                    shorter = shorter + moved * short[j : j + 1]
                high = shorter.astype(BF16)
                parts.append(high)
                lows.append((shorter - high.astype(F32)).astype(BF16))
                saved.append((joined[prompt_len:], normed[prompt_len:]))
            high = jnp.concatenate(parts, axis=1)
            short_out[s, :, wide] = high
            rhs = jnp.concatenate([high, jnp.concatenate(lows, axis=1), high], axis=0)
            base = pl.multiple_of(block * groups * length, groups * length)
            stacked = jnp.dot(
                toep[s, pl.ds(base, groups * length), :], rhs, preferred_element_type=F32
            )
            longer_all = pick(stacked, length)
            for m in range(micro):
                rows = slice(m * length, (m + 1) * length)
                longer = longer_all[:, m * LANES : (m + 1) * LANES]
                long_out[s, rows, lanes] = longer
                mixed = (saved[m][0] + saved[m][1] * longer).astype(BF16)
                rows_in[s + 1, rows, lanes] = mixed
                mixed = mixed.astype(F32)
                stat_acc[rows, :] += mixed * mixed
                score_acc[rows, :] += mixed * head_ref[0:1, head_slice(block)]
            return carry

        lax.fori_loop(0, blocks, run, 0)

        return carry

    lax.fori_loop(0, sections, forward, 0)

    live = []
    for m in range(micro):
        count = jnp.full((length, LANES), length_ref[m, 0], jnp.int32)
        live.append(jnp.where(t_row < count, 1.0, 0.0) / jnp.sqrt(count.astype(F32)))
    tile_rows = []
    for m in range(micro):
        rows = slice(m * length, (m + 1) * length)
        line = jnp.sum(score_acc[rows, :] * live[m], axis=0, keepdims=True)
        tile_rows.append(jnp.broadcast_to(jnp.sum(line, axis=1, keepdims=True), (1, LANES)))
    tile_rows.append(jnp.zeros((8 - micro, LANES), F32))
    score_tile = jnp.concatenate(tile_rows, axis=0)
    own_score = start_stats(sections, score_tile, score_tile)()[0]
    score_ref[...] = own_score
    resp_out[...] = own_score
    swap("resp", n_resp, me_resp, resp_out, resp_in, resp_sems)()
    winner, loser = ends_ref[0], ends_ref[1]

    def signs(r):
        return jnp.where(winner == r, 1.0, 0.0) - jnp.where(loser == r, 1.0, 0.0)

    margin = lax.fori_loop(
        0, n_resp, lambda r, acc: acc + resp_in[r] * signs(r), jnp.zeros((8, LANES), F32)
    )
    weight = 1.0 / (1.0 + jnp.exp(margin))
    slopes = -jnp.sum(signs(me_resp) * weight, axis=1, keepdims=True)

    def seed(block, carry):
        lanes = lane_slice(block)
        for m in range(micro):
            rows = slice(m * length, (m + 1) * length)
            upstream[rows, lanes] = live[m] * slopes[m : m + 1] * head_ref[0:1, head_slice(block)]
        return carry

    lax.fori_loop(0, blocks, seed, 0)

    keep_pair = total - 1 - s_lane <= prompt_len + t_row
    reverse = (
        lax.broadcasted_iota(jnp.int32, (total, total), 0)
        + lax.broadcasted_iota(jnp.int32, (total, total), 1)
        == total - 1
    )
    reverse = jnp.where(reverse, 1.0, 0.0).astype(BF16)

    share = 2 * blocks // n_resp

    def part_slice(r):
        return pl.ds(r * share, share)

    def part_steps(s, action):
        def each(step):
            peer = lax.rem(me_resp + step, n_resp)
            action(
                pltpu.make_async_remote_copy(
                    src_ref=tiles_own.at[s, part_slice(peer)],
                    dst_ref=tiles_in.at[s, me_resp],
                    send_sem=part_sems.at[0, s, step],
                    recv_sem=part_sems.at[1, s, step],
                    device_id={"resp": peer},
                    device_id_type=MESH,
                )
            )

        loop(1, n_resp, each)

    def tile_copy(s, step, k, r):
        return pltpu.make_async_remote_copy(
            src_ref=tiles_sum.at[s],
            dst_ref=tiles_all.at[k, r],
            send_sem=tile_send.at[s, step],
            recv_sem=tile_recv.at[k, r],
            device_id={"section": s, "resp": lax.rem(me_resp + step, n_resp)},
            device_id_type=MESH,
        )

    def tile_steps(s, action):
        def each(step):
            @pl.when(jnp.logical_not((s == me) & (step == 0)))
            def _():
                action(tile_copy(s, step, me, me_resp))

        loop(0, n_resp, each)

    def backward(step, carry):
        s = sections - 1 - step
        stat_acc[...] = jnp.zeros_like(stat_acc)

        def run(block, carry):
            lanes = lane_slice(block)
            wide = wide_slice(block)
            gain = gain_ref[s, :, lanes]
            short = short_ref[s, :, lanes]
            parts, saved = [], []
            for m in range(micro):
                rows = slice(m * length, (m + 1) * length)
                joined, factor = joined_rows(s, m, lanes)
                scaled = joined * factor
                normed = scaled * gain
                above = upstream[rows, lanes]
                parts.append((above * normed[prompt_len:]).astype(BF16))
                saved.append((joined[prompt_len:], scaled, normed, above))
            d_long = jnp.concatenate(parts, axis=1)
            base = pl.multiple_of(block * groups * total, groups * total)
            stacked = jnp.dot(
                toep_t[s, pl.ds(base, groups * total), :][:, :length],
                d_long,
                preferred_element_type=F32,
            )
            d_short_all = pick(stacked, total)
            turned = jnp.dot(reverse, short_out[s, :, wide], preferred_element_type=F32)
            d_wide = d_long.astype(F32)
            masked = jnp.concatenate(
                [
                    jnp.where(wide_group == g, d_wide, 0.0).astype(BF16)
                    for g in range(groups)
                ],
                axis=0,
            )
            pairs = lax.dot_general(
                masked,
                turned.astype(BF16),
                (((1,), (1,)), ((), ())),
                preferred_element_type=F32,
            )
            lines = []
            for g in range(groups):
                one = jnp.where(keep_pair, pairs[g * length : (g + 1) * length], 0.0)
                one = pltpu.roll(one, LANES + 1 - length, 1, stride=1, stride_axis=0)
                lines.append(jnp.sum(one, axis=0, keepdims=True))
            tiles_own[s, 2 * block + 1] = jnp.concatenate(lines, axis=0)
            grads = [jnp.zeros((1, LANES), F32)] * (tap_count + 1)
            for m in range(micro):
                rows = slice(m * length, (m + 1) * length)
                joined_c, scaled, normed, above = saved[m]
                d_short = d_short_all[:, m * LANES : (m + 1) * LANES]
                d_normed = d_short * short[0:1]
                grads[1] = grads[1] + jnp.sum(d_short * normed, axis=0, keepdims=True)
                for j in range(1, tap_count):
                    moved = jnp.where(
                        row_id < total - j, pltpu.roll(d_short, total - j, 0), 0.0
                    )
                    d_normed = d_normed + moved * short[j : j + 1]
                    grads[1 + j] = grads[1 + j] + jnp.sum(
                        moved * normed, axis=0, keepdims=True
                    )
                direct = above * long_out[s, rows, lanes]
                d_normed = jnp.concatenate(
                    [d_normed[:prompt_len], d_normed[prompt_len:] + direct], axis=0
                )
                grads[0] = grads[0] + jnp.sum(d_normed * scaled, axis=0, keepdims=True)
                inner = d_normed[prompt_len:] * gain
                partial[rows, lanes] = inner
                stat_acc[rows, :] += inner * joined_c
            tiles_own[s, 2 * block] = jnp.concatenate(grads, axis=0)
            return carry

        lax.fori_loop(0, blocks, run, 0)

        if direct:
            part_steps(s, lambda copy: copy.start())
            parts_in = tiles_in.at[s]
            parts_in[me_resp] = tiles_own[s, part_slice(me_resp)]

        @pl.when(s > 0)
        def _():
            line = rows_to_line(stat_acc[...])
            all_sums = start_stats(sections + 1 + step, line, line)()[0]
            factor = fac_c[s]
            pull = line_to_rows(all_sums) * (1.0 / width) * factor * factor * factor

            def finish(block, carry):
                lanes = lane_slice(block)
                grad = (
                    upstream[:, lanes]
                    + factor * partial[:, lanes]
                    - rows_in[s, :, lanes].astype(F32) * pull
                )
                upstream[:, lanes] = grad.astype(BF16).astype(F32)
                return carry

            lax.fori_loop(0, blocks, finish, 0)

        if direct:
            part_steps(s, lambda copy: copy.wait())
            tiles_sum[s] = jnp.sum(tiles_in[s], axis=0)

            @pl.when(s == me)
            def _():
                tiles_all[me, me_resp] = tiles_sum[s]

            tile_steps(s, lambda copy: copy.start())

        return carry

    lax.fori_loop(0, sections, backward, 0)

    if direct:
        loop(0, sections, lambda s: tile_steps(s, lambda copy: copy.wait_send()))

        def arrive(step):
            k, r = step // n_resp, step % n_resp

            @pl.when(jnp.logical_not((k == me) & (r == me_resp)))
            def _():
                tile_copy(0, 0, k, r).wait_recv()

        loop(0, sections * n_resp, arrive)
        gain_out, taps_short_out, taps_long_out = outs
        per_line = LANES // groups
        for line in range(sections * blocks // per_line):
            lines = []
            for place in range(per_line):
                block = line * per_line + place
                lanes = slice(block * LANES, (block + 1) * LANES)
                owner, local = divmod(2 * block, 2 * blocks)
                first, second = (divmod(local + kind, share) for kind in range(2))
                tile = tiles_all[owner, first[0], first[1]]
                gain_out[:, lanes] = tile[0:1]
                taps_short_out[:, lanes] = tile[1:]
                lines.append(tiles_all[owner, second[0], second[1]])
            lanes = slice(line * LANES, (line + 1) * LANES)
            taps_long_out[:, lanes] = jnp.transpose(jnp.concatenate(lines, axis=0))
    else:
        outs[0][...] = tiles_own[...]


def run_kernel(dims, direct, *arrays):
    sections, n_resp, micro, length, prompt_len, chans, per_group, width = dims
    rows = micro * length
    total = prompt_len + length
    group_total = chans // per_group
    tile = (8, LANES)
    tiles = 2 * chans // LANES
    share = tiles // n_resp if direct else 1
    ranks = n_resp if direct else 1
    vmem = pl.BlockSpec(memory_space=pltpu.VMEM)
    hbm = pl.BlockSpec(memory_space=pl.ANY)
    smem = pl.BlockSpec(memory_space=pltpu.SMEM)
    tap_count = arrays[3].shape[0]
    if direct:
        out_shapes = [(1, width), (tap_count, width), (LANES, width // per_group)]
    else:
        out_shapes = [(sections, tiles) + tile]
    return pl.pallas_call(
        functools.partial(kernel, dims, direct),
        out_shape=(
            jax.ShapeDtypeStruct(tile, F32),
            *(jax.ShapeDtypeStruct(shape, F32) for shape in out_shapes),
        ),
        in_specs=[hbm, hbm if direct else vmem, hbm, hbm, hbm, smem, vmem, vmem, smem],
        out_specs=(vmem,) * (1 + len(out_shapes)),
        scratch_shapes=[
            pltpu.VMEM((sections, group_total * length, 3 * LANES), BF16),
            pltpu.VMEM((sections, group_total * total, LANES), BF16),
            pltpu.VMEM((sections, ranks, prompt_len, chans), BF16),
            pltpu.VMEM((sections, micro * prompt_len, chans), BF16),
            pltpu.VMEM((sections, 1, chans), F32),
            pltpu.VMEM((sections, tap_count, chans), F32),
            pltpu.VMEM((sections, group_total, 2 * LANES), F32),
            pltpu.VMEM((sections + 1, rows, chans), BF16),
            pltpu.VMEM((sections, total, micro * chans), BF16),
            pltpu.VMEM((sections, rows, chans), F32),
            pltpu.VMEM((sections, micro * prompt_len, LANES), F32),
            pltpu.VMEM((sections, rows, LANES), F32),
            pltpu.VMEM((rows, chans), F32),
            pltpu.VMEM((rows, chans), F32),
            pltpu.VMEM((rows, LANES), F32),
            pltpu.VMEM((rows, LANES), F32),
            pltpu.VMEM((micro * prompt_len, LANES), F32),
            pltpu.VMEM((2 * sections, 2) + tile, F32),
            pltpu.VMEM((2 * sections, sections, 2) + tile, F32),
            pltpu.VMEM(tile, F32),
            pltpu.VMEM((n_resp,) + tile, F32),
            pltpu.VMEM((sections, tiles) + tile, F32),
            pltpu.VMEM((sections, ranks, share) + tile, F32),
            pltpu.VMEM((sections, share) + tile, F32),
            pltpu.VMEM((sections, ranks, share) + tile, F32),
            pltpu.SemaphoreType.DMA((5,)),
            pltpu.SemaphoreType.DMA((2, 3, sections)),
            pltpu.SemaphoreType.DMA((2, sections)),
            pltpu.SemaphoreType.DMA((2, sections, ranks)),
            pltpu.SemaphoreType.DMA((2 * sections, 2, sections)),
            pltpu.SemaphoreType.DMA((2, n_resp)),
            pltpu.SemaphoreType.DMA((2, sections, ranks)),
            pltpu.SemaphoreType.DMA((sections, ranks)),
            pltpu.SemaphoreType.DMA((sections, ranks)),
        ],
        compiler_params=pltpu.CompilerParams(
            has_side_effects=True, vmem_limit_bytes=56 * 1024 * 1024
        ),
    )(*arrays)


def body(
    completion_rows,
    prompt_pool,
    norm_gain,
    short_taps,
    long_taps,
    score_head,
    live_lengths,
    prompt_owner,
    pair_index,
):
    sections = lax.axis_size("section")
    n_resp = lax.axis_size("resp")
    me_resp = lax.axis_index("resp")
    micro, _, length, width = completion_rows.shape
    prompt_len = prompt_pool.shape[2]
    chans = width // sections
    tap_len, group_all = long_taps.shape[1:]
    per_group = width // group_all
    dims = (sections, n_resp, micro, length, prompt_len, chans, per_group, width)

    tiles = 2 * chans // LANES
    direct = n_resp <= 8 and tiles % n_resp == 0

    taps = long_taps[0].T
    flipped = jnp.concatenate([taps[:, :1], taps[:, :0:-1]], axis=1)
    taps = jnp.concatenate([flipped, taps], axis=1)
    prompts = prompt_pool[0, 0]
    if not direct:
        split = prompts.reshape(prompt_len, sections, chans).transpose(1, 0, 2)
        split = lax.all_to_all(split, "section", 0, 0, tiled=True)
        here = (prompt_owner == me_resp)[None, :, None, None]
        split = lax.psum(jnp.where(here, split[:, None], jnp.zeros((), BF16)), "resp")
        prompts = split.reshape(sections, micro * prompt_len, chans)
    rows = completion_rows.reshape(micro * length, width)
    head = score_head[None]

    ends = jnp.pad(
        pair_index.transpose(2, 0, 1),
        ((0, 0), (0, 8 - micro), (0, LANES - pair_index.shape[1])),
        constant_values=-1,
    )
    scores, *grads = run_kernel(
        dims,
        direct,
        rows,
        prompts,
        norm_gain,
        short_taps[0],
        taps,
        prompt_owner,
        head,
        ends,
        live_lengths,
    )
    scores = scores[:micro, :1].astype(BF16)
    if direct:
        return (scores, grads[0], grads[1][None], grads[2][None])
    grads = lax.psum(grads[0], "resp")
    grads = lax.all_to_all(grads, "section", 0, 0, tiled=True)
    grads = grads.reshape(sections * tiles // 2, 2, 8, LANES)
    gs_grad = grads[:, 0].transpose(1, 0, 2).reshape(8, width)
    taps_grad = grads[:, 1].reshape(group_all, tap_len).T
    return (
        scores,
        gs_grad[:1],
        gs_grad[None, 1:],
        taps_grad[None],
    )


SIDE = 8


def wide_kernel(
    dims,
    comp_hbm,
    prompt_hbm,
    gain_hbm,
    short_hbm,
    taps_hbm,
    head_hbm,
    owner_ref,
    pair_ref,
    length_ref,
    score_ref,
    short_grad_out,
    long_grad_out,
    comp_full,
    prompt_full,
    taps_full,
    head_own,
    comp_in,
    staged,
    pool,
    gain_in,
    short_in,
    taps_src,
    taps_in,
    order_c,
    order_p,
    lined,
    first_out,
    first_in,
    stat_out,
    stat_in,
    rows_in,
    prompt_rows,
    long_out,
    short_out,
    toep,
    toep_p,
    toep_t,
    params,
    heads,
    fac_c,
    fac_p,
    normed_buf,
    d_short_buf,
    upstream,
    inner_buf,
    d_long_buf,
    acc_ref,
    scales,
    tiles_own,
    short_own,
    long_own,
    local_sem,
    comp_send,
    comp_recv,
    weight_send,
    weight_recv,
    pool_send,
    pool_recv,
    pool_own,
    spread_send,
    spread_recv,
    first_send,
    first_recv,
    stat_send,
    stat_recv,
    part_send,
    part_recv,
):
    sections, n_resp, micro, length, chans, per_group, width = dims
    comps = micro * n_resp
    ranks = sections * n_resp
    blocks = chans // LANES
    per_block = LANES // per_group
    groups = blocks * per_block
    tap_count = short_in.shape[1]
    total = 2 * length
    me = lax.axis_index("section")
    me_resp = lax.axis_index("resp")
    rank = me * n_resp + me_resp

    def loop(low, high, step_of):
        def run(index, carry):
            step_of(index)
            return carry

        lax.fori_loop(low, high, run, 0)

    def lockstep(low, high, count, step_of):
        def run(index, carry):
            live = [step_of(index * count + k, k) for k in range(count)]
            while live:
                live = [step for step in live if next(step, 0) is None]
            return carry

        lax.fori_loop(low // count, high // count, run, 0)

    def add_up(values):
        while len(values) > 1:
            values = [a + b for a, b in zip(values[::2], values[1::2])] + (
                values[-1:] if len(values) % 2 else []
            )
        return values[0]

    def place(peer):
        return {"section": peer // n_resp, "resp": lax.rem(peer, n_resp)}

    def lanes_of(peer):
        return pl.ds(pl.multiple_of(peer * chans, chans), chans)

    def groups_of(peer):
        return pl.ds(pl.multiple_of(peer * groups, groups), groups)

    def remote(src, dst, send_sem, recv_sem, device):
        return pltpu.make_async_remote_copy(
            src_ref=src,
            dst_ref=dst,
            send_sem=send_sem,
            recv_sem=recv_sem,
            device_id=device,
            device_id_type=MESH,
        )

    load_comp = pltpu.make_async_copy(comp_hbm, comp_full, local_sem.at[0])
    load_prompt = pltpu.make_async_copy(prompt_hbm, prompt_full, local_sem.at[1])
    load_taps = pltpu.make_async_copy(taps_hbm, taps_full, local_sem.at[2])
    load_head = pltpu.make_async_copy(head_hbm.at[:, lanes_of(rank)], head_own, local_sem.at[3])
    own_comp = pltpu.make_async_copy(
        comp_hbm.at[:, lanes_of(rank)], comp_in.at[me_resp], local_sem.at[4]
    )
    own_stage = pltpu.make_async_copy(
        prompt_hbm.at[:, pl.ds(pl.multiple_of(me * n_resp * chans, n_resp * chans), n_resp * chans)],
        staged.at[me],
        local_sem.at[5],
    )
    own_gain = pltpu.make_async_copy(
        gain_hbm.at[:, lanes_of(rank)], gain_in.at[me], local_sem.at[6]
    )
    own_short = pltpu.make_async_copy(
        short_hbm.at[:, :, lanes_of(rank)], short_in.at[me], local_sem.at[7]
    )

    def comp_copy(step):
        peer_resp = lax.rem(me_resp + step, n_resp)
        return remote(
            comp_hbm.at[:, lanes_of(me * n_resp + peer_resp)],
            comp_in.at[me_resp],
            comp_send.at[step],
            comp_recv.at[me_resp],
            {"resp": peer_resp},
        )

    def comp_wait(step):
        source = lax.rem(me_resp + step, n_resp)
        remote(
            comp_hbm.at[:, lanes_of(rank)],
            comp_in.at[source],
            comp_send.at[step],
            comp_recv.at[source],
            {"resp": source},
        ).wait_recv()

    def weight_parts(peer_rank, source):
        return (
            (gain_hbm.at[:, lanes_of(peer_rank)], gain_in.at[source]),
            (short_hbm.at[:, :, lanes_of(peer_rank)], short_in.at[source]),
            (taps_src.at[groups_of(peer_rank), :], taps_in.at[source]),
        )

    def weight_copy(kind, step):
        peer = lax.rem(me + step, sections)
        src, dst = weight_parts(peer * n_resp + me_resp, me)[kind]
        return remote(
            src, dst, weight_send.at[kind, step], weight_recv.at[kind, me], {"section": peer}
        )

    def weight_wait(kind, step):
        source = lax.rem(me + step, sections)
        src, dst = weight_parts(rank, source)[kind]
        remote(
            src,
            dst,
            weight_send.at[kind, step],
            weight_recv.at[kind, source],
            {"section": source},
        ).wait_recv()

    def far_lanes(peer):
        span = n_resp * chans
        return pl.ds(pl.multiple_of(peer * span, span), span)

    def spread_copy(step):
        peer = lax.rem(me + step, sections)
        return remote(
            prompt_hbm.at[:, far_lanes(peer)],
            staged.at[me],
            spread_send.at[step],
            spread_recv.at[me],
            {"section": peer},
        )

    def spread_wait(s):
        remote(
            prompt_hbm.at[:, far_lanes(me)],
            staged.at[s],
            spread_send.at[0],
            spread_recv.at[s],
            {"section": s},
        ).wait_recv()

    def pool_copy(s, step):
        peer = lax.rem(me_resp + step, n_resp)
        return remote(
            staged.at[s, :, pl.ds(pl.multiple_of(peer * chans, chans), chans)],
            pool.at[s, me_resp],
            pool_send.at[s, step],
            pool_recv.at[s, me_resp],
            {"resp": peer},
        )

    def own_pool(s):
        return pltpu.make_async_copy(
            staged.at[s, :, pl.ds(pl.multiple_of(me_resp * chans, chans), chans)],
            pool.at[s, me_resp],
            pool_own.at[s],
        )

    def start_pool(s):
        @pl.when(s == me)
        def _():
            own_stage.wait()

        @pl.when(s != me)
        def _():
            spread_wait(s)

        loop(1, n_resp, lambda step: pool_copy(s, step).start())
        own_pool(s).start()

    def pool_wait(s):
        def each(step):
            source = lax.rem(me_resp + step, n_resp)
            remote(
                pool.at[s, source],
                pool.at[s, source],
                pool_send.at[s, step],
                pool_recv.at[s, source],
                {"resp": source},
            ).wait_recv()

        loop(1, n_resp, each)
        own_pool(s).wait()

    def first_copy(step):
        peer = lax.rem(rank + step, ranks)
        return remote(
            first_out, first_in.at[rank], first_send.at[step], first_recv.at[rank], place(peer)
        )

    def first_wait(step):
        source = lax.rem(rank + step, ranks)
        remote(
            first_out,
            first_in.at[source],
            first_send.at[step],
            first_recv.at[source],
            place(source),
        ).wait_recv()

    peers = []
    for j in range(1, n_resp):
        hop = jnp.where(me_resp * 2 < n_resp, n_resp - j, j)
        peer_resp = lax.rem(me_resp + hop, n_resp)
        peers += [(lax.rem(me + k, sections), peer_resp) for k in range(sections)]
    peers += [(lax.rem(me + k, sections), me_resp) for k in range(1, sections)]

    def stat_start(slot, tile):
        stat_out[slot] = tile
        for peer, peer_resp in peers:
            remote(
                stat_out.at[slot],
                stat_in.at[slot, rank],
                stat_send.at[slot],
                stat_recv.at[slot],
                {"section": peer, "resp": peer_resp},
            ).start()
        stat_in[slot, rank] = tile

    def stat_wait(slot, sem):
        bulk = stat_in.at[slot, pl.ds(0, ranks - 1)]
        pltpu.make_async_copy(bulk, bulk, sem.at[slot]).wait()

    def stat_finish(slot):
        stat_wait(slot, stat_recv)
        return jnp.sum(stat_in[slot], axis=0)

    def result_parts(s):
        return (
            (short_own.at[s], short_grad_out.at[:, :, lanes_of(rank)]),
            (long_own.at[s], long_grad_out.at[groups_of(rank), :]),
        )

    def result_own(s, kind):
        src, dst = result_parts(s)[kind]
        return pltpu.make_async_copy(src, dst, local_sem.at[8 + kind])

    def result_start(s):
        def each(step):
            @pl.when(jnp.logical_not((s == me) & (step == 0)))
            def _():
                for kind, (src, dst) in enumerate(result_parts(s)):
                    remote(
                        src,
                        dst,
                        part_send.at[kind],
                        part_recv.at[kind],
                        {"section": s, "resp": lax.rem(me_resp + step, n_resp)},
                    ).start()

        loop(0, n_resp, each)

        @pl.when(s == me)
        def _():
            for kind in range(2):
                result_own(s, kind).start()

    def result_wait(sem):
        for kind, bulk in enumerate(
            (
                short_grad_out.at[:, :, pl.ds(0, (ranks - 1) * chans)],
                long_grad_out.at[pl.ds(0, (ranks - 1) * groups), :],
            )
        ):
            pltpu.make_async_copy(bulk, bulk, sem.at[kind]).wait()

    for copy in (load_taps, load_comp, load_prompt, load_head):
        copy.start()
    for copy in (own_comp, own_stage, own_gain, own_short):
        copy.start()
    barrier = pltpu.get_barrier_semaphore()
    loop(
        1,
        ranks,
        lambda step: pl.semaphore_signal(
            barrier,
            inc=1,
            device_id=place(lax.rem(rank + step, ranks)),
            device_id_type=MESH,
        ),
    )

    tile_row = lax.broadcasted_iota(jnp.int32, (LANES, LANES), 0)
    tile_lane = lax.broadcasted_iota(jnp.int32, (LANES, LANES), 1)
    row_target = (tile_row // per_group) * LANES + tile_row % per_group
    prompt_key = (tile_lane // (n_resp * per_group)) * (n_resp * per_group) + (
        tile_lane % per_group
    )

    def fill_order(c):
        rows = pl.ds(pl.multiple_of(c * LANES, LANES), LANES)
        for n in range(per_block):
            hit = row_target + c * per_group == tile_lane + n * LANES
            order_c[rows, n * LANES : (n + 1) * LANES] = jnp.where(hit, 1.0, 0.0).astype(BF16)

    loop(0, comps, fill_order)
    for m in range(micro):
        for n in range(per_block):
            hit = row_target + m * n_resp * per_group == prompt_key + n * LANES
            order_p[m * LANES : (m + 1) * LANES, n * LANES : (n + 1) * LANES] = jnp.where(
                hit, 1.0, 0.0
            ).astype(BF16)
    pad = 8
    for g in range(groups):
        normed_buf[g, :pad] = jnp.zeros((pad, LANES), F32)
        for s in range(sections):
            d_short_buf[s, g, total:] = jnp.zeros((pad, LANES), F32)

    load_taps.wait()
    upright = jnp.transpose(taps_full[...])
    mirror = jnp.where(lax.rem(tile_row + tile_lane, LANES) == 0, 1.0, 0.0)
    taps_src[:, :LANES] = jnp.dot(
        upright, mirror, preferred_element_type=F32, precision=lax.Precision.HIGHEST
    )
    taps_src[:, LANES:] = upright

    ones = jnp.ones((16, 2 * LANES), BF16)

    def split(values):
        high = values.astype(BF16)
        return high, (values - high.astype(F32)).astype(BF16)

    def lane_sums(acc, weights, below=None):
        if acc.shape[0] < LANES:
            rest = [] if below is None else [below]
            rows = LANES - acc.shape[0] - sum(block.shape[0] for block in rest)
            acc = jnp.concatenate([acc] + rest + [jnp.zeros((rows, LANES), F32)], axis=0)
        both = jnp.concatenate(split(acc), axis=1)
        return lax.dot_general(
            weights, both, (((1,), (1,)), ((), ())), preferred_element_type=F32
        )[:8]

    def square_rows(ref):
        def step(block, acc):
            values = ref[:, pl.ds(pl.multiple_of(block * LANES, LANES), LANES)].astype(F32)
            return acc + values * values

        return lax.fori_loop(
            0, width // LANES, step, jnp.zeros((ref.shape[0], LANES), F32), unroll=2
        )

    load_comp.wait()
    comp_line = lane_sums(square_rows(comp_full), ones)
    load_prompt.wait()
    prompt_line = lane_sums(square_rows(prompt_full), ones)
    eight_row = lax.broadcasted_iota(jnp.int32, (8, LANES), 0)
    eight_lane = lax.broadcasted_iota(jnp.int32, (8, LANES), 1)
    message = jnp.where(eight_row == 0, comp_line, prompt_line)
    for m in range(micro):
        count = jnp.full((8, LANES), length_ref[0, m], jnp.int32).astype(F32)
        message = jnp.where(eight_row == 2 + m, count, message)
    first_out[...] = message

    pl.semaphore_wait(barrier, ranks - 1)
    @pl.when(me == 0)
    def _():
        loop(1, sections, lambda step: spread_copy(step).start())

    loop(1, n_resp, lambda step: comp_copy(step).start())
    loop(1, sections, lambda step: weight_copy(2, step).start())

    loop(1, ranks, lambda step: first_copy(step).start())

    def start_vectors(step):
        weight_copy(0, step).start()
        weight_copy(1, step).start()

    loop(1, sections, start_vectors)
    @pl.when(me != 0)
    def _():
        loop(1, sections, lambda step: spread_copy(step).start())

    first_in[rank] = message
    taps_in[me] = taps_src[groups_of(rank), :]

    own_gain.wait()
    own_short.wait()
    load_head.wait()

    def weights_arrive(step):
        for kind in range(3):
            weight_wait(kind, step)

    loop(1, sections, weights_arrive)

    def tile_lanes(values, n):
        out = pltpu.roll(values, (LANES - n * per_group) % LANES, 1)
        out = jnp.where(eight_lane < per_group, out, 0.0)
        span = per_group
        while span < LANES:
            out = out + pltpu.roll(out, span, 1)
            span *= 2
        return out

    t_row = lax.broadcasted_iota(jnp.int32, (length, LANES), 0)
    s_lane = lax.broadcasted_iota(jnp.int32, (length, LANES), 1)
    keep = s_lane <= length + t_row
    keep_t = tile_row <= length + tile_lane

    def spread_params(s):
        for b in range(blocks):
            lanes = slice(b * LANES, (b + 1) * LANES)
            rows = jnp.concatenate(
                [gain_in[s, :, lanes]] + [short_in[s, j, :, lanes] for j in range(tap_count)],
                axis=0,
            )
            for n in range(per_block):
                params[s, b * per_block + n] = tile_lanes(rows, n)

    loop(0, sections, spread_params)
    for b in range(blocks):
        rows = jnp.broadcast_to(head_own[:, b * LANES : (b + 1) * LANES], (8, LANES))
        for n in range(per_block):
            heads[b * per_block + n] = tile_lanes(rows, n)

    def build(s, g, k):
        line = taps_in[s, pl.ds(g, 1), :]
        wide = jnp.broadcast_to(line[:, :LANES], (length, LANES))
        wide = pltpu.roll(wide, length, 1, stride=1, stride_axis=0)
        wide_t = jnp.broadcast_to(line[:, LANES:], (total, LANES))
        wide_t = pltpu.roll(wide_t, length, 1, stride=1, stride_axis=0)
        yield
        wide = jnp.where(keep, wide, 0.0)
        high = wide.astype(BF16).astype(F32)
        low = wide - high
        low_turned = pltpu.roll(low, length, 1)
        high_turned = pltpu.roll(high, length, 1)
        toep_t[s, g] = jnp.where(keep_t, wide_t, 0.0).astype(BF16)
        yield
        first = s_lane < length
        toep_p[s, g] = jnp.where(first, high, low_turned).astype(BF16)
        toep[s, g] = jnp.where(first, high_turned, low).astype(BF16)

    start_pool(0)
    def build_section(s):
        lockstep(0, groups, 4, lambda g, k: build(s, g, k))

    build_section(0)

    def spread_rows(lines):
        tall = jnp.concatenate(
            [jnp.broadcast_to(lines[c : c + 1], (per_group, LANES)) for c in range(comps)],
            axis=0,
        )
        return jnp.transpose(tall)[:length]

    def to_factor(sums):
        return lax.rsqrt(sums * (1.0 / width) + 1e-06)

    loop(1, ranks, first_wait)
    own_lines = jnp.concatenate(
        [first_in[me * n_resp + r, 0:1] for r in range(n_resp)], axis=0
    )
    own_lines = jnp.concatenate(
        [
            own_lines if m == 0 else pltpu.roll(own_lines, LANES - m * length, 1)
            for m in range(micro)
        ],
        axis=0,
    )
    fac_c[0] = spread_rows(to_factor(own_lines))

    def prompt_factor(s):
        lines = []
        for m in range(micro):
            owner = jnp.full((8, LANES), owner_ref[m], jnp.int32)
            line = jnp.zeros((8, LANES), F32)
            for r in range(n_resp):
                line = jnp.where(owner == r, first_in[s * n_resp + r], line)
            lines += [line[1:2]] * n_resp
        fac_p[s] = spread_rows(to_factor(jnp.concatenate(lines, axis=0)))

    loop(0, sections, prompt_factor)

    def conv_short(ref, g, start, taps):
        out = ref[g, pl.ds(start, length)] * taps[1:2]
        for j in range(1, tap_count):
            out = out + ref[g, pl.ds(start - j, length)] * taps[1 + j : 2 + j]
        return out

    def conv_long(matrix, high, low):
        left = jnp.concatenate([matrix, matrix], axis=1)
        right = jnp.concatenate([high, high, low, low], axis=0)
        return jnp.dot(left, right, preferred_element_type=F32)

    def prepare(s):
        pool_wait(s)

        sides = []
        for b in range(blocks):
            lanes = slice(b * LANES, (b + 1) * LANES)
            row = []
            for m in range(micro):
                owner = jnp.full((length, LANES), owner_ref[m], jnp.int32)
                picked = pool[s, 0, :, lanes].astype(F32)
                for r in range(1, n_resp):
                    picked = jnp.where(owner == r, pool[s, r, :, lanes].astype(F32), picked)
                row.append(picked.astype(BF16))
            sides.append(jnp.concatenate(row, axis=1))
        side = jnp.concatenate(sides, axis=0)
        step = 2 * LANES
        for n in range(per_block // 2):
            part = jnp.dot(
                side, order_p[:, n * step : (n + 1) * step], preferred_element_type=F32
            ).astype(BF16)
            for b in range(blocks):
                for k in range(2):
                    prompt_rows[s, b * per_block + 2 * n + k] = part[
                        b * length : (b + 1) * length, k * LANES : (k + 1) * LANES
                    ]
        factor = fac_p[s]

        def each(g, k):
            taps = params[s, g]
            normed = prompt_rows[s, g].astype(F32) * factor * taps[0:1]
            normed_buf[g, pl.ds(pad, length)] = normed
            yield
            shorter = conv_short(normed_buf, g, pad, taps)
            high, low = split(shorter)
            short_out[s, g, :length] = high
            yield
            longer = conv_long(toep_p[s, g], high, low)
            yield
            long_out[s, g] = longer

        lockstep(0, groups, groups, each)

    loop(1, n_resp, comp_wait)
    start_pool(1)
    own_comp.wait()
    for b in range(blocks):
        lanes = slice(b * LANES, (b + 1) * LANES)
        for m in range(micro):
            for r in range(n_resp):
                c = m * n_resp + r
                lined[b * length : (b + 1) * length, c * LANES : (c + 1) * LANES] = comp_in[
                    r, m * length : (m + 1) * length, lanes
                ]
    for n in range(per_block // 2):
        step = 2 * LANES
        part = jnp.dot(
            lined[...], order_c[:, n * step : (n + 1) * step], preferred_element_type=F32
        ).astype(BF16)
        for b in range(blocks):
            for k in range(2):
                rows_in[0, b * per_block + 2 * n + k] = part[
                    b * length : (b + 1) * length, k * LANES : (k + 1) * LANES
                ]
    prepare(0)

    fold_row = lax.broadcasted_iota(jnp.int32, (16, 2 * LANES), 0)
    fold_lane = lax.broadcasted_iota(jnp.int32, (16, 2 * LANES), 1)
    fold = jnp.where((fold_lane % LANES) // per_group == fold_row, 1.0, 0.0).astype(BF16)

    def forward(s, last):
        acc_ref[...] = jnp.zeros_like(acc_ref)
        factor = fac_c[s]

        sums = []

        def each(g, k):
            taps = params[s, g]
            rows = rows_in[s, g].astype(F32)
            normed = rows * factor * taps[0:1]
            normed_buf[g, pl.ds(pad + length, length)] = normed
            yield
            shorter = conv_short(normed_buf, g, pad + length, taps)
            high, low = split(shorter)
            short_out[s, g, length:] = high
            yield
            longer = conv_long(toep[s, g], high, low)
            yield
            longer = long_out[s, g] + longer
            normed = normed_buf[g, pl.ds(pad + length, length)]
            mixed = (rows_in[s, g].astype(F32) + normed * longer).astype(BF16)
            sums.append((longer, mixed))
            yield
            longer, mixed = sums[k]
            long_out[s, g] = longer
            if not last:
                rows_in[s + 1, g] = mixed
            mixed = mixed.astype(F32)
            sums[k] = mixed * (heads[g, 0:1] if last else mixed)
            yield
            if k == groups - 1:
                acc_ref[...] += add_up(sums)
                sums.clear()

        lockstep(0, groups, groups, each)

    def forward_step(s):
        forward(s, False)
        stat_start(s, lane_sums(acc_ref[...], fold))
        build_section(s + 1)
        prepare(s + 1)

        @pl.when(s + 2 < sections)
        def _():
            start_pool(s + 2)

        fac_c[s + 1] = spread_rows(to_factor(stat_finish(s)))

    loop(0, sections - 1, forward_step)
    forward(sections - 1, True)

    comp_lane = eight_lane // per_group
    counts = jnp.zeros((8, LANES), F32)
    for m in range(micro):
        for r in range(n_resp):
            row = first_in[me * n_resp + r, 2 + m : 3 + m]
            counts = jnp.where(comp_lane == m * n_resp + r, row, counts)
    alive = t_row.astype(F32) < counts[0:1]
    live = jnp.where(alive, 1.0, 0.0) / jnp.sqrt(counts[0:1])
    score_line = jnp.sum(acc_ref[...] * live, axis=0, keepdims=True)
    score_line = jnp.where(eight_row == 0, score_line, 0.0)

    def seed(g, k):
        upstream[sections - 1, g] = live * heads[g, 0:1]
        yield

    lockstep(0, groups, SIDE, seed)

    def backward(s, last):
        acc_ref[...] = jnp.zeros_like(acc_ref)
        factor = fac_c[s]

        sums = []

        def each(g, k):
            taps = params[s, g]
            rows = rows_in[s, g].astype(F32)
            d_long = (upstream[s, g] * (rows * factor * taps[0:1])).astype(BF16)
            yield
            d_long_buf[s, g] = d_long
            d_short = jnp.dot(
                toep_t[s, g][:, :length], d_long, preferred_element_type=F32
            )
            yield
            d_short_buf[s, g, pl.ds(0, total)] = d_short
            if last:
                return
            yield
            d_normed = upstream[s, g] * long_out[s, g]
            for j in range(tap_count):
                d_normed = d_normed + d_short_buf[s, g, pl.ds(length + j, length)] * taps[1 + j : 2 + j]
            inner = d_normed * taps[0:1]
            sums.append(inner)
            yield
            inner_buf[g] = sums[k]
            sums[k] = sums[k] * rows_in[s, g].astype(F32)
            yield
            if k == groups - 1:
                acc_ref[...] += add_up(sums)
                sums.clear()

        lockstep(0, groups, groups, each)

    keep_pair = total - 1 - s_lane <= length + t_row
    reverse = jnp.where(tile_row + tile_lane == total - 1, 1.0, 0.0).astype(BF16)

    def gradients(s):
        factor_c = fac_c[s]
        factor_p = fac_p[s]
        scale = scales[s, 0:1]
        tops, longs = [], []

        def each(g, k):
            turned = jnp.dot(reverse, short_out[s, g], preferred_element_type=F32)
            yield
            pairs = lax.dot_general(
                (d_long_buf[s, g].astype(F32) * scale).astype(BF16),
                turned.astype(BF16),
                (((1,), (1,)), ((), ())),
                preferred_element_type=F32,
            )
            yield
            taps = params[s, g]
            scaled_p = prompt_rows[s, g].astype(F32) * factor_p
            scaled_c = rows_in[s, g].astype(F32) * factor_c
            lines = [
                jnp.sum(upstream[s, g] * long_out[s, g] * scaled_c, axis=0, keepdims=True)
            ]
            for j in range(tap_count):
                part = (
                    d_short_buf[s, g, pl.ds(j, length)] * scaled_p
                    + d_short_buf[s, g, pl.ds(length + j, length)] * scaled_c
                )
                lines.append(jnp.sum(part, axis=0, keepdims=True))
            tile = jnp.concatenate(lines, axis=0) * scale
            yield
            pairs = jnp.where(keep_pair, pairs, 0.0)
            pairs = pltpu.roll(pairs, LANES + 1 - length, 1, stride=1, stride_axis=0)
            yield
            span = per_group
            while span < LANES:
                tile = tile + pltpu.roll(tile, span, 1)
                span *= 2
            yield
            top = tile + jnp.sum(
                jnp.where(eight_row > 0, tile * taps, 0.0), axis=0, keepdims=True
            )
            tops.append(jnp.where(eight_row == 0, top, tile * taps[0:1]))
            longs.append(jnp.sum(pairs, axis=0, keepdims=True))
            yield
            if k < SIDE - 1:
                return
            b, n = g // per_block, lax.rem(g, per_block)
            tile = tiles_own[b]
            for i in range(SIDE):
                tile = jnp.where(comp_lane == n - (SIDE - 1) + i, tops[i], tile)
            tiles_own[b] = tile
            long_own[s, pl.ds(pl.multiple_of(g - (SIDE - 1), SIDE), SIDE)] = jnp.concatenate(
                longs, axis=0
            )
            tops.clear()
            longs.clear()

        for b in range(blocks):
            tiles_own[b] = jnp.zeros((8, LANES), F32)
        lockstep(0, groups, SIDE, each)
        for b in range(blocks):
            tile = tiles_own[b]
            for j in range(1 + tap_count):
                short_own[s, j, :, b * LANES : (b + 1) * LANES] = tile[j : j + 1]
        result_start(s)

    def go_down(s, sums, scale):
        factor = fac_c[s]
        pull = spread_rows(sums * (1.0 / width)) * factor * factor * factor

        def finish(g, k):
            grad = upstream[s, g] + factor * inner_buf[g] - rows_in[s, g].astype(F32) * pull
            yield
            if scale is not None:
                grad = grad * scale
            upstream[s - 1, g] = grad.astype(BF16).astype(F32)

        lockstep(0, groups, groups, finish)

    last = sections - 1
    backward(last, False)
    stat_start(last, lane_sums(acc_ref[...], fold, score_line))
    loop(1, n_resp, lambda step: comp_copy(step).wait_send())

    def weights_sent(step):
        for kind in range(3):
            weight_copy(kind, step).wait_send()

    loop(1, sections, weights_sent)

    loop(1, ranks, lambda step: first_copy(step).wait_send())
    loop(1, sections, lambda step: spread_copy(step).wait_send())

    def pools_sent(s):
        loop(1, n_resp, lambda step: pool_copy(s, step).wait_send())

    loop(0, sections, pools_sent)
    winner = jnp.full((8, LANES), -1, jnp.int32)
    loser = winner
    for m in range(micro):
        for p in range(pair_ref.shape[2]):
            here = (eight_row == m) & (eight_lane == p)
            winner = jnp.where(here, pair_ref[m, 0, p], winner)
            loser = jnp.where(here, pair_ref[m, 1, p], loser)
    signs = [
        jnp.where(winner == r, 1.0, 0.0) - jnp.where(loser == r, 1.0, 0.0)
        for r in range(n_resp)
    ]
    masks = [comp_lane == eight_row * n_resp + r for r in range(n_resp)]
    sums = stat_finish(last)
    totals = jnp.sum(jnp.where(eight_lane == length, sums, 0.0), axis=1, keepdims=True)
    totals = jnp.broadcast_to(totals, (8, LANES))
    scores = []
    for r in range(n_resp):
        rows = totals[r : r + 1]
        for m in range(1, micro):
            rows = jnp.where(eight_row == m, totals[m * n_resp + r : m * n_resp + r + 1], rows)
        scores.append(jnp.broadcast_to(rows, (8, LANES)))
    own_score = scores[0]
    margin = jnp.zeros((8, LANES), F32)
    for r in range(n_resp):
        margin = margin + scores[r] * signs[r]
        own_score = jnp.where(me_resp == r, scores[r], own_score)
    score_ref[...] = own_score[:micro, :1].astype(BF16)
    weight = 1.0 / (1.0 + jnp.exp(margin))
    slopes = jnp.zeros((8, LANES), F32)
    for r in range(n_resp):
        slope = -jnp.sum(signs[r] * weight, axis=1, keepdims=True)
        slopes = jnp.where(masks[r], slope, slopes)
    slopes = jnp.sum(slopes, axis=0, keepdims=True)
    for s in range(sections - 1):
        scales[s] = jnp.ones((8, LANES), F32)
    scales[last] = jnp.broadcast_to(slopes, (8, LANES))
    go_down(last, sums, slopes)

    def backward_step(step):
        s = sections - 1 - step
        slot = last + step
        backward(s, False)
        stat_start(slot, lane_sums(acc_ref[...], fold))
        loop(s, jnp.where(step == 1, s + 2, s + 1), gradients)
        go_down(s, stat_finish(slot), None)

    loop(1, sections - 1, backward_step)
    backward(0, True)
    gradients(0)

    loop(0, 2 * sections - 2, lambda slot: stat_wait(slot, stat_send))
    for kind in range(2):
        result_own(me, kind).wait()
    result_wait(part_send)
    result_wait(part_recv)


def flush_kernel(score_in, short_in, long_in, score_ref, gain_ref, short_ref, long_ref):
    score_ref[...] = score_in[...]
    gain_ref[...] = short_in[0]
    short_ref[...] = short_in[1:]
    long_ref[...] = jnp.transpose(long_in[...])


def flush(scores, short_grad, long_grad):
    vmem = pl.BlockSpec(memory_space=pltpu.VMEM)
    rows, _, width = short_grad.shape
    return pl.pallas_call(
        flush_kernel,
        out_shape=(
            jax.ShapeDtypeStruct(scores.shape, BF16),
            jax.ShapeDtypeStruct((1, width), F32),
            jax.ShapeDtypeStruct((rows - 1, 1, width), F32),
            jax.ShapeDtypeStruct(long_grad.shape[::-1], F32),
        ),
        in_specs=[vmem] * 3,
        out_specs=(vmem,) * 4,
    )(scores, short_grad, long_grad)


def run_wide(dims, *arrays):
    sections, n_resp, micro, length, chans, per_group, width = dims
    comps = micro * n_resp
    ranks = sections * n_resp
    groups = chans // per_group
    blocks = chans // LANES
    total = 2 * length
    tap_count = arrays[3].shape[0]
    group_all = width // per_group
    tile = (8, LANES)
    vmem = pl.BlockSpec(memory_space=pltpu.VMEM)
    hbm = pl.BlockSpec(memory_space=pl.ANY)
    smem = pl.BlockSpec(memory_space=pltpu.SMEM)
    slots = 2 * sections - 2
    per = (sections, groups)
    dma = pltpu.SemaphoreType.DMA
    return pl.pallas_call(
        functools.partial(wide_kernel, dims),
        out_shape=(
            jax.ShapeDtypeStruct((micro, 1), BF16),
            jax.ShapeDtypeStruct((1 + tap_count, 1, width), F32),
            jax.ShapeDtypeStruct((group_all, LANES), F32),
        ),
        in_specs=[hbm] * 6 + [smem] * 3,
        out_specs=(vmem,) * 3,
        scratch_shapes=[
            pltpu.VMEM((micro * length, width), BF16),
            pltpu.VMEM((length, width), BF16),
            pltpu.VMEM((LANES, group_all), F32),
            pltpu.VMEM((1, chans), F32),
            pltpu.VMEM((n_resp, micro * length, chans), BF16),
            pltpu.VMEM((sections, length, n_resp * chans), BF16),
            pltpu.VMEM((sections, n_resp, length, chans), BF16),
            pltpu.VMEM((sections, 1, chans), F32),
            pltpu.VMEM((sections, tap_count, 1, chans), F32),
            pltpu.VMEM((group_all, 2 * LANES), F32),
            pltpu.VMEM((sections, groups, 2 * LANES), F32),
            pltpu.VMEM((comps * LANES, (LANES // per_group) * LANES), BF16),
            pltpu.VMEM((micro * LANES, (LANES // per_group) * LANES), BF16),
            pltpu.VMEM((blocks * length, comps * LANES), BF16),
            pltpu.VMEM(tile, F32),
            pltpu.VMEM((ranks,) + tile, F32),
            pltpu.VMEM((slots,) + tile, F32),
            pltpu.VMEM((slots, ranks) + tile, F32),
            pltpu.VMEM(per + (length, LANES), BF16),
            pltpu.VMEM(per + (length, LANES), BF16),
            pltpu.VMEM(per + (length, LANES), F32),
            pltpu.VMEM(per + (total, LANES), BF16),
            pltpu.VMEM(per + (length, LANES), BF16),
            pltpu.VMEM(per + (length, LANES), BF16),
            pltpu.VMEM(per + (total, LANES), BF16),
            pltpu.VMEM(per + tile, F32),
            pltpu.VMEM((groups,) + tile, F32),
            pltpu.VMEM((sections, length, LANES), F32),
            pltpu.VMEM((sections, length, LANES), F32),
            pltpu.VMEM((groups, 8 + total, LANES), F32),
            pltpu.VMEM(per + (total + 8, LANES), F32),
            pltpu.VMEM(per + (length, LANES), F32),
            pltpu.VMEM((groups, length, LANES), F32),
            pltpu.VMEM(per + (length, LANES), BF16),
            pltpu.VMEM((length, LANES), F32),
            pltpu.VMEM((sections,) + tile, F32),
            pltpu.VMEM((blocks,) + tile, F32),
            pltpu.VMEM((sections, 1 + tap_count, 1, chans), F32),
            pltpu.VMEM((sections, groups, LANES), F32),
            dma((10,)),
            dma((n_resp,)),
            dma((n_resp,)),
            dma((3, sections)),
            dma((3, sections)),
            dma((sections, n_resp)),
            dma((sections, n_resp)),
            dma((sections,)),
            dma((sections,)),
            dma((sections,)),
            dma((ranks,)),
            dma((ranks,)),
            dma((slots,)),
            dma((slots,)),
            dma((2,)),
            dma((2,)),
        ],
        compiler_params=pltpu.CompilerParams(
            collective_id=1, has_side_effects=True, vmem_limit_bytes=56 * 1024 * 1024
        ),
    )(*arrays)


def wide_body(
    completion_rows,
    prompt_pool,
    norm_gain,
    short_taps,
    long_taps,
    score_head,
    live_lengths,
    prompt_owner,
    pair_index,
):
    sections = lax.axis_size("section")
    n_resp = lax.axis_size("resp")
    micro, _, length, width = completion_rows.shape
    chans = width // (sections * n_resp)
    per_group = width // long_taps.shape[2]
    results = run_wide(
        (sections, n_resp, micro, length, chans, per_group, width),
        completion_rows.reshape(micro * length, width),
        prompt_pool[0, 0],
        norm_gain,
        short_taps.transpose(1, 0, 2),
        long_taps[0],
        score_head[None],
        prompt_owner,
        pair_index.transpose(0, 2, 1),
        live_lengths.T,
    )
    scores, gain_grad, short_grad, long_grad = flush(*results)
    return (
        scores,
        gain_grad,
        short_grad.transpose(1, 0, 2),
        long_grad[None],
    )


def is_wide(
    completion_rows,
    prompt_pool,
    norm_gain,
    short_taps,
    long_taps,
    score_head,
    live_lengths,
    prompt_owner,
    pair_index,
):
    sections = lax.axis_size("section")
    n_resp = lax.axis_size("resp")
    micro, _, length, width = completion_rows.shape
    per_group = width // long_taps.shape[2]
    return (
        micro * n_resp * per_group == LANES
        and micro * n_resp == 8
        and width % (sections * n_resp * LANES) == 0
        and prompt_pool.shape[2] == length
        and long_taps.shape[1] == 2 * length == LANES
        and micro * length == LANES
        and short_taps.shape[1] == 7
        and sections >= 3
    )


def either(*arrays):
    return wide_body(*arrays) if is_wide(*arrays) else body(*arrays)


def solution(mesh):
    placed = (
        P(None, ("groups", "resp"), None, None),
        P("section", ("groups", "resp"), None, None),
        P("section", None),
        P("section", None, None),
        P("section", None, None),
        P(),
        P(None, ("groups", "resp")),
        P("groups"),
        P(None, "groups", None),
    )
    return jax.shard_map(
        either,
        mesh=mesh,
        in_specs=placed,
        out_specs=(
            P(None, ("groups", "resp")),
            P("section", "groups"),
            P("section", "groups", None),
            P("section", "groups", None),
        ),
        check_vma=False,
    )
```

```python
import functools

import jax
import jax.numpy as jnp
from jax import lax
from jax.experimental import pallas as pl
from jax.experimental.pallas import tpu as pltpu
from jax.sharding import PartitionSpec as P

LANES = 128
MESH = pl.DeviceIdType.MESH
F32 = jnp.float32
BF16 = jnp.bfloat16


def rows_to_line(block):
    line = jnp.sum(jnp.transpose(block), axis=0, keepdims=True)
    return jnp.broadcast_to(line, (8, LANES))


def line_to_rows(tile):
    return jnp.transpose(jnp.broadcast_to(tile[0:1], (LANES, LANES)))


def kernel(
    dims,
    direct,
    comp_ref,
    prompt_ref,
    gain_hbm,
    short_hbm,
    taps_hbm,
    owner_ref,
    head_ref,
    ends_ref,
    length_ref,
    score_ref,
    *rest,
):
    sections, n_resp, micro, length, prompt_len, chans, per_group, width = dims
    outs, rest = (rest[:3], rest[3:]) if direct else (rest[:1], rest[1:])
    (
        toep,
        toep_t,
        pool,
        chosen_rows,
        gain_ref,
        short_ref,
        taps_ref,
        rows_in,
        short_out,
        long_out,
        fac_p,
        fac_c,
        upstream,
        partial,
        stat_acc,
        score_acc,
        prompt_acc,
        stat_out,
        stat_in,
        resp_out,
        resp_in,
        tiles_own,
        tiles_in,
        tiles_sum,
        tiles_all,
        local_sem,
        weight_sems,
        spread_sems,
        pool_sems,
        stat_sems,
        resp_sems,
        part_sems,
        tile_send,
        tile_recv,
    ) = rest
    groups = LANES // per_group
    blocks = chans // LANES
    group_rows = blocks * groups
    total = prompt_len + length
    me = lax.axis_index("section")
    me_resp = lax.axis_index("resp")
    own_lanes = pl.ds(pl.multiple_of(me * chans, chans), chans)

    def lane_slice(block):
        return pl.ds(pl.multiple_of(block * LANES, LANES), LANES)

    def head_slice(block):
        return pl.ds(pl.multiple_of(me * chans + block * LANES, LANES), LANES)

    def wide_slice(block):
        return pl.ds(pl.multiple_of(block * micro * LANES, LANES), micro * LANES)

    def loop(low, high, step_of):
        def run(index, carry):
            step_of(index)
            return carry

        lax.fori_loop(low, high, run, 0)

    def swap(axis, count, mine, out_ref, in_ref, sems):
        def copy(step):
            return pltpu.make_async_remote_copy(
                src_ref=out_ref,
                dst_ref=in_ref.at[mine],
                send_sem=sems.at[0, step],
                recv_sem=sems.at[1, step],
                device_id={axis: lax.rem(mine + step, count)},
                device_id_type=MESH,
            )

        loop(1, count, lambda step: copy(step).start())
        in_ref[mine] = out_ref[...]
        return lambda: loop(1, count, lambda step: copy(step).wait())

    def start_stats(slot, first, second):
        stat_out[slot, 0] = first
        stat_out[slot, 1] = second
        wait = swap(
            "section", sections, me, stat_out.at[slot], stat_in.at[slot], stat_sems.at[slot]
        )

        def finish():
            wait()
            return jnp.sum(stat_in[slot], axis=0)

        return finish

    def weight_copies(step):
        peer = lax.rem(me + step, sections)
        lanes = pl.ds(pl.multiple_of(peer * chans, chans), chans)
        rows = pl.ds(pl.multiple_of(peer * group_rows, group_rows), group_rows)
        return [
            pltpu.make_async_remote_copy(
                src_ref=source,
                dst_ref=target,
                send_sem=weight_sems.at[0, kind, step],
                recv_sem=weight_sems.at[1, kind, step],
                device_id={"section": peer},
                device_id_type=MESH,
            )
            for kind, source, target in (
                (0, gain_hbm.at[:, lanes], gain_ref.at[me]),
                (2, short_hbm.at[:, lanes], short_ref.at[me]),
                (1, taps_hbm.at[rows, :], taps_ref.at[me]),
            )
        ]

    def start_weights(step):
        for copy in weight_copies(step):
            copy.start()

    def wait_weights(step):
        for copy in weight_copies(step):
            copy.wait()

    own_rows = pl.ds(pl.multiple_of(me * group_rows, group_rows), group_rows)
    local_copies = [
        pltpu.make_async_copy(comp_ref.at[:, own_lanes], rows_in.at[0], local_sem.at[0]),
        pltpu.make_async_copy(gain_hbm.at[:, own_lanes], gain_ref.at[me], local_sem.at[1]),
        pltpu.make_async_copy(short_hbm.at[:, own_lanes], short_ref.at[me], local_sem.at[3]),
        pltpu.make_async_copy(taps_hbm.at[own_rows, :], taps_ref.at[me], local_sem.at[2]),
    ]

    def spread_copy(step):
        peer = lax.rem(me + step, sections)
        lanes = pl.ds(pl.multiple_of(peer * chans, chans), chans)
        return pltpu.make_async_remote_copy(
            src_ref=prompt_ref.at[:, lanes],
            dst_ref=pool.at[me, me_resp],
            send_sem=spread_sems.at[0, step],
            recv_sem=spread_sems.at[1, step],
            device_id={"section": peer},
            device_id_type=MESH,
        )

    def pool_copy(s, step):
        return pltpu.make_async_remote_copy(
            src_ref=pool.at[s, me_resp],
            dst_ref=pool.at[s, me_resp],
            send_sem=pool_sems.at[0, s, step],
            recv_sem=pool_sems.at[1, s, step],
            device_id={"resp": lax.rem(me_resp + step, n_resp)},
            device_id_type=MESH,
        )

    def own_pool():
        return pltpu.make_async_copy(
            prompt_ref.at[:, own_lanes], pool.at[me, me_resp], local_sem.at[4]
        )

    def start_pool(s):
        step = lax.rem(me - s + sections, sections)

        @pl.when(step == 0)
        def _():
            own_pool().wait()

        @pl.when(step > 0)
        def _():
            spread_copy(step).wait()

        loop(1, n_resp, lambda d: pool_copy(s, d).start())

    def wait_pool(s):
        loop(1, n_resp, lambda d: pool_copy(s, d).wait())

    if direct:
        own_pool().start()
        loop(1, sections, lambda step: spread_copy(step).start())
    for copy in local_copies:
        copy.start()
    loop(1, sections, start_weights)
    if direct:
        start_pool(0)
    for copy in local_copies:
        copy.wait()

    def first_stats(block):
        wide = rows_in[0, :, lane_slice(block)].astype(F32)
        stat_acc[...] += wide * wide

    stat_acc[...] = jnp.zeros_like(stat_acc)
    loop(0, blocks, first_stats)
    loop(1, sections, wait_weights)

    t_row = lax.broadcasted_iota(jnp.int32, (length, LANES), 0)
    s_lane = lax.broadcasted_iota(jnp.int32, (length, LANES), 1)
    keep = s_lane <= prompt_len + t_row
    s_row = lax.broadcasted_iota(jnp.int32, (total, LANES), 0)
    t_lane = lax.broadcasted_iota(jnp.int32, (total, LANES), 1)
    keep_t = s_row <= prompt_len + t_lane

    def build(s, block):
        rows = pl.ds(pl.multiple_of(block * groups, groups), groups)
        both = taps_ref[s, rows, :]
        flipped, plain = both[:, :LANES], both[:, LANES:]
        for g in range(groups):
            base = pl.multiple_of((block * groups + g) * length, length)
            wide = jnp.broadcast_to(flipped[g : g + 1], (length, LANES))
            wide = pltpu.roll(wide, prompt_len, 1, stride=1, stride_axis=0)
            wide = jnp.where(keep, wide, 0.0)
            high = wide.astype(BF16)
            low = (wide - high.astype(F32)).astype(BF16)
            toep[s, pl.ds(base, length), :] = jnp.concatenate([high, high, low], axis=1)
            base = pl.multiple_of((block * groups + g) * total, total)
            wide = jnp.broadcast_to(plain[g : g + 1], (total, LANES))
            wide = pltpu.roll(wide, prompt_len, 1, stride=1, stride_axis=0)
            toep_t[s, pl.ds(base, total), :] = jnp.where(keep_t, wide, 0.0).astype(BF16)

    def choose(s, block):
        lanes = lane_slice(block)
        for m in range(micro):
            rows = slice(m * prompt_len, (m + 1) * prompt_len)
            if direct:
                picked = jnp.zeros((prompt_len, LANES), F32)
                for r in range(n_resp):
                    flag = jnp.full((prompt_len, LANES), owner_ref[m], jnp.int32) == r
                    picked = jnp.where(flag, pool[s, r, :, lanes].astype(F32), picked)
                chosen_rows[s, rows, lanes] = picked.astype(BF16)
            else:
                picked = prompt_ref[s, rows, lanes].astype(F32)
                chosen_rows[s, rows, lanes] = prompt_ref[s, rows, lanes]
            prompt_acc[rows, :] += picked * picked

    row_id = lax.broadcasted_iota(jnp.int32, (total, LANES), 0)
    wide_group = (
        lax.broadcasted_iota(jnp.int32, (1, micro * LANES), 1) % LANES
    ) // per_group
    tap_count = short_ref.shape[1]

    def pick(stacked, rows):
        out = stacked[0:rows]
        for g in range(1, groups):
            out = jnp.where(wide_group == g, stacked[g * rows : (g + 1) * rows], out)
        return out

    def joined_rows(s, m, lanes):
        rows_p = slice(m * prompt_len, (m + 1) * prompt_len)
        rows_c = slice(m * length, (m + 1) * length)
        joined = jnp.concatenate(
            [chosen_rows[s, rows_p, lanes].astype(F32), rows_in[s, rows_c, lanes].astype(F32)],
            axis=0,
        )
        factor = jnp.concatenate([fac_p[s, rows_p, :], fac_c[s, rows_c, :]], axis=0)
        return joined, factor

    def forward(s, carry):
        if direct:
            wait_pool(s)

            @pl.when(s + 1 < sections)
            def _():
                start_pool(s + 1)

        prompt_acc[...] = jnp.zeros_like(prompt_acc)
        loop(0, blocks, lambda block: choose(s, block))
        finish = start_stats(s, rows_to_line(stat_acc[...]), rows_to_line(prompt_acc[...]))
        loop(0, blocks, lambda block: build(s, block))
        sums = finish()
        fac_c[s] = lax.rsqrt(line_to_rows(sums[0]) * (1.0 / width) + 1e-06)
        fac_p[s] = lax.rsqrt(line_to_rows(sums[1]) * (1.0 / width) + 1e-06)
        stat_acc[...] = jnp.zeros_like(stat_acc)
        score_acc[...] = jnp.zeros_like(score_acc)

        def run(block, carry):
            lanes = lane_slice(block)
            wide = wide_slice(block)
            gain = gain_ref[s, :, lanes]
            short = short_ref[s, :, lanes]
            parts, lows, saved = [], [], []
            for m in range(micro):
                joined, factor = joined_rows(s, m, lanes)
                normed = joined * factor * gain
                shorter = normed * short[0:1]
                for j in range(1, tap_count):
                    moved = jnp.where(row_id >= j, pltpu.roll(normed, j, 0), 0.0)
                    shorter = shorter + moved * short[j : j + 1]
                high = shorter.astype(BF16)
                parts.append(high)
                lows.append((shorter - high.astype(F32)).astype(BF16))
                saved.append((joined[prompt_len:], normed[prompt_len:]))
            high = jnp.concatenate(parts, axis=1)
            short_out[s, :, wide] = high
            rhs = jnp.concatenate([high, jnp.concatenate(lows, axis=1), high], axis=0)
            base = pl.multiple_of(block * groups * length, groups * length)
            stacked = jnp.dot(
                toep[s, pl.ds(base, groups * length), :], rhs, preferred_element_type=F32
            )
            longer_all = pick(stacked, length)
            for m in range(micro):
                rows = slice(m * length, (m + 1) * length)
                longer = longer_all[:, m * LANES : (m + 1) * LANES]
                long_out[s, rows, lanes] = longer
                mixed = (saved[m][0] + saved[m][1] * longer).astype(BF16)
                rows_in[s + 1, rows, lanes] = mixed
                mixed = mixed.astype(F32)
                stat_acc[rows, :] += mixed * mixed
                score_acc[rows, :] += mixed * head_ref[0:1, head_slice(block)]
            return carry

        lax.fori_loop(0, blocks, run, 0)

        return carry

    lax.fori_loop(0, sections, forward, 0)

    live = []
    for m in range(micro):
        count = jnp.full((length, LANES), length_ref[m, 0], jnp.int32)
        live.append(jnp.where(t_row < count, 1.0, 0.0) / jnp.sqrt(count.astype(F32)))
    tile_rows = []
    for m in range(micro):
        rows = slice(m * length, (m + 1) * length)
        line = jnp.sum(score_acc[rows, :] * live[m], axis=0, keepdims=True)
        tile_rows.append(jnp.broadcast_to(jnp.sum(line, axis=1, keepdims=True), (1, LANES)))
    tile_rows.append(jnp.zeros((8 - micro, LANES), F32))
    score_tile = jnp.concatenate(tile_rows, axis=0)
    own_score = start_stats(sections, score_tile, score_tile)()[0]
    score_ref[...] = own_score
    resp_out[...] = own_score
    swap("resp", n_resp, me_resp, resp_out, resp_in, resp_sems)()
    winner, loser = ends_ref[0], ends_ref[1]

    def signs(r):
        return jnp.where(winner == r, 1.0, 0.0) - jnp.where(loser == r, 1.0, 0.0)

    margin = lax.fori_loop(
        0, n_resp, lambda r, acc: acc + resp_in[r] * signs(r), jnp.zeros((8, LANES), F32)
    )
    weight = 1.0 / (1.0 + jnp.exp(margin))
    slopes = -jnp.sum(signs(me_resp) * weight, axis=1, keepdims=True)

    def seed(block, carry):
        lanes = lane_slice(block)
        for m in range(micro):
            rows = slice(m * length, (m + 1) * length)
            upstream[rows, lanes] = live[m] * slopes[m : m + 1] * head_ref[0:1, head_slice(block)]
        return carry

    lax.fori_loop(0, blocks, seed, 0)

    keep_pair = total - 1 - s_lane <= prompt_len + t_row
    reverse = (
        lax.broadcasted_iota(jnp.int32, (total, total), 0)
        + lax.broadcasted_iota(jnp.int32, (total, total), 1)
        == total - 1
    )
    reverse = jnp.where(reverse, 1.0, 0.0).astype(BF16)

    share = 2 * blocks // n_resp

    def part_slice(r):
        return pl.ds(r * share, share)

    def part_steps(s, action):
        def each(step):
            peer = lax.rem(me_resp + step, n_resp)
            action(
                pltpu.make_async_remote_copy(
                    src_ref=tiles_own.at[s, part_slice(peer)],
                    dst_ref=tiles_in.at[s, me_resp],
                    send_sem=part_sems.at[0, s, step],
                    recv_sem=part_sems.at[1, s, step],
                    device_id={"resp": peer},
                    device_id_type=MESH,
                )
            )

        loop(1, n_resp, each)

    def tile_copy(s, step, k, r):
        return pltpu.make_async_remote_copy(
            src_ref=tiles_sum.at[s],
            dst_ref=tiles_all.at[k, r],
            send_sem=tile_send.at[s, step],
            recv_sem=tile_recv.at[k, r],
            device_id={"section": s, "resp": lax.rem(me_resp + step, n_resp)},
            device_id_type=MESH,
        )

    def tile_steps(s, action):
        def each(step):
            @pl.when(jnp.logical_not((s == me) & (step == 0)))
            def _():
                action(tile_copy(s, step, me, me_resp))

        loop(0, n_resp, each)

    def backward(step, carry):
        s = sections - 1 - step
        stat_acc[...] = jnp.zeros_like(stat_acc)

        def run(block, carry):
            lanes = lane_slice(block)
            wide = wide_slice(block)
            gain = gain_ref[s, :, lanes]
            short = short_ref[s, :, lanes]
            parts, saved = [], []
            for m in range(micro):
                rows = slice(m * length, (m + 1) * length)
                joined, factor = joined_rows(s, m, lanes)
                scaled = joined * factor
                normed = scaled * gain
                above = upstream[rows, lanes]
                parts.append((above * normed[prompt_len:]).astype(BF16))
                saved.append((joined[prompt_len:], scaled, normed, above))
            d_long = jnp.concatenate(parts, axis=1)
            base = pl.multiple_of(block * groups * total, groups * total)
            stacked = jnp.dot(
                toep_t[s, pl.ds(base, groups * total), :][:, :length],
                d_long,
                preferred_element_type=F32,
            )
            d_short_all = pick(stacked, total)
            turned = jnp.dot(reverse, short_out[s, :, wide], preferred_element_type=F32)
            d_wide = d_long.astype(F32)
            masked = jnp.concatenate(
                [
                    jnp.where(wide_group == g, d_wide, 0.0).astype(BF16)
                    for g in range(groups)
                ],
                axis=0,
            )
            pairs = lax.dot_general(
                masked,
                turned.astype(BF16),
                (((1,), (1,)), ((), ())),
                preferred_element_type=F32,
            )
            lines = []
            for g in range(groups):
                one = jnp.where(keep_pair, pairs[g * length : (g + 1) * length], 0.0)
                one = pltpu.roll(one, LANES + 1 - length, 1, stride=1, stride_axis=0)
                lines.append(jnp.sum(one, axis=0, keepdims=True))
            tiles_own[s, 2 * block + 1] = jnp.concatenate(lines, axis=0)
            grads = [jnp.zeros((1, LANES), F32)] * (tap_count + 1)
            for m in range(micro):
                rows = slice(m * length, (m + 1) * length)
                joined_c, scaled, normed, above = saved[m]
                d_short = d_short_all[:, m * LANES : (m + 1) * LANES]
                d_normed = d_short * short[0:1]
                grads[1] = grads[1] + jnp.sum(d_short * normed, axis=0, keepdims=True)
                for j in range(1, tap_count):
                    moved = jnp.where(
                        row_id < total - j, pltpu.roll(d_short, total - j, 0), 0.0
                    )
                    d_normed = d_normed + moved * short[j : j + 1]
                    grads[1 + j] = grads[1 + j] + jnp.sum(
                        moved * normed, axis=0, keepdims=True
                    )
                direct = above * long_out[s, rows, lanes]
                d_normed = jnp.concatenate(
                    [d_normed[:prompt_len], d_normed[prompt_len:] + direct], axis=0
                )
                grads[0] = grads[0] + jnp.sum(d_normed * scaled, axis=0, keepdims=True)
                inner = d_normed[prompt_len:] * gain
                partial[rows, lanes] = inner
                stat_acc[rows, :] += inner * joined_c
            tiles_own[s, 2 * block] = jnp.concatenate(grads, axis=0)
            return carry

        lax.fori_loop(0, blocks, run, 0)

        if direct:
            part_steps(s, lambda copy: copy.start())
            parts_in = tiles_in.at[s]
            parts_in[me_resp] = tiles_own[s, part_slice(me_resp)]

        @pl.when(s > 0)
        def _():
            line = rows_to_line(stat_acc[...])
            all_sums = start_stats(sections + 1 + step, line, line)()[0]
            factor = fac_c[s]
            pull = line_to_rows(all_sums) * (1.0 / width) * factor * factor * factor

            def finish(block, carry):
                lanes = lane_slice(block)
                grad = (
                    upstream[:, lanes]
                    + factor * partial[:, lanes]
                    - rows_in[s, :, lanes].astype(F32) * pull
                )
                upstream[:, lanes] = grad.astype(BF16).astype(F32)
                return carry

            lax.fori_loop(0, blocks, finish, 0)

        if direct:
            part_steps(s, lambda copy: copy.wait())
            tiles_sum[s] = jnp.sum(tiles_in[s], axis=0)

            @pl.when(s == me)
            def _():
                tiles_all[me, me_resp] = tiles_sum[s]

            tile_steps(s, lambda copy: copy.start())

        return carry

    lax.fori_loop(0, sections, backward, 0)

    if direct:
        loop(0, sections, lambda s: tile_steps(s, lambda copy: copy.wait_send()))

        def arrive(step):
            k, r = step // n_resp, step % n_resp

            @pl.when(jnp.logical_not((k == me) & (r == me_resp)))
            def _():
                tile_copy(0, 0, k, r).wait_recv()

        loop(0, sections * n_resp, arrive)
        gain_out, taps_short_out, taps_long_out = outs
        per_line = LANES // groups
        for line in range(sections * blocks // per_line):
            lines = []
            for place in range(per_line):
                block = line * per_line + place
                lanes = slice(block * LANES, (block + 1) * LANES)
                owner, local = divmod(2 * block, 2 * blocks)
                first, second = (divmod(local + kind, share) for kind in range(2))
                tile = tiles_all[owner, first[0], first[1]]
                gain_out[:, lanes] = tile[0:1]
                taps_short_out[:, lanes] = tile[1:]
                lines.append(tiles_all[owner, second[0], second[1]])
            lanes = slice(line * LANES, (line + 1) * LANES)
            taps_long_out[:, lanes] = jnp.transpose(jnp.concatenate(lines, axis=0))
    else:
        outs[0][...] = tiles_own[...]


def run_kernel(dims, direct, *arrays):
    sections, n_resp, micro, length, prompt_len, chans, per_group, width = dims
    rows = micro * length
    total = prompt_len + length
    group_total = chans // per_group
    tile = (8, LANES)
    tiles = 2 * chans // LANES
    share = tiles // n_resp if direct else 1
    ranks = n_resp if direct else 1
    vmem = pl.BlockSpec(memory_space=pltpu.VMEM)
    hbm = pl.BlockSpec(memory_space=pl.ANY)
    smem = pl.BlockSpec(memory_space=pltpu.SMEM)
    tap_count = arrays[3].shape[0]
    if direct:
        out_shapes = [(1, width), (tap_count, width), (LANES, width // per_group)]
    else:
        out_shapes = [(sections, tiles) + tile]
    return pl.pallas_call(
        functools.partial(kernel, dims, direct),
        out_shape=(
            jax.ShapeDtypeStruct(tile, F32),
            *(jax.ShapeDtypeStruct(shape, F32) for shape in out_shapes),
        ),
        in_specs=[hbm, hbm if direct else vmem, hbm, hbm, hbm, smem, vmem, vmem, smem],
        out_specs=(vmem,) * (1 + len(out_shapes)),
        scratch_shapes=[
            pltpu.VMEM((sections, group_total * length, 3 * LANES), BF16),
            pltpu.VMEM((sections, group_total * total, LANES), BF16),
            pltpu.VMEM((sections, ranks, prompt_len, chans), BF16),
            pltpu.VMEM((sections, micro * prompt_len, chans), BF16),
            pltpu.VMEM((sections, 1, chans), F32),
            pltpu.VMEM((sections, tap_count, chans), F32),
            pltpu.VMEM((sections, group_total, 2 * LANES), F32),
            pltpu.VMEM((sections + 1, rows, chans), BF16),
            pltpu.VMEM((sections, total, micro * chans), BF16),
            pltpu.VMEM((sections, rows, chans), F32),
            pltpu.VMEM((sections, micro * prompt_len, LANES), F32),
            pltpu.VMEM((sections, rows, LANES), F32),
            pltpu.VMEM((rows, chans), F32),
            pltpu.VMEM((rows, chans), F32),
            pltpu.VMEM((rows, LANES), F32),
            pltpu.VMEM((rows, LANES), F32),
            pltpu.VMEM((micro * prompt_len, LANES), F32),
            pltpu.VMEM((2 * sections, 2) + tile, F32),
            pltpu.VMEM((2 * sections, sections, 2) + tile, F32),
            pltpu.VMEM(tile, F32),
            pltpu.VMEM((n_resp,) + tile, F32),
            pltpu.VMEM((sections, tiles) + tile, F32),
            pltpu.VMEM((sections, ranks, share) + tile, F32),
            pltpu.VMEM((sections, share) + tile, F32),
            pltpu.VMEM((sections, ranks, share) + tile, F32),
            pltpu.SemaphoreType.DMA((5,)),
            pltpu.SemaphoreType.DMA((2, 3, sections)),
            pltpu.SemaphoreType.DMA((2, sections)),
            pltpu.SemaphoreType.DMA((2, sections, ranks)),
            pltpu.SemaphoreType.DMA((2 * sections, 2, sections)),
            pltpu.SemaphoreType.DMA((2, n_resp)),
            pltpu.SemaphoreType.DMA((2, sections, ranks)),
            pltpu.SemaphoreType.DMA((sections, ranks)),
            pltpu.SemaphoreType.DMA((sections, ranks)),
        ],
        compiler_params=pltpu.CompilerParams(
            has_side_effects=True, vmem_limit_bytes=56 * 1024 * 1024
        ),
    )(*arrays)


def body(
    completion_rows,
    prompt_pool,
    norm_gain,
    short_taps,
    long_taps,
    score_head,
    live_lengths,
    prompt_owner,
    pair_index,
):
    sections = lax.axis_size("section")
    n_resp = lax.axis_size("resp")
    me_resp = lax.axis_index("resp")
    micro, _, length, width = completion_rows.shape
    prompt_len = prompt_pool.shape[2]
    chans = width // sections
    tap_len, group_all = long_taps.shape[1:]
    per_group = width // group_all
    dims = (sections, n_resp, micro, length, prompt_len, chans, per_group, width)

    tiles = 2 * chans // LANES
    direct = n_resp <= 8 and tiles % n_resp == 0

    taps = long_taps[0].T
    flipped = jnp.concatenate([taps[:, :1], taps[:, :0:-1]], axis=1)
    taps = jnp.concatenate([flipped, taps], axis=1)
    prompts = prompt_pool[0, 0]
    if not direct:
        split = prompts.reshape(prompt_len, sections, chans).transpose(1, 0, 2)
        split = lax.all_to_all(split, "section", 0, 0, tiled=True)
        here = (prompt_owner == me_resp)[None, :, None, None]
        split = lax.psum(jnp.where(here, split[:, None], jnp.zeros((), BF16)), "resp")
        prompts = split.reshape(sections, micro * prompt_len, chans)
    rows = completion_rows.reshape(micro * length, width)
    head = score_head[None]

    ends = jnp.pad(
        pair_index.transpose(2, 0, 1),
        ((0, 0), (0, 8 - micro), (0, LANES - pair_index.shape[1])),
        constant_values=-1,
    )
    scores, *grads = run_kernel(
        dims,
        direct,
        rows,
        prompts,
        norm_gain,
        short_taps[0],
        taps,
        prompt_owner,
        head,
        ends,
        live_lengths,
    )
    scores = scores[:micro, :1].astype(BF16)
    if direct:
        return (scores, grads[0], grads[1][None], grads[2][None])
    grads = lax.psum(grads[0], "resp")
    grads = lax.all_to_all(grads, "section", 0, 0, tiled=True)
    grads = grads.reshape(sections * tiles // 2, 2, 8, LANES)
    gs_grad = grads[:, 0].transpose(1, 0, 2).reshape(8, width)
    taps_grad = grads[:, 1].reshape(group_all, tap_len).T
    return (
        scores,
        gs_grad[:1],
        gs_grad[None, 1:],
        taps_grad[None],
    )


SIDE = 8


def wide_kernel(
    dims,
    comp_hbm,
    prompt_hbm,
    gain_hbm,
    short_hbm,
    taps_hbm,
    head_hbm,
    owner_ref,
    pair_ref,
    length_ref,
    score_ref,
    short_grad_out,
    long_grad_out,
    comp_full,
    prompt_full,
    taps_full,
    head_own,
    comp_in,
    staged,
    pool,
    gain_in,
    short_in,
    taps_src,
    taps_in,
    order_c,
    order_p,
    lined,
    first_out,
    first_in,
    stat_out,
    stat_in,
    rows_in,
    prompt_rows,
    long_out,
    short_out,
    toep,
    toep_p,
    toep_t,
    params,
    heads,
    fac_c,
    fac_p,
    normed_buf,
    d_short_buf,
    upstream,
    inner_buf,
    d_long_buf,
    acc_ref,
    scales,
    tiles_own,
    short_own,
    long_own,
    local_sem,
    comp_send,
    comp_recv,
    weight_send,
    weight_recv,
    pool_send,
    pool_recv,
    pool_own,
    spread_send,
    spread_recv,
    first_send,
    first_recv,
    stat_send,
    stat_recv,
    part_send,
    part_recv,
):
    sections, n_resp, micro, length, chans, per_group, width = dims
    comps = micro * n_resp
    ranks = sections * n_resp
    blocks = chans // LANES
    per_block = LANES // per_group
    groups = blocks * per_block
    tap_count = short_in.shape[1]
    total = 2 * length
    me = lax.axis_index("section")
    me_resp = lax.axis_index("resp")
    rank = me * n_resp + me_resp

    def loop(low, high, step_of):
        def run(index, carry):
            step_of(index)
            return carry

        lax.fori_loop(low, high, run, 0)

    def lockstep(low, high, count, step_of):
        def run(index, carry):
            live = [step_of(index * count + k, k) for k in range(count)]
            while live:
                live = [step for step in live if next(step, 0) is None]
            return carry

        lax.fori_loop(low // count, high // count, run, 0)

    def add_up(values):
        while len(values) > 1:
            values = [a + b for a, b in zip(values[::2], values[1::2])] + (
                values[-1:] if len(values) % 2 else []
            )
        return values[0]

    def place(peer):
        return {"section": peer // n_resp, "resp": lax.rem(peer, n_resp)}

    def lanes_of(peer):
        return pl.ds(pl.multiple_of(peer * chans, chans), chans)

    def groups_of(peer):
        return pl.ds(pl.multiple_of(peer * groups, groups), groups)

    def remote(src, dst, send_sem, recv_sem, device):
        return pltpu.make_async_remote_copy(
            src_ref=src,
            dst_ref=dst,
            send_sem=send_sem,
            recv_sem=recv_sem,
            device_id=device,
            device_id_type=MESH,
        )

    load_comp = pltpu.make_async_copy(comp_hbm, comp_full, local_sem.at[0])
    load_prompt = pltpu.make_async_copy(prompt_hbm, prompt_full, local_sem.at[1])
    load_taps = pltpu.make_async_copy(taps_hbm, taps_full, local_sem.at[2])
    load_head = pltpu.make_async_copy(head_hbm.at[:, lanes_of(rank)], head_own, local_sem.at[3])
    own_comp = pltpu.make_async_copy(
        comp_hbm.at[:, lanes_of(rank)], comp_in.at[me_resp], local_sem.at[4]
    )
    own_stage = pltpu.make_async_copy(
        prompt_hbm.at[:, pl.ds(pl.multiple_of(me * n_resp * chans, n_resp * chans), n_resp * chans)],
        staged.at[me],
        local_sem.at[5],
    )
    own_gain = pltpu.make_async_copy(
        gain_hbm.at[:, lanes_of(rank)], gain_in.at[me], local_sem.at[6]
    )
    own_short = pltpu.make_async_copy(
        short_hbm.at[:, :, lanes_of(rank)], short_in.at[me], local_sem.at[7]
    )

    def comp_copy(step):
        peer_resp = lax.rem(me_resp + step, n_resp)
        return remote(
            comp_hbm.at[:, lanes_of(me * n_resp + peer_resp)],
            comp_in.at[me_resp],
            comp_send.at[step],
            comp_recv.at[me_resp],
            {"resp": peer_resp},
        )

    def comp_wait(step):
        source = lax.rem(me_resp + step, n_resp)
        remote(
            comp_hbm.at[:, lanes_of(rank)],
            comp_in.at[source],
            comp_send.at[step],
            comp_recv.at[source],
            {"resp": source},
        ).wait_recv()

    def weight_parts(peer_rank, source):
        return (
            (gain_hbm.at[:, lanes_of(peer_rank)], gain_in.at[source]),
            (short_hbm.at[:, :, lanes_of(peer_rank)], short_in.at[source]),
            (taps_src.at[groups_of(peer_rank), :], taps_in.at[source]),
        )

    def weight_copy(kind, step):
        peer = lax.rem(me + step, sections)
        src, dst = weight_parts(peer * n_resp + me_resp, me)[kind]
        return remote(
            src, dst, weight_send.at[kind, step], weight_recv.at[kind, me], {"section": peer}
        )

    def weight_wait(kind, step):
        source = lax.rem(me + step, sections)
        src, dst = weight_parts(rank, source)[kind]
        remote(
            src,
            dst,
            weight_send.at[kind, step],
            weight_recv.at[kind, source],
            {"section": source},
        ).wait_recv()

    def far_lanes(peer):
        span = n_resp * chans
        return pl.ds(pl.multiple_of(peer * span, span), span)

    def spread_copy(step):
        peer = lax.rem(me + step, sections)
        return remote(
            prompt_hbm.at[:, far_lanes(peer)],
            staged.at[me],
            spread_send.at[step],
            spread_recv.at[me],
            {"section": peer},
        )

    def spread_wait(s):
        remote(
            prompt_hbm.at[:, far_lanes(me)],
            staged.at[s],
            spread_send.at[0],
            spread_recv.at[s],
            {"section": s},
        ).wait_recv()

    def pool_copy(s, step):
        peer = lax.rem(me_resp + step, n_resp)
        return remote(
            staged.at[s, :, pl.ds(pl.multiple_of(peer * chans, chans), chans)],
            pool.at[s, me_resp],
            pool_send.at[s, step],
            pool_recv.at[s, me_resp],
            {"resp": peer},
        )

    def own_pool(s):
        return pltpu.make_async_copy(
            staged.at[s, :, pl.ds(pl.multiple_of(me_resp * chans, chans), chans)],
            pool.at[s, me_resp],
            pool_own.at[s],
        )

    def start_pool(s):
        @pl.when(s == me)
        def _():
            own_stage.wait()

        @pl.when(s != me)
        def _():
            spread_wait(s)

        loop(1, n_resp, lambda step: pool_copy(s, step).start())
        own_pool(s).start()

    def pool_wait(s):
        def each(step):
            source = lax.rem(me_resp + step, n_resp)
            remote(
                pool.at[s, source],
                pool.at[s, source],
                pool_send.at[s, step],
                pool_recv.at[s, source],
                {"resp": source},
            ).wait_recv()

        loop(1, n_resp, each)
        own_pool(s).wait()

    def first_copy(step):
        peer = lax.rem(rank + step, ranks)
        return remote(
            first_out, first_in.at[rank], first_send.at[step], first_recv.at[rank], place(peer)
        )

    def first_wait(step):
        source = lax.rem(rank + step, ranks)
        remote(
            first_out,
            first_in.at[source],
            first_send.at[step],
            first_recv.at[source],
            place(source),
        ).wait_recv()

    peers = []
    for j in range(1, n_resp):
        hop = jnp.where(me_resp * 2 < n_resp, n_resp - j, j)
        peer_resp = lax.rem(me_resp + hop, n_resp)
        peers += [(lax.rem(me + k, sections), peer_resp) for k in range(sections)]
    peers += [(lax.rem(me + k, sections), me_resp) for k in range(1, sections)]

    def stat_start(slot, tile):
        stat_out[slot] = tile
        for peer, peer_resp in peers:
            remote(
                stat_out.at[slot],
                stat_in.at[slot, rank],
                stat_send.at[slot],
                stat_recv.at[slot],
                {"section": peer, "resp": peer_resp},
            ).start()
        stat_in[slot, rank] = tile

    def stat_wait(slot, sem):
        bulk = stat_in.at[slot, pl.ds(0, ranks - 1)]
        pltpu.make_async_copy(bulk, bulk, sem.at[slot]).wait()

    def stat_finish(slot):
        stat_wait(slot, stat_recv)
        return jnp.sum(stat_in[slot], axis=0)

    def result_parts(s):
        return (
            (short_own.at[s], short_grad_out.at[:, :, lanes_of(rank)]),
            (long_own.at[s], long_grad_out.at[groups_of(rank), :]),
        )

    def result_own(s, kind):
        src, dst = result_parts(s)[kind]
        return pltpu.make_async_copy(src, dst, local_sem.at[8 + kind])

    def result_start(s):
        def each(step):
            @pl.when(jnp.logical_not((s == me) & (step == 0)))
            def _():
                for kind, (src, dst) in enumerate(result_parts(s)):
                    remote(
                        src,
                        dst,
                        part_send.at[kind],
                        part_recv.at[kind],
                        {"section": s, "resp": lax.rem(me_resp + step, n_resp)},
                    ).start()

        loop(0, n_resp, each)

        @pl.when(s == me)
        def _():
            for kind in range(2):
                result_own(s, kind).start()

    def result_wait(sem):
        for kind, bulk in enumerate(
            (
                short_grad_out.at[:, :, pl.ds(0, (ranks - 1) * chans)],
                long_grad_out.at[pl.ds(0, (ranks - 1) * groups), :],
            )
        ):
            pltpu.make_async_copy(bulk, bulk, sem.at[kind]).wait()

    for copy in (load_taps, load_comp, load_prompt, load_head):
        copy.start()
    for copy in (own_comp, own_stage, own_gain, own_short):
        copy.start()
    barrier = pltpu.get_barrier_semaphore()
    loop(
        1,
        ranks,
        lambda step: pl.semaphore_signal(
            barrier,
            inc=1,
            device_id=place(lax.rem(rank + step, ranks)),
            device_id_type=MESH,
        ),
    )

    tile_row = lax.broadcasted_iota(jnp.int32, (LANES, LANES), 0)
    tile_lane = lax.broadcasted_iota(jnp.int32, (LANES, LANES), 1)
    row_target = (tile_row // per_group) * LANES + tile_row % per_group
    prompt_key = (tile_lane // (n_resp * per_group)) * (n_resp * per_group) + (
        tile_lane % per_group
    )

    def fill_order(c):
        rows = pl.ds(pl.multiple_of(c * LANES, LANES), LANES)
        for n in range(per_block):
            hit = row_target + c * per_group == tile_lane + n * LANES
            order_c[rows, n * LANES : (n + 1) * LANES] = jnp.where(hit, 1.0, 0.0).astype(BF16)

    loop(0, comps, fill_order)
    for m in range(micro):
        for n in range(per_block):
            hit = row_target + m * n_resp * per_group == prompt_key + n * LANES
            order_p[m * LANES : (m + 1) * LANES, n * LANES : (n + 1) * LANES] = jnp.where(
                hit, 1.0, 0.0
            ).astype(BF16)
    pad = 8
    for g in range(groups):
        normed_buf[g, :pad] = jnp.zeros((pad, LANES), F32)
        for s in range(sections):
            d_short_buf[s, g, total:] = jnp.zeros((pad, LANES), F32)

    load_taps.wait()
    upright = jnp.transpose(taps_full[...])
    mirror = jnp.where(lax.rem(tile_row + tile_lane, LANES) == 0, 1.0, 0.0)
    taps_src[:, :LANES] = jnp.dot(
        upright, mirror, preferred_element_type=F32, precision=lax.Precision.HIGHEST
    )
    taps_src[:, LANES:] = upright

    ones = jnp.ones((16, 2 * LANES), BF16)

    def split(values):
        high = values.astype(BF16)
        return high, (values - high.astype(F32)).astype(BF16)

    def lane_sums(acc, weights, below=None):
        if acc.shape[0] < LANES:
            rest = [] if below is None else [below]
            rows = LANES - acc.shape[0] - sum(block.shape[0] for block in rest)
            acc = jnp.concatenate([acc] + rest + [jnp.zeros((rows, LANES), F32)], axis=0)
        both = jnp.concatenate(split(acc), axis=1)
        return lax.dot_general(
            weights, both, (((1,), (1,)), ((), ())), preferred_element_type=F32
        )[:8]

    def square_rows(ref):
        def step(block, acc):
            values = ref[:, pl.ds(pl.multiple_of(block * LANES, LANES), LANES)].astype(F32)
            return acc + values * values

        return lax.fori_loop(
            0, width // LANES, step, jnp.zeros((ref.shape[0], LANES), F32), unroll=2
        )

    load_comp.wait()
    comp_line = lane_sums(square_rows(comp_full), ones)
    load_prompt.wait()
    prompt_line = lane_sums(square_rows(prompt_full), ones)
    eight_row = lax.broadcasted_iota(jnp.int32, (8, LANES), 0)
    eight_lane = lax.broadcasted_iota(jnp.int32, (8, LANES), 1)
    message = jnp.where(eight_row == 0, comp_line, prompt_line)
    for m in range(micro):
        count = jnp.full((8, LANES), length_ref[0, m], jnp.int32).astype(F32)
        message = jnp.where(eight_row == 2 + m, count, message)
    first_out[...] = message

    pl.semaphore_wait(barrier, ranks - 1)
    @pl.when(me == 0)
    def _():
        loop(1, sections, lambda step: spread_copy(step).start())

    loop(1, n_resp, lambda step: comp_copy(step).start())
    loop(1, sections, lambda step: weight_copy(2, step).start())

    loop(1, ranks, lambda step: first_copy(step).start())

    def start_vectors(step):
        weight_copy(0, step).start()
        weight_copy(1, step).start()

    loop(1, sections, start_vectors)
    @pl.when(me != 0)
    def _():
        loop(1, sections, lambda step: spread_copy(step).start())

    first_in[rank] = message
    taps_in[me] = taps_src[groups_of(rank), :]

    own_gain.wait()
    own_short.wait()
    load_head.wait()

    def weights_arrive(step):
        for kind in range(3):
            weight_wait(kind, step)

    loop(1, sections, weights_arrive)

    def tile_lanes(values, n):
        out = pltpu.roll(values, (LANES - n * per_group) % LANES, 1)
        out = jnp.where(eight_lane < per_group, out, 0.0)
        span = per_group
        while span < LANES:
            out = out + pltpu.roll(out, span, 1)
            span *= 2
        return out

    t_row = lax.broadcasted_iota(jnp.int32, (length, LANES), 0)
    s_lane = lax.broadcasted_iota(jnp.int32, (length, LANES), 1)
    keep = s_lane <= length + t_row
    keep_t = tile_row <= length + tile_lane

    def spread_params(s):
        for b in range(blocks):
            lanes = slice(b * LANES, (b + 1) * LANES)
            rows = jnp.concatenate(
                [gain_in[s, :, lanes]] + [short_in[s, j, :, lanes] for j in range(tap_count)],
                axis=0,
            )
            for n in range(per_block):
                params[s, b * per_block + n] = tile_lanes(rows, n)

    loop(0, sections, spread_params)
    for b in range(blocks):
        rows = jnp.broadcast_to(head_own[:, b * LANES : (b + 1) * LANES], (8, LANES))
        for n in range(per_block):
            heads[b * per_block + n] = tile_lanes(rows, n)

    def build(s, g, k):
        line = taps_in[s, pl.ds(g, 1), :]
        wide = jnp.broadcast_to(line[:, :LANES], (length, LANES))
        wide = pltpu.roll(wide, length, 1, stride=1, stride_axis=0)
        wide_t = jnp.broadcast_to(line[:, LANES:], (total, LANES))
        wide_t = pltpu.roll(wide_t, length, 1, stride=1, stride_axis=0)
        yield
        wide = jnp.where(keep, wide, 0.0)
        high = wide.astype(BF16).astype(F32)
        low = wide - high
        low_turned = pltpu.roll(low, length, 1)
        high_turned = pltpu.roll(high, length, 1)
        toep_t[s, g] = jnp.where(keep_t, wide_t, 0.0).astype(BF16)
        yield
        first = s_lane < length
        toep_p[s, g] = jnp.where(first, high, low_turned).astype(BF16)
        toep[s, g] = jnp.where(first, high_turned, low).astype(BF16)

    start_pool(0)
    def build_section(s):
        lockstep(0, groups, 4, lambda g, k: build(s, g, k))

    build_section(0)

    def spread_rows(lines):
        tall = jnp.concatenate(
            [jnp.broadcast_to(lines[c : c + 1], (per_group, LANES)) for c in range(comps)],
            axis=0,
        )
        return jnp.transpose(tall)[:length]

    def to_factor(sums):
        return lax.rsqrt(sums * (1.0 / width) + 1e-06)

    loop(1, ranks, first_wait)
    own_lines = jnp.concatenate(
        [first_in[me * n_resp + r, 0:1] for r in range(n_resp)], axis=0
    )
    own_lines = jnp.concatenate(
        [
            own_lines if m == 0 else pltpu.roll(own_lines, LANES - m * length, 1)
            for m in range(micro)
        ],
        axis=0,
    )
    fac_c[0] = spread_rows(to_factor(own_lines))

    def prompt_factor(s):
        lines = []
        for m in range(micro):
            owner = jnp.full((8, LANES), owner_ref[m], jnp.int32)
            line = jnp.zeros((8, LANES), F32)
            for r in range(n_resp):
                line = jnp.where(owner == r, first_in[s * n_resp + r], line)
            lines += [line[1:2]] * n_resp
        fac_p[s] = spread_rows(to_factor(jnp.concatenate(lines, axis=0)))

    loop(0, sections, prompt_factor)

    def conv_short(ref, g, start, taps):
        out = ref[g, pl.ds(start, length)] * taps[1:2]
        for j in range(1, tap_count):
            out = out + ref[g, pl.ds(start - j, length)] * taps[1 + j : 2 + j]
        return out

    def conv_long(matrix, high, low):
        left = jnp.concatenate([matrix, matrix], axis=1)
        right = jnp.concatenate([high, high, low, low], axis=0)
        return jnp.dot(left, right, preferred_element_type=F32)

    def prepare(s):
        pool_wait(s)

        sides = []
        for b in range(blocks):
            lanes = slice(b * LANES, (b + 1) * LANES)
            row = []
            for m in range(micro):
                owner = jnp.full((length, LANES), owner_ref[m], jnp.int32)
                picked = pool[s, 0, :, lanes].astype(F32)
                for r in range(1, n_resp):
                    picked = jnp.where(owner == r, pool[s, r, :, lanes].astype(F32), picked)
                row.append(picked.astype(BF16))
            sides.append(jnp.concatenate(row, axis=1))
        side = jnp.concatenate(sides, axis=0)
        step = 2 * LANES
        for n in range(per_block // 2):
            part = jnp.dot(
                side, order_p[:, n * step : (n + 1) * step], preferred_element_type=F32
            ).astype(BF16)
            for b in range(blocks):
                for k in range(2):
                    prompt_rows[s, b * per_block + 2 * n + k] = part[
                        b * length : (b + 1) * length, k * LANES : (k + 1) * LANES
                    ]
        factor = fac_p[s]

        def each(g, k):
            taps = params[s, g]
            normed = prompt_rows[s, g].astype(F32) * factor * taps[0:1]
            normed_buf[g, pl.ds(pad, length)] = normed
            yield
            shorter = conv_short(normed_buf, g, pad, taps)
            high, low = split(shorter)
            short_out[s, g, :length] = high
            yield
            longer = conv_long(toep_p[s, g], high, low)
            yield
            long_out[s, g] = longer

        lockstep(0, groups, groups, each)

    loop(1, n_resp, comp_wait)
    start_pool(1)
    own_comp.wait()
    for b in range(blocks):
        lanes = slice(b * LANES, (b + 1) * LANES)
        for m in range(micro):
            for r in range(n_resp):
                c = m * n_resp + r
                lined[b * length : (b + 1) * length, c * LANES : (c + 1) * LANES] = comp_in[
                    r, m * length : (m + 1) * length, lanes
                ]
    for n in range(per_block // 2):
        step = 2 * LANES
        part = jnp.dot(
            lined[...], order_c[:, n * step : (n + 1) * step], preferred_element_type=F32
        ).astype(BF16)
        for b in range(blocks):
            for k in range(2):
                rows_in[0, b * per_block + 2 * n + k] = part[
                    b * length : (b + 1) * length, k * LANES : (k + 1) * LANES
                ]
    prepare(0)

    fold_row = lax.broadcasted_iota(jnp.int32, (16, 2 * LANES), 0)
    fold_lane = lax.broadcasted_iota(jnp.int32, (16, 2 * LANES), 1)
    fold = jnp.where((fold_lane % LANES) // per_group == fold_row, 1.0, 0.0).astype(BF16)

    def forward(s, last):
        acc_ref[...] = jnp.zeros_like(acc_ref)
        factor = fac_c[s]

        sums = []

        def each(g, k):
            taps = params[s, g]
            rows = rows_in[s, g].astype(F32)
            normed = rows * factor * taps[0:1]
            normed_buf[g, pl.ds(pad + length, length)] = normed
            yield
            shorter = conv_short(normed_buf, g, pad + length, taps)
            high, low = split(shorter)
            short_out[s, g, length:] = high
            yield
            longer = conv_long(toep[s, g], high, low)
            yield
            longer = long_out[s, g] + longer
            normed = normed_buf[g, pl.ds(pad + length, length)]
            mixed = (rows_in[s, g].astype(F32) + normed * longer).astype(BF16)
            sums.append((longer, mixed))
            yield
            longer, mixed = sums[k]
            long_out[s, g] = longer
            if not last:
                rows_in[s + 1, g] = mixed
            mixed = mixed.astype(F32)
            sums[k] = mixed * (heads[g, 0:1] if last else mixed)
            yield
            if k == groups - 1:
                acc_ref[...] += add_up(sums)
                sums.clear()

        lockstep(0, groups, groups, each)

    def forward_step(s):
        forward(s, False)
        stat_start(s, lane_sums(acc_ref[...], fold))
        build_section(s + 1)
        prepare(s + 1)

        @pl.when(s + 2 < sections)
        def _():
            start_pool(s + 2)

        fac_c[s + 1] = spread_rows(to_factor(stat_finish(s)))

    loop(0, sections - 1, forward_step)
    forward(sections - 1, True)

    comp_lane = eight_lane // per_group
    counts = jnp.zeros((8, LANES), F32)
    for m in range(micro):
        for r in range(n_resp):
            row = first_in[me * n_resp + r, 2 + m : 3 + m]
            counts = jnp.where(comp_lane == m * n_resp + r, row, counts)
    alive = t_row.astype(F32) < counts[0:1]
    live = jnp.where(alive, 1.0, 0.0) / jnp.sqrt(counts[0:1])
    score_line = jnp.sum(acc_ref[...] * live, axis=0, keepdims=True)
    score_line = jnp.where(eight_row == 0, score_line, 0.0)

    def seed(g, k):
        upstream[sections - 1, g] = live * heads[g, 0:1]
        yield

    lockstep(0, groups, SIDE, seed)

    def backward(s, last):
        acc_ref[...] = jnp.zeros_like(acc_ref)
        factor = fac_c[s]

        sums = []

        def each(g, k):
            taps = params[s, g]
            rows = rows_in[s, g].astype(F32)
            d_long = (upstream[s, g] * (rows * factor * taps[0:1])).astype(BF16)
            yield
            d_long_buf[s, g] = d_long
            d_short = jnp.dot(
                toep_t[s, g][:, :length], d_long, preferred_element_type=F32
            )
            yield
            d_short_buf[s, g, pl.ds(0, total)] = d_short
            if last:
                return
            yield
            d_normed = upstream[s, g] * long_out[s, g]
            for j in range(tap_count):
                d_normed = d_normed + d_short_buf[s, g, pl.ds(length + j, length)] * taps[1 + j : 2 + j]
            inner = d_normed * taps[0:1]
            sums.append(inner)
            yield
            inner_buf[g] = sums[k]
            sums[k] = sums[k] * rows_in[s, g].astype(F32)
            yield
            if k == groups - 1:
                acc_ref[...] += add_up(sums)
                sums.clear()

        lockstep(0, groups, groups, each)

    keep_pair = total - 1 - s_lane <= length + t_row
    reverse = jnp.where(tile_row + tile_lane == total - 1, 1.0, 0.0).astype(BF16)

    def gradients(s):
        factor_c = fac_c[s]
        factor_p = fac_p[s]
        scale = scales[s, 0:1]
        tops, longs = [], []

        def each(g, k):
            turned = jnp.dot(reverse, short_out[s, g], preferred_element_type=F32)
            yield
            pairs = lax.dot_general(
                (d_long_buf[s, g].astype(F32) * scale).astype(BF16),
                turned.astype(BF16),
                (((1,), (1,)), ((), ())),
                preferred_element_type=F32,
            )
            yield
            taps = params[s, g]
            scaled_p = prompt_rows[s, g].astype(F32) * factor_p
            scaled_c = rows_in[s, g].astype(F32) * factor_c
            lines = [
                jnp.sum(upstream[s, g] * long_out[s, g] * scaled_c, axis=0, keepdims=True)
            ]
            for j in range(tap_count):
                part = (
                    d_short_buf[s, g, pl.ds(j, length)] * scaled_p
                    + d_short_buf[s, g, pl.ds(length + j, length)] * scaled_c
                )
                lines.append(jnp.sum(part, axis=0, keepdims=True))
            tile = jnp.concatenate(lines, axis=0) * scale
            yield
            pairs = jnp.where(keep_pair, pairs, 0.0)
            pairs = pltpu.roll(pairs, LANES + 1 - length, 1, stride=1, stride_axis=0)
            yield
            span = per_group
            while span < LANES:
                tile = tile + pltpu.roll(tile, span, 1)
                span *= 2
            yield
            top = tile + jnp.sum(
                jnp.where(eight_row > 0, tile * taps, 0.0), axis=0, keepdims=True
            )
            tops.append(jnp.where(eight_row == 0, top, tile * taps[0:1]))
            longs.append(jnp.sum(pairs, axis=0, keepdims=True))
            yield
            if k < groups - 1:
                return
            for b in range(blocks):
                tile = tops[b * per_block]
                for n in range(1, per_block):
                    tile = jnp.where(comp_lane == n, tops[b * per_block + n], tile)
                tiles_own[b] = tile
            long_own[s] = jnp.concatenate(longs, axis=0)
            tops.clear()
            longs.clear()

        lockstep(0, groups, groups, each)
        for b in range(blocks):
            tile = tiles_own[b]
            for j in range(1 + tap_count):
                short_own[s, j, :, b * LANES : (b + 1) * LANES] = tile[j : j + 1]
        result_start(s)

    def go_down(s, sums, scale):
        factor = fac_c[s]
        pull = spread_rows(sums * (1.0 / width)) * factor * factor * factor

        def finish(g, k):
            grad = upstream[s, g] + factor * inner_buf[g] - rows_in[s, g].astype(F32) * pull
            yield
            if scale is not None:
                grad = grad * scale
            upstream[s - 1, g] = grad.astype(BF16).astype(F32)

        lockstep(0, groups, groups, finish)

    last = sections - 1
    backward(last, False)
    stat_start(last, lane_sums(acc_ref[...], fold, score_line))
    loop(1, n_resp, lambda step: comp_copy(step).wait_send())

    def weights_sent(step):
        for kind in range(3):
            weight_copy(kind, step).wait_send()

    loop(1, sections, weights_sent)

    loop(1, ranks, lambda step: first_copy(step).wait_send())
    loop(1, sections, lambda step: spread_copy(step).wait_send())

    def pools_sent(s):
        loop(1, n_resp, lambda step: pool_copy(s, step).wait_send())

    loop(0, sections, pools_sent)
    winner = jnp.full((8, LANES), -1, jnp.int32)
    loser = winner
    for m in range(micro):
        for p in range(pair_ref.shape[2]):
            here = (eight_row == m) & (eight_lane == p)
            winner = jnp.where(here, pair_ref[m, 0, p], winner)
            loser = jnp.where(here, pair_ref[m, 1, p], loser)
    signs = [
        jnp.where(winner == r, 1.0, 0.0) - jnp.where(loser == r, 1.0, 0.0)
        for r in range(n_resp)
    ]
    masks = [comp_lane == eight_row * n_resp + r for r in range(n_resp)]
    sums = stat_finish(last)
    totals = jnp.sum(jnp.where(eight_lane == length, sums, 0.0), axis=1, keepdims=True)
    totals = jnp.broadcast_to(totals, (8, LANES))
    scores = []
    for r in range(n_resp):
        rows = totals[r : r + 1]
        for m in range(1, micro):
            rows = jnp.where(eight_row == m, totals[m * n_resp + r : m * n_resp + r + 1], rows)
        scores.append(jnp.broadcast_to(rows, (8, LANES)))
    own_score = scores[0]
    margin = jnp.zeros((8, LANES), F32)
    for r in range(n_resp):
        margin = margin + scores[r] * signs[r]
        own_score = jnp.where(me_resp == r, scores[r], own_score)
    score_ref[...] = own_score[:micro, :1].astype(BF16)
    weight = 1.0 / (1.0 + jnp.exp(margin))
    slopes = jnp.zeros((8, LANES), F32)
    for r in range(n_resp):
        slope = -jnp.sum(signs[r] * weight, axis=1, keepdims=True)
        slopes = jnp.where(masks[r], slope, slopes)
    slopes = jnp.sum(slopes, axis=0, keepdims=True)
    for s in range(sections - 1):
        scales[s] = jnp.ones((8, LANES), F32)
    scales[last] = jnp.broadcast_to(slopes, (8, LANES))
    go_down(last, sums, slopes)

    def backward_step(step):
        s = sections - 1 - step
        slot = last + step
        backward(s, False)
        stat_start(slot, lane_sums(acc_ref[...], fold))
        loop(s, jnp.where(step == 1, s + 2, s + 1), gradients)
        go_down(s, stat_finish(slot), None)

    loop(1, sections - 1, backward_step)
    backward(0, True)
    gradients(0)

    loop(0, 2 * sections - 2, lambda slot: stat_wait(slot, stat_send))
    for kind in range(2):
        result_own(me, kind).wait()
    result_wait(part_send)
    result_wait(part_recv)


def flush_kernel(score_in, short_in, long_in, score_ref, gain_ref, short_ref, long_ref):
    score_ref[...] = score_in[...]
    gain_ref[...] = short_in[0]
    short_ref[...] = short_in[1:]
    long_ref[...] = jnp.transpose(long_in[...])


def flush(scores, short_grad, long_grad):
    vmem = pl.BlockSpec(memory_space=pltpu.VMEM)
    rows, _, width = short_grad.shape
    return pl.pallas_call(
        flush_kernel,
        out_shape=(
            jax.ShapeDtypeStruct(scores.shape, BF16),
            jax.ShapeDtypeStruct((1, width), F32),
            jax.ShapeDtypeStruct((rows - 1, 1, width), F32),
            jax.ShapeDtypeStruct(long_grad.shape[::-1], F32),
        ),
        in_specs=[vmem] * 3,
        out_specs=(vmem,) * 4,
    )(scores, short_grad, long_grad)


def run_wide(dims, *arrays):
    sections, n_resp, micro, length, chans, per_group, width = dims
    comps = micro * n_resp
    ranks = sections * n_resp
    groups = chans // per_group
    blocks = chans // LANES
    total = 2 * length
    tap_count = arrays[3].shape[0]
    group_all = width // per_group
    tile = (8, LANES)
    vmem = pl.BlockSpec(memory_space=pltpu.VMEM)
    hbm = pl.BlockSpec(memory_space=pl.ANY)
    smem = pl.BlockSpec(memory_space=pltpu.SMEM)
    slots = 2 * sections - 2
    per = (sections, groups)
    dma = pltpu.SemaphoreType.DMA
    return pl.pallas_call(
        functools.partial(wide_kernel, dims),
        out_shape=(
            jax.ShapeDtypeStruct((micro, 1), BF16),
            jax.ShapeDtypeStruct((1 + tap_count, 1, width), F32),
            jax.ShapeDtypeStruct((group_all, LANES), F32),
        ),
        in_specs=[hbm] * 6 + [smem] * 3,
        out_specs=(vmem,) * 3,
        scratch_shapes=[
            pltpu.VMEM((micro * length, width), BF16),
            pltpu.VMEM((length, width), BF16),
            pltpu.VMEM((LANES, group_all), F32),
            pltpu.VMEM((1, chans), F32),
            pltpu.VMEM((n_resp, micro * length, chans), BF16),
            pltpu.VMEM((sections, length, n_resp * chans), BF16),
            pltpu.VMEM((sections, n_resp, length, chans), BF16),
            pltpu.VMEM((sections, 1, chans), F32),
            pltpu.VMEM((sections, tap_count, 1, chans), F32),
            pltpu.VMEM((group_all, 2 * LANES), F32),
            pltpu.VMEM((sections, groups, 2 * LANES), F32),
            pltpu.VMEM((comps * LANES, (LANES // per_group) * LANES), BF16),
            pltpu.VMEM((micro * LANES, (LANES // per_group) * LANES), BF16),
            pltpu.VMEM((blocks * length, comps * LANES), BF16),
            pltpu.VMEM(tile, F32),
            pltpu.VMEM((ranks,) + tile, F32),
            pltpu.VMEM((slots,) + tile, F32),
            pltpu.VMEM((slots, ranks) + tile, F32),
            pltpu.VMEM(per + (length, LANES), BF16),
            pltpu.VMEM(per + (length, LANES), BF16),
            pltpu.VMEM(per + (length, LANES), F32),
            pltpu.VMEM(per + (total, LANES), BF16),
            pltpu.VMEM(per + (length, LANES), BF16),
            pltpu.VMEM(per + (length, LANES), BF16),
            pltpu.VMEM(per + (total, LANES), BF16),
            pltpu.VMEM(per + tile, F32),
            pltpu.VMEM((groups,) + tile, F32),
            pltpu.VMEM((sections, length, LANES), F32),
            pltpu.VMEM((sections, length, LANES), F32),
            pltpu.VMEM((groups, 8 + total, LANES), F32),
            pltpu.VMEM(per + (total + 8, LANES), F32),
            pltpu.VMEM(per + (length, LANES), F32),
            pltpu.VMEM((groups, length, LANES), F32),
            pltpu.VMEM(per + (length, LANES), BF16),
            pltpu.VMEM((length, LANES), F32),
            pltpu.VMEM((sections,) + tile, F32),
            pltpu.VMEM((blocks,) + tile, F32),
            pltpu.VMEM((sections, 1 + tap_count, 1, chans), F32),
            pltpu.VMEM((sections, groups, LANES), F32),
            dma((10,)),
            dma((n_resp,)),
            dma((n_resp,)),
            dma((3, sections)),
            dma((3, sections)),
            dma((sections, n_resp)),
            dma((sections, n_resp)),
            dma((sections,)),
            dma((sections,)),
            dma((sections,)),
            dma((ranks,)),
            dma((ranks,)),
            dma((slots,)),
            dma((slots,)),
            dma((2,)),
            dma((2,)),
        ],
        compiler_params=pltpu.CompilerParams(
            collective_id=1, has_side_effects=True, vmem_limit_bytes=56 * 1024 * 1024
        ),
    )(*arrays)


def wide_body(
    completion_rows,
    prompt_pool,
    norm_gain,
    short_taps,
    long_taps,
    score_head,
    live_lengths,
    prompt_owner,
    pair_index,
):
    sections = lax.axis_size("section")
    n_resp = lax.axis_size("resp")
    micro, _, length, width = completion_rows.shape
    chans = width // (sections * n_resp)
    per_group = width // long_taps.shape[2]
    results = run_wide(
        (sections, n_resp, micro, length, chans, per_group, width),
        completion_rows.reshape(micro * length, width),
        prompt_pool[0, 0],
        norm_gain,
        short_taps.transpose(1, 0, 2),
        long_taps[0],
        score_head[None],
        prompt_owner,
        pair_index.transpose(0, 2, 1),
        live_lengths.T,
    )
    scores, gain_grad, short_grad, long_grad = flush(*results)
    return (
        scores,
        gain_grad,
        short_grad.transpose(1, 0, 2),
        long_grad[None],
    )


def is_wide(
    completion_rows,
    prompt_pool,
    norm_gain,
    short_taps,
    long_taps,
    score_head,
    live_lengths,
    prompt_owner,
    pair_index,
):
    sections = lax.axis_size("section")
    n_resp = lax.axis_size("resp")
    micro, _, length, width = completion_rows.shape
    per_group = width // long_taps.shape[2]
    return (
        micro * n_resp * per_group == LANES
        and micro * n_resp == 8
        and width % (sections * n_resp * LANES) == 0
        and prompt_pool.shape[2] == length
        and long_taps.shape[1] == 2 * length == LANES
        and micro * length == LANES
        and short_taps.shape[1] == 7
        and sections >= 3
    )


def either(*arrays):
    return wide_body(*arrays) if is_wide(*arrays) else body(*arrays)


def solution(mesh):
    placed = (
        P(None, ("groups", "resp"), None, None),
        P("section", ("groups", "resp"), None, None),
        P("section", None),
        P("section", None, None),
        P("section", None, None),
        P(),
        P(None, ("groups", "resp")),
        P("groups"),
        P(None, "groups", None),
    )
    return jax.shard_map(
        either,
        mesh=mesh,
        in_specs=placed,
        out_specs=(
            P(None, ("groups", "resp")),
            P("section", "groups"),
            P("section", "groups", None),
            P("section", "groups", None),
        ),
        check_vma=False,
    )
```
